32 devices in a mesh: gx: 4 (over z), gy: 4 (over x, core), gz: 2 (over y).
Axes of the slice: x: 2, y: 2, z: 4, core: 2. Of those that a mesh axis runs over, the one named last changes fastest.
Arguments:
- elevation: float32 [256, 8192], P('gx', ('gy', 'gz')), may hold values from -1 to 1
- surface_potential: float32 [256, 8192], P('gx', ('gy', 'gz')), may hold values from -2 to 2
- seabed: int32 [256, 8192], P('gx', 'gy'), may hold values from 384 to 1023
- interior_potential: float32 [16, 256, 8192], P('gz', 'gx', 'gy'), may hold values from -1.5 to 1.5
Outputs:
- new_elevation: float32 [256, 8192], P('gx', ('gy', 'gz'))
- new_potential: float32 [256, 8192], P('gx', ('gy', 'gz'))
- laplace_apply: float32 [16, 256, 8192], P('gz', 'gx', 'gy')
The draws below stay inside these ranges and needn't reach their ends.
All inputs are finite; a program needn't handle non-finite values.
Results may differ from the reference program's by a relative error of at most 0.0003.
Values sent between devices are 32-bit elements; how exact they have to be, the bound alone decides.
No kernel may reach another device: no remote copies, remote signals or barrier semaphores. Data moves between devices by JAX's collectives and lax.ppermute only.
A program may use at most 64 MiB of HBM per device.

```python
import jax
import jax.numpy as jnp
from jax import lax

NX = 256
NY = 8192
NL = 16


def plant(array, own_key, smallest, largest):
    extent = array.shape
    place = [jax.random.randint(jax.random.fold_in(own_key, axis), (), 0, extent[axis]) for axis in range(len(extent))]
    array = array.at[tuple(place)].set(smallest)
    longest = extent.index(max(extent))
    place[longest] = (place[longest] + 1) % extent[longest]
    return array.at[tuple(place)].set(largest)


def level_of(key, extent, split, smallest, top_value):
    def one(dim, shards_of):
        draws = jax.random.uniform(jax.random.fold_in(jax.random.fold_in(key, 6), dim), (shards_of,), jnp.float32, smallest / len(split), top_value / len(split))
        return jnp.repeat(jnp.exp(draws), extent[dim] // shards_of).reshape((-1,) + (1,) * (len(extent) - dim - 1))

    level = one(*split[0])
    for cut in split[1:]:
        level = level * one(*cut)
    return level


def scatter_about(rng, dims, spread, limit, shards=(), kind=jnp.bfloat16):
    result = jax.random.normal(rng, dims, jnp.float32) * spread
    if len(shards) > 0:
        result = level_of(rng, dims, shards, -0.22, 0.18) * result
    return jnp.clip(result, min=-limit, max=limit).astype(kind)


def setup_inputs(seed: int = 0) -> dict:
    seeds = jax.random.split(jax.random.key(seed), 5)
    return {
        "elevation": scatter_about(seeds[0], (NX, NY), 0.25, 1.0, ((0, 4), (1, 8)), jnp.float32),
        "surface_potential": scatter_about(seeds[1], (NX, NY), 0.5, 2.0, ((0, 4), (1, 8)), jnp.float32),
        "seabed": plant(jax.random.randint(seeds[2], (NX, NY), 384, 1024), jax.random.fold_in(seeds[2], 1), 384, 1023).astype(jnp.int32),
        "interior_potential": scatter_about(seeds[3], (NL, NX, NY), 0.25, 1.5, ((0, 2), (1, 4), (2, 4)), jnp.float32),
    }


time_step = 0.05
depth_unit = 0.015625


def shifted(source, step_north, step_east):
    return jnp.roll(source, (-step_north, -step_east), axis=(0, 1))


def first_north(source):
    return (8.0 * (shifted(source, 1, 0) - shifted(source, -1, 0)) - (shifted(source, 2, 0) - shifted(source, -2, 0))) / 12.0


def first_east(source):
    return (8.0 * (shifted(source, 0, 1) - shifted(source, 0, -1)) - (shifted(source, 0, 2) - shifted(source, 0, -2))) / 12.0


def curvature(source):
    north = (-shifted(source, 2, 0) + 16.0 * shifted(source, 1, 0) - 30.0 * source + 16.0 * shifted(source, -1, 0) - shifted(source, -2, 0)) / 12.0
    east = (-shifted(source, 0, 2) + 16.0 * shifted(source, 0, 1) - 30.0 * source + 16.0 * shifted(source, 0, -1) - shifted(source, 0, -2)) / 12.0
    return north + east


def rates(height, poten):
    height_north = first_north(height)
    height_east = first_east(height)
    poten_north = first_north(poten)
    poten_east = first_east(poten)
    rate_height = curvature(poten) - (height_north * poten_north + height_east * poten_east)
    rate_potential = -height - 0.5 * (poten_north * poten_north + poten_east * poten_east)
    return rate_height, rate_potential


def centred_north(source):
    return 0.5 * (shifted(source, 1, 0) - shifted(source, -1, 0))


def centred_east(source):
    return 0.5 * (shifted(source, 0, 1) - shifted(source, 0, -1))


def reference(elevation, surface_potential, seabed, interior_potential):
    rate_first, rate_second = rates(elevation, surface_potential)
    elevation_one = elevation + time_step * rate_first
    potential_one = surface_potential + time_step * rate_second
    rate_third, rate_fourth = rates(elevation_one, potential_one)
    new_elevation = 0.5 * (elevation + elevation_one + time_step * rate_third)
    new_potential = 0.5 * (surface_potential + potential_one + time_step * rate_fourth)
    depth = seabed.astype(jnp.float32) * depth_unit
    column = depth + new_elevation
    depth_north = centred_north(depth)
    depth_east = centred_east(depth)
    column_north = centred_north(column)
    column_east = centred_east(column)
    spacing = 1.0 / NL

    def one_layer(layer_index):
        centre = lax.dynamic_index_in_dim(interior_potential, layer_index, 0, keepdims=False)
        ghost_below = lax.dynamic_index_in_dim(interior_potential, jnp.maximum(layer_index - 1, 0).astype(jnp.int32), 0, keepdims=False)
        inner_above = lax.dynamic_index_in_dim(interior_potential, jnp.minimum(layer_index + 1, NL - 1).astype(jnp.int32), 0, keepdims=False)
        ghost_above = jnp.where(layer_index == NL - 1, 2.0 * new_potential - centre, inner_above)
        sigma_level = (layer_index.astype(jnp.float32) + 0.5) / NL
        slope_north = (depth_north - sigma_level * column_north) / column
        slope_east = (depth_east - sigma_level * column_east) / column
        second_north = shifted(centre, 1, 0) - 2.0 * centre + shifted(centre, -1, 0)
        second_east = shifted(centre, 0, 1) - 2.0 * centre + shifted(centre, 0, -1)
        mixed_north = (centred_north(ghost_above) - centred_north(ghost_below)) / (2.0 * spacing)
        mixed_east = (centred_east(ghost_above) - centred_east(ghost_below)) / (2.0 * spacing)
        vertical = (ghost_above - 2.0 * centre + ghost_below) / (spacing * spacing)
        weight = slope_north * slope_north + slope_east * slope_east + 1.0 / (column * column)
        return second_north + second_east + 2.0 * slope_north * mixed_north + 2.0 * slope_east * mixed_east + weight * vertical

    laplace_apply = lax.map(one_layer, jnp.arange(NL, dtype=jnp.int32))
    return new_elevation, new_potential, laplace_apply
```

```python
import functools

import jax
import jax.numpy as jnp
from jax import lax
from jax.experimental import pallas as pl
from jax.experimental.pallas import tpu as pltpu
from jax.sharding import PartitionSpec as P

time_step = 0.05
depth_unit = 0.015625
LANES = 128
SUBS = 8


def shift_rows(prev, cur, nxt, step):
    sub = lax.broadcasted_iota(jnp.int32, cur.shape, 0)
    if step < 0:
        return pltpu.roll(jnp.where(sub >= SUBS + step, prev, cur), -step, 0)
    return pltpu.roll(jnp.where(sub < step, nxt, cur), SUBS - step, 0)


def shift_lanes(left, cur, right, step):
    lane = lax.broadcasted_iota(jnp.int32, cur.shape, 1)
    if step < 0:
        return pltpu.roll(jnp.where(lane >= LANES + step, left, cur), -step, 1)
    return pltpu.roll(jnp.where(lane < step, right, cur), LANES - step, 1)


def square(tile, at_end):
    rest = jnp.zeros((LANES - tile.shape[0], LANES), tile.dtype)
    return jnp.concatenate([rest, tile] if at_end else [tile, rest], 0)


def first_pack(group, e_left, e_right, p_left, p_right, layer, seam, outer, layer_out):
    left = jnp.concatenate([e_left[...], p_left[...]], 0).T[:SUBS]
    right = jnp.concatenate([e_right[...], p_right[...]], 0).T[LANES - SUBS :]
    low = group[0] == 0
    seam[...] = jnp.where(low, right, left)
    outer[...] = jnp.where(low, left, right)
    layer_out[...] = layer[0]


def lazy_pack(v_top, v_bottom, v_left, v_right, s_top, s_bottom, s_left, s_right, up, down, to_right, to_left):
    layers, _, width = v_top.shape
    piece = width // SUBS
    for k in range(layers):
        up[k : k + 1, :width] = v_bottom[k, SUBS - 1 : SUBS, :]
        down[k : k + 1, :width] = v_top[k, 0:1, :]
    for q in range(SUBS):
        part = slice(q * piece, (q + 1) * piece)
        up[q : q + 1, width:] = s_bottom[SUBS - 1 : SUBS, part].astype(jnp.float32) * depth_unit
        down[q : q + 1, width:] = s_top[0:1, part].astype(jnp.float32) * depth_unit
    to_right[...] = jnp.zeros_like(to_right)
    to_left[...] = jnp.zeros_like(to_left)
    for j in range(layers // 2):
        both = jnp.concatenate([v_right[2 * j], v_right[2 * j + 1]], 0).T
        to_right[j : j + 1, :] = both[LANES - 1 :]
        both = jnp.concatenate([v_left[2 * j], v_left[2 * j + 1]], 0).T
        to_left[j : j + 1, :] = both[:1]
    j = layers // 2
    both = jnp.concatenate([s_right[...], s_right[...]], 0).astype(jnp.float32) * depth_unit
    to_right[j : j + 1, :] = both.T[LANES - 1 :]
    both = jnp.concatenate([s_left[...], s_left[...]], 0).astype(jnp.float32) * depth_unit
    to_left[j : j + 1, :] = both.T[:1]


def side_blocks(low, seam, outer):
    left = square(jnp.where(low, outer, seam), True).T
    right = square(jnp.where(low, seam, outer), False).T
    return left, right


def row_pack(group, e_top, e_bottom, p_top, p_bottom, seam, outer, up, down):
    left, right = side_blocks(group[0] == 0, seam[...], outer[...])
    rows = LANES // 2
    width = e_top.shape[1]
    for row, tops, bottoms in ((0, e_top, e_bottom), (SUBS, p_top, p_bottom)):
        base = 0 if row == 0 else rows
        up[row : row + SUBS, :LANES] = left[base + rows - SUBS : base + rows]
        up[row : row + SUBS, LANES : LANES + width] = bottoms[...]
        up[row : row + SUBS, LANES + width :] = right[base + rows - SUBS : base + rows]
        down[row : row + SUBS, :LANES] = left[base : base + SUBS]
        down[row : row + SUBS, LANES : LANES + width] = tops[...]
        down[row : row + SUBS, LANES + width :] = right[base : base + SUBS]


def neighbourhood(ref, block, lane, blocks):
    here = pl.multiple_of(block * SUBS, SUBS)
    above = pl.multiple_of(jnp.maximum(block - 1, 0) * SUBS, SUBS)
    below = pl.multiple_of(jnp.minimum(block + 1, blocks - 1) * SUBS, SUBS)
    at = lambda row, column: ref[pl.ds(row, SUBS), column : column + LANES]
    cur = at(here, lane)
    prev, nxt = at(above, lane), at(below, lane)
    left, right = at(here, lane - LANES), at(here, lane + LANES)
    rows = [shift_rows(prev, cur, nxt, step) for step in (-2, -1, 1, 2)]
    lanes = [shift_lanes(left, cur, right, step) for step in (-2, -1, 1, 2)]
    return cur, rows, lanes


def slope(values):
    return (8.0 * (values[2] - values[1]) - (values[3] - values[0])) * (1.0 / 12.0)


def tile_rates(e_near, p_near):
    e, e_rows, e_lanes = e_near
    p, p_rows, p_lanes = p_near
    p_x, p_y = slope(p_rows), slope(p_lanes)
    bend = 16.0 * ((p_rows[1] + p_rows[2]) + (p_lanes[1] + p_lanes[2]))
    bend = bend - ((p_rows[0] + p_rows[3]) + (p_lanes[0] + p_lanes[3])) - 60.0 * p
    rate_e = bend * (1.0 / 12.0) - (slope(e_rows) * p_x + slope(e_lanes) * p_y)
    rate_p = -e - 0.5 * (p_x * p_x + p_y * p_y)
    return e, p, rate_e, rate_p


def surface(
    group, e, p, seam, outer, north, south, far_north, far_south, x_left, x_right,
    new_e, new_p, wide_e, wide_p, rims, e0, p0, e1, p1,
):
    rows, width = e.shape
    low = group[0] == 0
    left, right = side_blocks(low, seam[...], outer[...])
    blocks = rows // SUBS + 2
    pad = 2 * LANES
    for old, source, base in ((e0, e, 0), (p0, p, LANES // 2)):
        half = SUBS if base else 0
        old[:SUBS, LANES : LANES + width + pad] = north[half : half + SUBS, :]
        old[rows + SUBS :, LANES : LANES + width + pad] = south[half : half + SUBS, :]
        old[SUBS : SUBS + rows, pad : pad + width] = source[...]
        old[SUBS : SUBS + rows, LANES:pad] = left[base : base + rows]
        old[SUBS : SUBS + rows, pad + width : pad + width + LANES] = right[base : base + rows]
    chunks = range(LANES, width + 3 * LANES, LANES)

    def first(block, carry):
        here = pl.multiple_of(block * SUBS, SUBS)
        for lane in chunks:
            old_e, old_p, rate_e, rate_p = tile_rates(
                neighbourhood(e0, block, lane, blocks), neighbourhood(p0, block, lane, blocks)
            )
            e1[pl.ds(here, SUBS), lane : lane + LANES] = old_e + time_step * rate_e
            p1[pl.ds(here, SUBS), lane : lane + LANES] = old_p + time_step * rate_p
        return carry

    lax.fori_loop(0, blocks, first, 0)

    def second(block, carry):
        here = pl.multiple_of(block * SUBS, SUBS)
        for lane in chunks:
            one_e, one_p, rate_e, rate_p = tile_rates(
                neighbourhood(e1, block, lane, blocks), neighbourhood(p1, block, lane, blocks)
            )
            old_e = e0[pl.ds(here, SUBS), lane : lane + LANES]
            old_p = p0[pl.ds(here, SUBS), lane : lane + LANES]
            to = lane - LANES
            wide_e[pl.ds(here, SUBS), to : to + LANES] = 0.5 * (old_e + one_e + time_step * rate_e)
            wide_p[pl.ds(here, SUBS), to : to + LANES] = 0.5 * (old_p + one_p + time_step * rate_p)
        return carry

    lax.fori_loop(0, blocks, second, 0)
    new_e[...] = wide_e[SUBS : SUBS + rows, LANES : LANES + width]
    new_p[...] = wide_p[SUBS : SUBS + rows, LANES : LANES + width]
    rims[...] = jnp.zeros_like(rims)
    layers = far_north.shape[0]
    tile = 2 * width
    rims[0:1, :] = jnp.where(low, far_north[layers - 1 : layers, :tile], far_north[0:1, :tile])
    rims[1:2, :] = jnp.where(low, far_south[layers - 1 : layers, :tile], far_south[0:1, :tile])
    for row, wide in ((2, wide_e), (3, wide_p)):
        rims[row : row + 1, :width] = wide[SUBS - 1 : SUBS, LANES : LANES + width]
        rims[row : row + 1, width:] = wide[SUBS + rows : SUBS + rows + 1, LANES : LANES + width]
    pairs = layers // 2
    for lane, side in ((0, x_left), (LANES, x_right)):
        top_pair = pltpu.roll(side[...], LANES // 2, 1)[pairs - 1 : pairs]
        rims[4:5, lane : lane + LANES] = jnp.where(low, top_pair, side[0:1, :])
    inner = slice(SUBS, SUBS + rows)
    left = jnp.concatenate([wide_e[inner, :LANES], wide_p[inner, :LANES]], 0).T[LANES - 1 :]
    right = jnp.concatenate([wide_e[inner, LANES + width :], wide_p[inner, LANES + width :]], 0).T[:1]
    rims[4:5, 2 * LANES : 3 * LANES] = jnp.where(low, left, right)


def widen(low, group, wide, other, rims, row, base, target):
    rows, width = other.shape
    inner = slice(SUBS, SUBS + rows)
    own = pl.multiple_of(LANES + group * width, LANES)
    far = pl.multiple_of(LANES + (1 - group) * width, LANES)
    own_side = pl.multiple_of(group * (2 * width + LANES), LANES)
    far_side = pl.multiple_of((1 - group) * (2 * width + LANES), LANES)
    target[:, pl.ds(own, width)] = wide[:, LANES : LANES + width]
    target[:, pl.ds(own_side, LANES)] = jnp.where(low, wide[:, :LANES], wide[:, LANES + width :])
    target[inner, pl.ds(far, width)] = other[...]
    target[SUBS - 1 : SUBS, pl.ds(far, width)] = rims[row : row + 1, :width]
    target[SUBS + rows : SUBS + rows + 1, pl.ds(far, width)] = rims[row : row + 1, width:]
    column = square(rims[:, 2 * LANES : 3 * LANES], False).T[base : base + rows]
    column = jnp.where(low, pltpu.roll(column, LANES - 4, 1), pltpu.roll(column, LANES - 5, 1))
    target[inner, pl.ds(far_side, LANES)] = column


def laplace(
    total_layers, group_ref, v, far_layer, sea, far_north, far_south, x_left, x_right, rims, wide_e, other_e,
    out, coefficients, volume, column, depth, sems,
):
    block = pl.program_id(0)
    group = group_ref[0]
    low = group == 0
    layers, rows, tile = v.shape
    blocks = rows // SUBS
    inner = slice(SUBS, SUBS + rows)
    far_slot = jnp.where(low, layers + 1, 0)
    own_slot = layers + 1 - far_slot
    own_source = jnp.where(low, 0, layers - 1)

    def copies(index):
        part = pl.ds(pl.multiple_of(index * SUBS, SUBS), SUBS)
        into = pl.ds(pl.multiple_of((index + 1) * SUBS, SUBS), SUBS)
        return (
            pltpu.make_async_copy(
                v.at[:, part, :], volume.at[1 : layers + 1, into, LANES : LANES + tile], sems.at[0, index]
            ),
            pltpu.make_async_copy(
                v.at[own_source, part, :], volume.at[own_slot, into, LANES : LANES + tile], sems.at[1, index]
            ),
            pltpu.make_async_copy(
                far_layer.at[part, :], volume.at[far_slot, into, LANES : LANES + tile], sems.at[2, index]
            ),
        )

    @pl.when(block == 0)
    def _():
        for index in range(blocks):
            for copy in copies(index):
                copy.start()
        left = square(x_left[...], False).T
        right = square(x_right[...], False).T
        half = LANES // 2
        pairs = layers // 2

        def sides(slot, from_left, from_right, north, south):
            volume[slot, inner, :LANES] = from_left
            volume[slot, inner, LANES + tile :] = from_right
            volume[slot, SUBS - 1 : SUBS, LANES : LANES + tile] = north
            volume[slot, SUBS + rows : SUBS + rows + 1, LANES : LANES + tile] = south

        def own_sides(k):
            base = (k % 2) * half
            return (
                pltpu.roll(left, LANES - 1 - k // 2, 1)[base : base + rows],
                pltpu.roll(right, (LANES - k // 2) % LANES, 1)[base : base + rows],
                far_north[k : k + 1, :tile],
                far_south[k : k + 1, :tile],
            )

        for k in range(layers):
            sides(k + 1, *own_sides(k))
        first, last = own_sides(0), own_sides(layers - 1)
        sides(own_slot, *(jnp.where(low, a, b) for a, b in zip(first, last)))
        far_left = pltpu.roll(square(rims[:, :LANES], False).T, LANES - 5, 1)[:rows]
        far_right = pltpu.roll(square(rims[:, LANES : 2 * LANES], False).T, LANES - 4, 1)[:rows]
        sides(far_slot, far_left, far_right, rims[0:1, :], rims[1:2, :])

        depth[inner, LANES : LANES + tile] = sea[...].astype(jnp.float32) * depth_unit
        piece = tile // SUBS
        for q in range(SUBS):
            part = slice(LANES + q * piece, LANES + (q + 1) * piece)
            depth[SUBS - 1 : SUBS, part] = far_north[q : q + 1, tile:]
            depth[SUBS + rows : SUBS + rows + 1, part] = far_south[q : q + 1, tile:]
        depth[inner, :LANES] = pltpu.roll(left, LANES - 1 - pairs, 1)[:rows]
        depth[inner, LANES + tile :] = pltpu.roll(right, LANES - pairs, 1)[:rows]
        widen(low, group, wide_e, other_e, rims, 2, 0, column)
        column[...] = column[...] + depth[...]
        for copy in copies(0):
            copy.wait()

    @pl.when(block < blocks - 1)
    def _():
        for copy in copies(block + 1):
            copy.wait()

    spacing = 1.0 / total_layers
    sigma = (group * layers).astype(jnp.float32) * spacing + 0.5 * spacing
    sign = (1 - 2 * group).astype(jnp.float32)
    here = pl.multiple_of((block + 1) * SUBS, SUBS)
    above = pl.multiple_of(block * SUBS, SUBS)
    below = pl.multiple_of((block + 2) * SUBS, SUBS)

    def near(ref, lane):
        at = lambda row, start: ref[pl.ds(row, SUBS), pl.ds(start, LANES)]
        cur = at(here, lane)
        prev, nxt = at(above, lane), at(below, lane)
        left = at(here, pl.multiple_of(lane - LANES, LANES))
        right = at(here, pl.multiple_of(lane + LANES, LANES))
        return (
            cur,
            shift_rows(prev, cur, nxt, -1),
            shift_rows(prev, cur, nxt, 1),
            shift_lanes(left, cur, right, -1),
            shift_lanes(left, cur, right, 1),
        )

    def chunk(lane):
        to = pl.multiple_of(lane - LANES, LANES)
        c, c_up, c_down, c_left, c_right = near(column, lane)
        _, d_up, d_down, d_left, d_right = near(depth, lane)
        inverse = 1.0 / c
        scale = (0.25 / spacing) * inverse
        bx, by = scale * (c_down - c_up), scale * (c_right - c_left)
        ax, ay = scale * (d_down - d_up), scale * (d_right - d_left)
        ux, uy = ax - sigma * bx, ay - sigma * by
        bx, by = spacing * bx, spacing * by
        scaled = inverse * (1.0 / spacing)
        weight = 4.0 * (ux * ux + uy * uy) + scaled * scaled
        bend = 4.0 * (bx * bx + by * by)
        step = bend - 8.0 * (ux * bx + uy * by)
        bend = bend + bend

        def level(slot):
            p, up, down, left, right = near(volume.at[slot], lane)
            return p, down - up, right - left, (down + up) + (right + left)

        below_level = level(0)
        this = level(1)
        for k in range(layers):
            above_level = level(k + 2)
            p, north, east, _ = above_level
            if k == layers - 1:
                p, north, east = sign * p, sign * north, sign * east
            centre = this[0]
            twice = centre + centre
            value = this[3] - (twice + twice)
            value = value + ux * (north - below_level[1]) + uy * (east - below_level[2])
            value = value + weight * ((p + below_level[0]) - twice)
            out[k, :, pl.ds(to, LANES)] = value
            if k == layers - 1:
                coefficients[0, :, pl.ds(to, LANES)] = ux
                coefficients[1, :, pl.ds(to, LANES)] = uy
                coefficients[2, :, pl.ds(to, LANES)] = weight
            else:
                ux, uy = ux - bx, uy - by
                weight, step = weight + step, step + bend
            below_level, this = this, above_level

    group_of = 2

    def pair(index, carry):
        for inside in range(group_of):
            chunk(pl.multiple_of((index * group_of + inside + 1) * LANES, LANES))
        return carry

    lax.fori_loop(0, tile // LANES // group_of, pair, 0)


def top(group_ref, before, coefficients, rims, wide_p, other_p, out, potential):
    group = group_ref[0]
    low = group == 0
    rows, tile = before.shape[1], before.shape[2]
    widen(low, group, wide_p, other_p, rims, 3, LANES // 2, potential)
    gain = 2.0 * group.astype(jnp.float32)

    def body(block, carry):
        here = pl.multiple_of((block + 1) * SUBS, SUBS)
        above = pl.multiple_of(block * SUBS, SUBS)
        below = pl.multiple_of((block + 2) * SUBS, SUBS)
        for lane in range(LANES, LANES + tile, LANES):
            at = lambda row, start: potential[pl.ds(row, SUBS), start : start + LANES]
            cur = at(here, lane)
            prev, nxt = at(above, lane), at(below, lane)
            left, right = at(here, lane - LANES), at(here, lane + LANES)
            north = shift_rows(prev, cur, nxt, 1) - shift_rows(prev, cur, nxt, -1)
            east = shift_lanes(left, cur, right, 1) - shift_lanes(left, cur, right, -1)
            spot = (pl.ds(above, SUBS), slice(lane - LANES, lane))
            value = coefficients[(0, *spot)] * north + coefficients[(1, *spot)] * east
            value = value + coefficients[(2, *spot)] * cur
            out[(0, *spot)] = before[(0, *spot)] + gain * value
        return carry

    lax.fori_loop(0, rows // SUBS, body, 0)


def ring(axis, step):
    count = lax.axis_size(axis)
    return [(i, (i + step) % count) for i in range(count)]


def shards(elevation, surface_potential, seabed, interior_potential):
    rows, width = elevation.shape
    layers, _, tile = interior_potential.shape
    assert 2 * rows == LANES and tile == 2 * width and layers == SUBS
    assert lax.axis_size("gz") == 2
    total_layers = layers * lax.axis_size("gz")
    f32 = jnp.float32
    shape = lambda *dims: jax.ShapeDtypeStruct(dims, f32)
    whole = lambda *dims: pl.BlockSpec(dims, lambda *_: (0,) * len(dims))
    group = lax.axis_index("gz").astype(jnp.int32).reshape((1,))
    scalar = pl.BlockSpec(memory_space=pltpu.SMEM)
    last_row, last_half, last_tile = rows // SUBS - 1, width // LANES - 1, tile // LANES - 1

    def block(dims, *index):
        return pl.BlockSpec(dims, lambda *_: index)

    params = pltpu.CompilerParams(vmem_limit_bytes=40 * 1024 * 1024)
    seam, outer, layer = pl.pallas_call(
        first_pack,
        out_shape=(shape(SUBS, LANES), shape(SUBS, LANES), shape(rows, tile)),
        grid_spec=pltpu.PrefetchScalarGridSpec(
            num_scalar_prefetch=1,
            grid=(1,),
            in_specs=[
                block((rows, LANES), 0, 0),
                block((rows, LANES), 0, last_half),
                block((rows, LANES), 0, 0),
                block((rows, LANES), 0, last_half),
                pl.BlockSpec((1, rows, tile), lambda _, g: (jnp.where(g[0] == 0, layers - 1, 0), 0, 0)),
            ],
            out_specs=[whole(SUBS, LANES), whole(SUBS, LANES), whole(rows, tile)],
        ),
        compiler_params=params,
        name="first_pack",
    )(group, elevation, elevation, surface_potential, surface_potential, interior_potential)

    flat = ("gy", "gz")
    count = lax.axis_size("gy")
    partner = [(2 * i + g, 2 * i + 1 - g) for i in range(count) for g in range(2)]
    across = [(2 * i + 1, (2 * i + 2) % (2 * count)) for i in range(count)]
    across = across + [(b, a) for a, b in across]
    with jax.named_scope("seam"):
        seam = lax.ppermute(seam, flat, partner)
    with jax.named_scope("outer"):
        outer = lax.ppermute(outer, flat, across)
    with jax.named_scope("layer"):
        far_layer = lax.ppermute(layer, flat, partner)

    up, down, to_right, to_left = pl.pallas_call(
        lazy_pack,
        out_shape=(shape(SUBS, tile + tile // SUBS),) * 2 + (shape(SUBS, LANES),) * 2,
        grid=(1,),
        in_specs=[
            block((layers, SUBS, tile), 0, 0, 0),
            block((layers, SUBS, tile), 0, last_row, 0),
            block((layers, rows, LANES), 0, 0, 0),
            block((layers, rows, LANES), 0, 0, last_tile),
            block((SUBS, tile), 0, 0),
            block((SUBS, tile), last_row, 0),
            block((rows, LANES), 0, 0),
            block((rows, LANES), 0, last_tile),
        ],
        out_specs=[whole(SUBS, tile + tile // SUBS)] * 2 + [whole(SUBS, LANES)] * 2,
        compiler_params=params,
        name="lazy_pack",
    )(*(interior_potential,) * 4, *(seabed,) * 4)

    wide = width + 2 * LANES
    row_up, row_down = pl.pallas_call(
        row_pack,
        out_shape=(shape(2 * SUBS, wide),) * 2,
        grid=(1,),
        in_specs=[
            scalar,
            block((SUBS, width), 0, 0),
            block((SUBS, width), last_row, 0),
            block((SUBS, width), 0, 0),
            block((SUBS, width), last_row, 0),
            whole(SUBS, LANES),
            whole(SUBS, LANES),
        ],
        out_specs=[whole(2 * SUBS, wide)] * 2,
        compiler_params=params,
        name="row_pack",
    )(group, elevation, elevation, surface_potential, surface_potential, seam, outer)
    with jax.named_scope("rows"):
        north = lax.ppermute(row_up, "gx", ring("gx", 1))
        south = lax.ppermute(row_down, "gx", ring("gx", -1))
    with jax.named_scope("far"):
        far_north = lax.ppermute(up, "gx", ring("gx", 1))
        far_south = lax.ppermute(down, "gx", ring("gx", -1))
        x_left = lax.ppermute(to_right, "gy", ring("gy", 1))
        x_right = lax.ppermute(to_left, "gy", ring("gy", -1))

    deep = rows + 2 * SUBS
    scratch = pltpu.VMEM((deep, wide + 2 * LANES), f32)
    new_e, new_p, wide_e, wide_p, rims = pl.pallas_call(
        surface,
        out_shape=(shape(rows, width),) * 2 + (shape(deep, wide),) * 2 + (shape(SUBS, tile),),
        in_specs=[scalar] + [pl.BlockSpec(memory_space=pltpu.VMEM)] * 10,
        out_specs=[pl.BlockSpec(memory_space=pltpu.VMEM)] * 5,
        scratch_shapes=[scratch] * 4,
        compiler_params=params,
        name="surface",
    )(
        group, elevation, surface_potential, seam, outer, north, south,
        far_north, far_south, x_left, x_right,
    )
    with jax.named_scope("rims"):
        far_rims = lax.ppermute(rims, flat, partner)
    with jax.named_scope("height"):
        other_e = lax.ppermute(new_e, flat, partner)
    with jax.named_scope("potential"):
        other_p = lax.ppermute(new_p, flat, partner)

    blocks = rows // SUBS
    anywhere = pl.BlockSpec(memory_space=pl.ANY)
    partial, coefficients = pl.pallas_call(
        functools.partial(laplace, total_layers),
        out_shape=(shape(layers, rows, tile), shape(3, rows, tile)),
        grid=(blocks,),
        in_specs=[
            scalar,
            anywhere,
            anywhere,
            whole(rows, tile),
            whole(SUBS, tile + tile // SUBS),
            whole(SUBS, tile + tile // SUBS),
            whole(SUBS, LANES),
            whole(SUBS, LANES),
            whole(SUBS, tile),
            whole(deep, wide),
            whole(rows, width),
        ],
        out_specs=[
            pl.BlockSpec((layers, SUBS, tile), lambda i: (0, i, 0)),
            pl.BlockSpec((3, SUBS, tile), lambda i: (0, i, 0)),
        ],
        scratch_shapes=[
            pltpu.VMEM((layers + 2, deep, tile + 2 * LANES), f32),
            pltpu.VMEM((deep, tile + 2 * LANES), f32),
            pltpu.VMEM((deep, tile + 2 * LANES), f32),
            pltpu.SemaphoreType.DMA((3, blocks)),
        ],
        compiler_params=params,
        name="laplace",
    )(
        group, interior_potential, far_layer, seabed, far_north, far_south,
        x_left, x_right, far_rims, wide_e, other_e,
    )
    last_layer = pl.BlockSpec((1, rows, tile), lambda i: (layers - 1, 0, 0))
    result = pl.pallas_call(
        top,
        out_shape=shape(layers, rows, tile),
        grid=(1,),
        in_specs=[
            scalar,
            last_layer,
            whole(3, rows, tile),
            whole(SUBS, tile),
            whole(deep, wide),
            whole(rows, width),
        ],
        out_specs=last_layer,
        scratch_shapes=[pltpu.VMEM((deep, tile + 2 * LANES), f32)],
        input_output_aliases={1: 0},
        compiler_params=params,
        name="top",
    )(group, partial, coefficients, far_rims, wide_p, other_p)
    return new_e, new_p, result


def solution(mesh):
    return jax.shard_map(
        shards,
        mesh=mesh,
        in_specs=(P("gx", ("gy", "gz")), P("gx", ("gy", "gz")), P("gx", "gy"), P("gz", "gx", "gy")),
        out_specs=(P("gx", ("gy", "gz")), P("gx", ("gy", "gz")), P("gz", "gx", "gy")),
        check_vma=False,
    )
```

```python
import functools

import jax
import jax.numpy as jnp
from jax import lax
from jax.experimental import pallas as pl
from jax.experimental.pallas import tpu as pltpu
from jax.sharding import PartitionSpec as P

time_step = 0.05
depth_unit = 0.015625
LANES = 128
SUBS = 8


def shift_lanes(left, cur, right, step):
    lane = lax.broadcasted_iota(jnp.int32, cur.shape, 1)
    if step < 0:
        return pltpu.roll(jnp.where(lane >= LANES + step, left, cur), -step, 1)
    return pltpu.roll(jnp.where(lane < step, right, cur), LANES - step, 1)


def square(tile, at_end):
    rest = jnp.zeros((LANES - tile.shape[0], LANES), tile.dtype)
    return jnp.concatenate([rest, tile] if at_end else [tile, rest], 0)


def first_pack(group, e, p, v, seam, outer, layer, edges, sems):
    rows, width = e.shape
    low = group[0] == 0
    source = jnp.where(low, v.shape[0] - 1, 0)
    whole = pltpu.make_async_copy(v.at[source], layer, sems.at[4])
    copies = []
    for index, (field, start) in enumerate(((e, 0), (p, 0), (e, width - LANES), (p, width - LANES))):
        into = edges.at[index // 2, (index % 2) * rows : (index % 2 + 1) * rows, :]
        copies.append(pltpu.make_async_copy(field.at[:, start : start + LANES], into, sems.at[index]))
    for copy in copies:
        copy.start()
    whole.start()
    for copy in copies:
        copy.wait()
    left = edges[0].T[:SUBS]
    right = edges[1].T[LANES - SUBS :]
    seam[...] = jnp.where(low, right, left)
    outer[...] = jnp.where(low, left, right)
    whole.wait()


def lazy_pack(v_top, v_bottom, v_left, v_right, s_top, s_bottom, s_left, s_right, up, down, to_right, to_left):
    layers, _, width = v_top.shape
    piece = width // SUBS
    for k in range(layers):
        up[k : k + 1, :width] = v_bottom[k, SUBS - 1 : SUBS, :]
        down[k : k + 1, :width] = v_top[k, 0:1, :]
    for q in range(SUBS):
        part = slice(q * piece, (q + 1) * piece)
        up[q : q + 1, width:] = s_bottom[SUBS - 1 : SUBS, part].astype(jnp.float32) * depth_unit
        down[q : q + 1, width:] = s_top[0:1, part].astype(jnp.float32) * depth_unit
    to_right[...] = jnp.zeros_like(to_right)
    to_left[...] = jnp.zeros_like(to_left)
    for j in range(layers // 2):
        both = jnp.concatenate([v_right[2 * j], v_right[2 * j + 1]], 0).T
        to_right[j : j + 1, :] = both[LANES - 1 :]
        both = jnp.concatenate([v_left[2 * j], v_left[2 * j + 1]], 0).T
        to_left[j : j + 1, :] = both[:1]
    j = layers // 2
    both = jnp.concatenate([s_right[...], s_right[...]], 0).astype(jnp.float32) * depth_unit
    to_right[j : j + 1, :] = both.T[LANES - 1 :]
    both = jnp.concatenate([s_left[...], s_left[...]], 0).astype(jnp.float32) * depth_unit
    to_left[j : j + 1, :] = both.T[:1]


def side_blocks(low, seam, outer):
    left = square(jnp.where(low, outer, seam), True).T
    right = square(jnp.where(low, seam, outer), False).T
    return left, right


def row_pack(group, e_top, e_bottom, p_top, p_bottom, seam, outer, up, down):
    left, right = side_blocks(group[0] == 0, seam[...], outer[...])
    rows = LANES // 2
    width = e_top.shape[1]
    for row, tops, bottoms in ((0, e_top, e_bottom), (SUBS, p_top, p_bottom)):
        base = 0 if row == 0 else rows
        up[row : row + SUBS, :LANES] = left[base + rows - SUBS : base + rows]
        up[row : row + SUBS, LANES : LANES + width] = bottoms[...]
        up[row : row + SUBS, LANES + width :] = right[base + rows - SUBS : base + rows]
        down[row : row + SUBS, :LANES] = left[base : base + SUBS]
        down[row : row + SUBS, LANES : LANES + width] = tops[...]
        down[row : row + SUBS, LANES + width :] = right[base : base + SUBS]


def neighbourhood(ref, lane_tile, row):
    last = ref.shape[0] - 1
    at = lambda column, step: ref[column, pl.ds(row + step, SUBS), :]
    cur = at(lane_tile, 0)
    left, right = at(max(lane_tile - 1, 0), 0), at(min(lane_tile + 1, last), 0)
    rows = [at(lane_tile, step) for step in (-2, -1, 1, 2)]
    lanes = [shift_lanes(left, cur, right, step) for step in (-2, -1, 1, 2)]
    return cur, rows, lanes


def slope(values):
    return (2.0 / 3.0) * (values[2] - values[1]) - (1.0 / 12.0) * (values[3] - values[0])


def tile_rates(e_near, p_near):
    e, e_rows, e_lanes = e_near
    p, p_rows, p_lanes = p_near
    p_x, p_y = slope(p_rows), slope(p_lanes)
    near = (p_rows[1] + p_rows[2]) + (p_lanes[1] + p_lanes[2])
    far = (p_rows[0] + p_rows[3]) + (p_lanes[0] + p_lanes[3])
    bend = (4.0 / 3.0) * near - (1.0 / 12.0) * far - 5.0 * p
    rate_e = bend - (slope(e_rows) * p_x + slope(e_lanes) * p_y)
    rate_p = 0.5 * (p_x * p_x + p_y * p_y) + e
    return e, p, time_step * rate_e, -time_step * rate_p


def surface(
    group, e, p, seam, outer, north, south,
    new_e, new_p, height, wide_e, wide_p, e0, p0, e1, p1,
):
    rows, width = e.shape
    low = group[0] == 0
    left, right = side_blocks(low, seam[...], outer[...])
    tiles = width // LANES + 2
    inner = slice(SUBS, SUBS + rows)
    for old, source, base in ((e0, e, 0), (p0, p, LANES // 2)):
        half = SUBS if base else 0
        for t in range(tiles):
            part = slice(t * LANES, (t + 1) * LANES)
            old[t, :SUBS, :] = north[half : half + SUBS, part]
            old[t, SUBS + rows : 2 * SUBS + rows, :] = south[half : half + SUBS, part]
            if 0 < t < tiles - 1:
                old[t, inner, :] = source[:, (t - 1) * LANES : t * LANES]
        old[0, inner, :] = left[base : base + rows]
        old[tiles - 1, inner, :] = right[base : base + rows]
    blocks = rows // SUBS + 1

    def first(block, carry):
        row = block * SUBS + SUBS - 3
        for t in range(tiles):
            old_e, old_p, step_e, step_p = tile_rates(neighbourhood(e0, t, row), neighbourhood(p0, t, row))
            e1[t, pl.ds(row, SUBS), :] = old_e + step_e
            p1[t, pl.ds(row, SUBS), :] = old_p + step_p
        return carry

    lax.fori_loop(0, blocks, first, 0)

    def second(block, carry):
        row = block * SUBS + SUBS - 1
        for t in range(tiles):
            one_e, one_p, step_e, step_p = tile_rates(neighbourhood(e1, t, row), neighbourhood(p1, t, row))
            old_e = e0[t, pl.ds(row, SUBS), :]
            old_p = p0[t, pl.ds(row, SUBS), :]
            wide_e[t, pl.ds(row, SUBS), :] = 0.5 * ((old_e + one_e) + step_e)
            wide_p[t, pl.ds(row, SUBS), :] = 0.5 * ((old_p + one_p) + step_p)
        return carry

    lax.fori_loop(0, blocks, second, 0)
    for t in range(1, tiles - 1):
        part = slice((t - 1) * LANES, t * LANES)
        tile_e = wide_e[t, inner, :]
        new_e[:, part] = tile_e
        height[:rows, part] = tile_e
        new_p[:, part] = wide_p[t, inner, :]
        for row, wide in ((0, wide_e), (2, wide_p)):
            height[rows + row : rows + row + 1, part] = wide[t, SUBS - 1 : SUBS, :]
            height[rows + row + 1 : rows + row + 2, part] = wide[t, SUBS + rows : SUBS + rows + 1, :]
        height[rows + 4 :, part] = jnp.zeros((4, LANES), jnp.float32)
    left = jnp.concatenate([wide_e[0, inner, :], wide_p[0, inner, :]], 0).T[LANES - 1 :]
    right = jnp.concatenate([wide_e[tiles - 1, inner, :], wide_p[tiles - 1, inner, :]], 0).T[:1]
    height[rows + 4 : rows + 5, :LANES] = jnp.where(low, left, right)


def rim_pack(group, far_north, far_south, x_left, x_right, rims):
    low = group[0] == 0
    layers = far_north.shape[0]
    width = rims.shape[1]
    pairs = layers // 2
    rims[...] = jnp.zeros_like(rims)
    for row, side in ((0, far_north), (2, far_south)):
        for half in range(2):
            part = slice(half * width, (half + 1) * width)
            rims[row + half : row + half + 1, :] = jnp.where(low, side[layers - 1 : layers, part], side[0:1, part])
    for lane, side in ((0, x_left), (LANES, x_right)):
        top_pair = pltpu.roll(side[...], LANES // 2, 1)[pairs - 1 : pairs]
        rims[4:5, lane : lane + LANES] = jnp.where(low, top_pair, side[0:1, :])


def prepare(v, sea, far_north, far_south, x_left, x_right, volume, depth, sems):
    layers, rows, tile = v.shape
    tiles = tile // LANES
    inner = slice(SUBS, SUBS + rows)
    copies = []
    for t in range(tiles):
        copies.append(
            pltpu.make_async_copy(
                v.at[:, :, t * LANES : (t + 1) * LANES], volume.at[:, t + 1, inner, :], sems.at[t]
            )
        )
        copies[-1].start()
    left = square(x_left[...], False).T
    right = square(x_right[...], False).T
    half, pairs = LANES // 2, layers // 2
    for k in range(layers):
        base = (k % 2) * half
        volume[k, 0, inner, :] = pltpu.roll(left, LANES - 1 - k // 2, 1)[base : base + rows]
        volume[k, tiles + 1, inner, :] = pltpu.roll(right, (LANES - k // 2) % LANES, 1)[base : base + rows]
        for t in range(tiles):
            part = slice(t * LANES, (t + 1) * LANES)
            volume[k, t + 1, SUBS - 1 : SUBS, :] = far_north[k : k + 1, part]
            volume[k, t + 1, SUBS + rows : SUBS + rows + 1, :] = far_south[k : k + 1, part]
    depth[0, inner, :] = pltpu.roll(left, LANES - 1 - pairs, 1)[:rows]
    depth[tiles + 1, inner, :] = pltpu.roll(right, LANES - pairs, 1)[:rows]
    piece = tile // SUBS // LANES
    for t in range(tiles):
        part = slice(t * LANES, (t + 1) * LANES)
        depth[t + 1, inner, :] = sea[:, part].astype(jnp.float32) * depth_unit
        q, start = t // piece, tile + (t % piece) * LANES
        depth[t + 1, SUBS - 1 : SUBS, :] = far_north[q : q + 1, start : start + LANES]
        depth[t + 1, SUBS + rows : SUBS + rows + 1, :] = far_south[q : q + 1, start : start + LANES]
    for copy in copies:
        copy.wait()


def laplace(
    total_layers, group_ref, volume, depth, far_layer, rims, wide_e, wide_p, height,
    out, part, coefficients, column, ghost,
):
    block = pl.program_id(0)
    group = group_ref[0]
    low = group == 0
    layers = volume.shape[0]
    rows, tile = far_layer.shape
    width = tile // 2
    tiles, halves = tile // LANES, width // LANES
    inner = slice(SUBS, SUBS + rows)

    @pl.when(block == 0)
    def _():
        far_left = pltpu.roll(square(rims[:, :LANES], False).T, LANES - 5, 1)[:rows]
        far_right = pltpu.roll(square(rims[:, LANES : 2 * LANES], False).T, LANES - 4, 1)[:rows]
        ghost[0, inner, :] = far_left
        ghost[tiles + 1, inner, :] = far_right
        for t in range(tiles):
            ghost[t + 1, inner, :] = far_layer[:, t * LANES : (t + 1) * LANES]
            half, spot = t // halves, slice((t % halves) * LANES, (t % halves + 1) * LANES)
            ghost[t + 1, SUBS - 1 : SUBS, :] = rims[half : half + 1, spot]
            ghost[t + 1, SUBS + rows : SUBS + rows + 1, :] = rims[2 + half : 3 + half, spot]
        own = group * halves + 1
        other = (1 - group) * halves + 1
        for t in range(halves):
            spot = slice(t * LANES, (t + 1) * LANES)
            column[own + t, : rows + 2 * SUBS, :] = wide_e[t + 1, : rows + 2 * SUBS, :] + depth[own + t]
            column[other + t, inner, :] = height[:rows, spot] + depth[other + t, inner, :]
            for row, at in ((SUBS - 1, rows), (SUBS + rows, rows + 1)):
                column[other + t, row : row + 1, :] = height[at : at + 1, spot] + depth[other + t, row : row + 1, :]
        own_side = group * (tiles + 1)
        other_side = (1 - group) * (tiles + 1)
        edge = jnp.where(low, wide_e[0, inner, :], wide_e[halves + 1, inner, :])
        column[own_side, inner, :] = edge + depth[own_side, inner, :]
        edge = square(height[rows:, :LANES], False).T[:rows]
        edge = jnp.where(low, pltpu.roll(edge, LANES - 4, 1), pltpu.roll(edge, LANES - 5, 1))
        column[other_side, inner, :] = edge + depth[other_side, inner, :]

    spacing = 1.0 / total_layers
    sigma = (group * layers).astype(jnp.float32) * spacing + 0.5 * spacing
    sign = (1 - 2 * group).astype(jnp.float32)
    gain = (2 * group).astype(jnp.float32)
    here = pl.multiple_of((block + 1) * SUBS, SUBS)

    def near(ref, t):
        at = lambda column, step: ref[column, pl.ds(here + step, SUBS), :]
        cur = at(t, 0)
        left, right = at(t - 1, 0), at(t + 1, 0)
        return cur, at(t, -1), at(t, 1), shift_lanes(left, cur, right, -1), shift_lanes(left, cur, right, 1)

    def differences(ref, t):
        p, up, down, left, right = near(ref, t)
        return p, down - up, right - left

    def chunk(t, mine):
        c, c_up, c_down, c_left, c_right = near(column, t)
        _, d_x, d_y = differences(depth, t)
        inverse = 1.0 / c
        scale = (0.25 / spacing) * inverse
        bx, by = scale * (c_down - c_up), scale * (c_right - c_left)
        ux, uy = scale * d_x - sigma * bx, scale * d_y - sigma * by
        bx, by = spacing * bx, spacing * by
        scaled = inverse * (1.0 / spacing)
        weight = 4.0 * (ux * ux + uy * uy) + scaled * scaled
        bend = 4.0 * (bx * bx + by * by)
        step = bend - 8.0 * (ux * bx + uy * by)
        bend = bend + bend

        def level(k):
            p, up, down, left, right = near(volume.at[k], t)
            return p, down - up, right - left, ((down + up) + (right + left)) - 4.0 * p

        far = differences(ghost, t)
        this = level(0)
        lower = [jnp.where(low, a, b) for a, b in zip(this, far)]
        rise_below = this[0] - lower[0]
        spot = pl.ds(pl.multiple_of((t - 1) * LANES, LANES), LANES)
        for k in range(layers):
            if k < layers - 1:
                upper = level(k + 1)
            else:
                upper = [jnp.where(low, a, -b) for a, b in zip(far, this)]
                if mine is not None:
                    upper = [a + gain * b for a, b in zip(upper, differences(wide_p, mine))]
            rise = upper[0] - this[0]
            value = this[3] + ux * (upper[1] - lower[1]) + uy * (upper[2] - lower[2])
            value = value + weight * (rise - rise_below)
            out[k, :, spot] = value
            if k < layers - 1:
                ux, uy = ux - bx, uy - by
                weight, step = weight + step, step + bend
            elif mine is None:
                local = pl.ds(pl.multiple_of((t - 1 - (1 - group) * halves) * LANES, LANES), LANES)
                part[:, local] = value
                coefficients[0, :, local] = ux
                coefficients[1, :, local] = uy
                coefficients[2, :, local] = weight
            lower, this, rise_below = this, upper, rise

    def own_pair(index, carry):
        for inside in range(2):
            mine = index * 2 + inside + 1
            chunk(group * halves + mine, mine)
        return carry

    def other_pair(index, carry):
        for inside in range(2):
            chunk((1 - group) * halves + index * 2 + inside + 1, None)
        return carry

    lax.fori_loop(0, halves // 2, own_pair, 0)
    lax.fori_loop(0, halves // 2, other_pair, 0)


def top(group_ref, before, part, coefficients, height, wide_p, other_p, out, potential):
    del before
    low = group_ref[0] == 0
    rows, width = other_p.shape
    halves = width // LANES
    inner = slice(SUBS, SUBS + rows)
    edge = square(height[rows:, :LANES], False).T[LANES // 2 : LANES // 2 + rows]
    potential[0, inner, :] = pltpu.roll(edge, LANES - 5, 1)
    potential[halves + 1, inner, :] = wide_p[1, inner, :]
    for t in range(halves):
        spot = slice(t * LANES, (t + 1) * LANES)
        potential[t + 1, inner, :] = other_p[:, spot]
        potential[t + 1, SUBS - 1 : SUBS, :] = height[rows + 2 : rows + 3, spot]
        potential[t + 1, SUBS + rows : SUBS + rows + 1, :] = height[rows + 3 : rows + 4, spot]

    def body(block, carry):
        here = pl.multiple_of((block + 1) * SUBS, SUBS)
        to = pl.ds(pl.multiple_of(block * SUBS, SUBS), SUBS)
        for t in range(1, halves + 1):
            at = lambda column, step: potential[column, pl.ds(here + step, SUBS), :]
            cur, left, right = at(t, 0), at(t - 1, 0), at(t + 1, 0)
            east = shift_lanes(left, cur, right, 1) - shift_lanes(left, cur, right, -1)
            spot = slice((t - 1) * LANES, t * LANES)
            value = coefficients[0, to, spot] * (at(t, 1) - at(t, -1)) + coefficients[1, to, spot] * east
            value = value + coefficients[2, to, spot] * cur
            partial = part[to, spot]
            out[0, to, spot] = jnp.where(low, partial, partial + 2.0 * value)
        return carry

    lax.fori_loop(0, rows // SUBS, body, 0)


def ring(axis, step):
    count = lax.axis_size(axis)
    return [(i, (i + step) % count) for i in range(count)]


def shards(elevation, surface_potential, seabed, interior_potential):
    rows, width = elevation.shape
    layers, _, tile = interior_potential.shape
    assert 2 * rows == LANES and tile == 2 * width and layers == SUBS
    assert lax.axis_size("gz") == 2
    total_layers = layers * lax.axis_size("gz")
    f32 = jnp.float32
    shape = lambda *dims: jax.ShapeDtypeStruct(dims, f32)
    whole = lambda *dims: pl.BlockSpec(dims, lambda *_: (0,) * len(dims))
    group = lax.axis_index("gz").astype(jnp.int32).reshape((1,))
    scalar = pl.BlockSpec(memory_space=pltpu.SMEM)
    last_row, last_tile = rows // SUBS - 1, tile // LANES - 1

    def block(dims, *index):
        return pl.BlockSpec(dims, lambda *_: index)

    params = pltpu.CompilerParams(vmem_limit_bytes=24 * 1024 * 1024)
    vmem = pl.BlockSpec(memory_space=pltpu.VMEM)
    hbm = pl.BlockSpec(memory_space=pltpu.HBM)
    seam, outer, layer = pl.pallas_call(
        first_pack,
        out_shape=(shape(SUBS, LANES), shape(SUBS, LANES), shape(rows, tile)),
        in_specs=[scalar, hbm, hbm, hbm],
        out_specs=[vmem] * 3,
        scratch_shapes=[pltpu.VMEM((2, LANES, LANES), f32), pltpu.SemaphoreType.DMA((5,))],
        compiler_params=params,
        name="first_pack",
    )(group, *(pltpu.with_memory_space_constraint(x, pltpu.HBM) for x in (elevation, surface_potential, interior_potential)))

    flat = ("gy", "gz")
    count = lax.axis_size("gy")
    partner = [(2 * i + g, 2 * i + 1 - g) for i in range(count) for g in range(2)]
    across = [(2 * i + 1, (2 * i + 2) % (2 * count)) for i in range(count)]
    across = across + [(b, a) for a, b in across]
    seam = lax.ppermute(seam, flat, partner)
    far_layer = lax.ppermute(layer, flat, partner)
    outer = lax.ppermute(outer, flat, across)

    up, down, to_right, to_left = pl.pallas_call(
        lazy_pack,
        out_shape=(shape(SUBS, tile + tile // SUBS),) * 2 + (shape(SUBS, LANES),) * 2,
        grid=(1,),
        in_specs=[
            block((layers, SUBS, tile), 0, 0, 0),
            block((layers, SUBS, tile), 0, last_row, 0),
            block((layers, rows, LANES), 0, 0, 0),
            block((layers, rows, LANES), 0, 0, last_tile),
            block((SUBS, tile), 0, 0),
            block((SUBS, tile), last_row, 0),
            block((rows, LANES), 0, 0),
            block((rows, LANES), 0, last_tile),
        ],
        out_specs=[whole(SUBS, tile + tile // SUBS)] * 2 + [whole(SUBS, LANES)] * 2,
        compiler_params=params,
        name="lazy_pack",
    )(*(interior_potential,) * 4, *(seabed,) * 4)

    wide = width + 2 * LANES
    row_up, row_down = pl.pallas_call(
        row_pack,
        out_shape=(shape(2 * SUBS, wide),) * 2,
        grid=(1,),
        in_specs=[
            scalar,
            block((SUBS, width), 0, 0),
            block((SUBS, width), last_row, 0),
            block((SUBS, width), 0, 0),
            block((SUBS, width), last_row, 0),
            whole(SUBS, LANES),
            whole(SUBS, LANES),
        ],
        out_specs=[whole(2 * SUBS, wide)] * 2,
        compiler_params=params,
        name="row_pack",
    )(group, elevation, elevation, surface_potential, surface_potential, seam, outer)
    north = lax.ppermute(row_up, "gx", ring("gx", 1))
    south = lax.ppermute(row_down, "gx", ring("gx", -1))

    deep = rows + 3 * SUBS
    padded = (width // LANES + 2, deep, LANES)
    new_e, new_p, height, wide_e, wide_p = pl.pallas_call(
        surface,
        out_shape=(shape(rows, width),) * 2 + (shape(rows + SUBS, width),) + (shape(*padded),) * 2,
        in_specs=[scalar] + [vmem] * 6,
        out_specs=[vmem] * 5,
        scratch_shapes=[pltpu.VMEM(padded, f32)] * 4,
        compiler_params=params,
        name="surface",
    )(group, elevation, surface_potential, seam, outer, north, south)
    far_height = lax.ppermute(height, flat, partner)
    far_north = lax.ppermute(up, "gx", ring("gx", 1))
    far_south = lax.ppermute(down, "gx", ring("gx", -1))
    x_left = lax.ppermute(to_right, "gy", ring("gy", 1))
    x_right = lax.ppermute(to_left, "gy", ring("gy", -1))
    rims = pl.pallas_call(
        rim_pack,
        out_shape=shape(SUBS, width),
        in_specs=[scalar] + [vmem] * 4,
        out_specs=vmem,
        compiler_params=params,
        name="rim_pack",
    )(group, far_north, far_south, x_left, x_right)
    far_rims = lax.ppermute(rims, flat, partner)
    other_p = lax.ppermute(new_p, flat, partner)

    blocks = rows // SUBS
    tiles = tile // LANES
    tall = rows + 2 * SUBS
    volume, depth = pl.pallas_call(
        prepare,
        out_shape=(shape(layers, tiles + 2, tall, LANES), shape(tiles + 2, tall, LANES)),
        in_specs=[hbm] + [vmem] * 5,
        out_specs=[vmem] * 2,
        scratch_shapes=[pltpu.SemaphoreType.DMA((tiles,))],
        compiler_params=params,
        name="prepare",
    )(pltpu.with_memory_space_constraint(interior_potential, pltpu.HBM), seabed, far_north, far_south, x_left, x_right)
    partial, part, coefficients = pl.pallas_call(
        functools.partial(laplace, total_layers),
        out_shape=(shape(layers, rows, tile), shape(rows, width), shape(3, rows, width)),
        grid=(blocks,),
        in_specs=[scalar] + [vmem] * 7,
        out_specs=[
            pl.BlockSpec((layers, SUBS, tile), lambda i: (0, i, 0)),
            pl.BlockSpec((SUBS, width), lambda i: (i, 0)),
            pl.BlockSpec((3, SUBS, width), lambda i: (0, i, 0)),
        ],
        scratch_shapes=[pltpu.VMEM((tiles + 2, tall, LANES), f32)] * 2,
        compiler_params=params,
        name="laplace",
    )(group, volume, depth, far_layer, far_rims, wide_e, wide_p, far_height)
    result = pl.pallas_call(
        top,
        out_shape=shape(layers, rows, tile),
        grid_spec=pltpu.PrefetchScalarGridSpec(
            num_scalar_prefetch=1,
            grid=(1,),
            in_specs=[hbm] + [vmem] * 5,
            out_specs=pl.BlockSpec((1, rows, width), lambda i, g: (layers - 1, 0, 1 - g[0])),
            scratch_shapes=[pltpu.VMEM((width // LANES + 2, tall, LANES), f32)],
        ),
        input_output_aliases={1: 0},
        compiler_params=params,
        name="top",
    )(group, partial, part, coefficients, far_height, wide_p, other_p)
    return new_e, new_p, result


def solution(mesh):
    return jax.shard_map(
        shards,
        mesh=mesh,
        in_specs=(P("gx", ("gy", "gz")), P("gx", ("gy", "gz")), P("gx", "gy"), P("gz", "gx", "gy")),
        out_specs=(P("gx", ("gy", "gz")), P("gx", ("gy", "gz")), P("gz", "gx", "gy")),
        check_vma=False,
    )
```

```python
import functools

import jax
import jax.numpy as jnp
from jax import lax
from jax.experimental import pallas as pl
from jax.experimental.pallas import tpu as pltpu
from jax.sharding import PartitionSpec as P

time_step = 0.05
depth_unit = 0.015625
LANES = 128
SUBS = 8


def shift_lanes(left, cur, right, step):
    lane = lax.broadcasted_iota(jnp.int32, cur.shape, 1)
    if step < 0:
        return pltpu.roll(jnp.where(lane >= LANES + step, left, cur), -step, 1)
    return pltpu.roll(jnp.where(lane < step, right, cur), LANES - step, 1)


def square(tile, at_end):
    rest = jnp.zeros((LANES - tile.shape[0], LANES), tile.dtype)
    return jnp.concatenate([rest, tile] if at_end else [tile, rest], 0)


def first_pack(group, e, p, v, seam, outer, layer, edges, sems):
    rows, width = e.shape
    low = group[0] == 0
    source = jnp.where(low, v.shape[0] - 1, 0)
    whole = pltpu.make_async_copy(v.at[source], layer, sems.at[4])
    copies = []
    for index, (field, start) in enumerate(((e, 0), (p, 0), (e, width - LANES), (p, width - LANES))):
        into = edges.at[index // 2, (index % 2) * rows : (index % 2 + 1) * rows, :]
        copies.append(pltpu.make_async_copy(field.at[:, start : start + LANES], into, sems.at[index]))
    for copy in copies:
        copy.start()
    whole.start()
    for copy in copies:
        copy.wait()
    left = edges[0].T[:SUBS]
    right = edges[1].T[LANES - SUBS :]
    seam[...] = jnp.where(low, right, left)
    whole.wait()
    tile = layer.shape[1]
    sides = jnp.concatenate([layer[:, :LANES], layer[:, tile - LANES :]], 0).T
    ends = pltpu.roll(sides[LANES - SUBS :], LANES // 2, 1)
    side = jnp.where(low, sides[:1], ends[SUBS - 1 :])
    sub = lax.broadcasted_iota(jnp.int32, outer.shape, 0)
    place = jnp.where(low, SUBS - 1, 0)
    outer[...] = jnp.where(sub == place, side, jnp.where(low, left, right))


def lazy_pack(v_top, v_bottom, v_left, v_right, s_top, s_bottom, s_left, s_right, up, down, to_right, to_left):
    layers, _, width = v_top.shape
    piece = width // SUBS
    for k in range(layers):
        up[k : k + 1, :width] = v_bottom[k, SUBS - 1 : SUBS, :]
        down[k : k + 1, :width] = v_top[k, 0:1, :]
    for q in range(SUBS):
        part = slice(q * piece, (q + 1) * piece)
        up[q : q + 1, width:] = s_bottom[SUBS - 1 : SUBS, part].astype(jnp.float32) * depth_unit
        down[q : q + 1, width:] = s_top[0:1, part].astype(jnp.float32) * depth_unit
    to_right[...] = jnp.zeros_like(to_right)
    to_left[...] = jnp.zeros_like(to_left)
    for j in range(layers // 2):
        both = jnp.concatenate([v_right[2 * j], v_right[2 * j + 1]], 0).T
        to_right[j : j + 1, :] = both[LANES - 1 :]
        both = jnp.concatenate([v_left[2 * j], v_left[2 * j + 1]], 0).T
        to_left[j : j + 1, :] = both[:1]
    j = layers // 2
    both = jnp.concatenate([s_right[...], s_right[...]], 0).astype(jnp.float32) * depth_unit
    to_right[j : j + 1, :] = both.T[LANES - 1 :]
    both = jnp.concatenate([s_left[...], s_left[...]], 0).astype(jnp.float32) * depth_unit
    to_left[j : j + 1, :] = both.T[:1]


def side_blocks(low, seam, outer):
    left = square(jnp.where(low, outer, seam), True).T
    right = square(jnp.where(low, seam, outer), False).T
    return left, right


def row_pack(group, e_top, e_bottom, p_top, p_bottom, seam, outer, up, down):
    left, right = side_blocks(group[0] == 0, seam[...], outer[...])
    rows = LANES // 2
    width = e_top.shape[1]
    for row, tops, bottoms in ((0, e_top, e_bottom), (SUBS, p_top, p_bottom)):
        base = 0 if row == 0 else rows
        up[row : row + SUBS, :LANES] = left[base + rows - SUBS : base + rows]
        up[row : row + SUBS, LANES : LANES + width] = bottoms[...]
        up[row : row + SUBS, LANES + width :] = right[base + rows - SUBS : base + rows]
        down[row : row + SUBS, :LANES] = left[base : base + SUBS]
        down[row : row + SUBS, LANES : LANES + width] = tops[...]
        down[row : row + SUBS, LANES + width :] = right[base : base + SUBS]


def neighbourhood(ref, lane_tile, row):
    last = ref.shape[0] - 1
    at = lambda column, step: ref[column, pl.ds(row + step, SUBS), :]
    cur = at(lane_tile, 0)
    left, right = at(max(lane_tile - 1, 0), 0), at(min(lane_tile + 1, last), 0)
    rows = [at(lane_tile, step) for step in (-2, -1, 1, 2)]
    lanes = [shift_lanes(left, cur, right, step) for step in (-2, -1, 1, 2)]
    return cur, rows, lanes


def slope(values):
    return (2.0 / 3.0) * (values[2] - values[1]) - (1.0 / 12.0) * (values[3] - values[0])


def tile_rates(e_near, p_near):
    e, e_rows, e_lanes = e_near
    p, p_rows, p_lanes = p_near
    p_x, p_y = slope(p_rows), slope(p_lanes)
    near = (p_rows[1] + p_rows[2]) + (p_lanes[1] + p_lanes[2])
    far = (p_rows[0] + p_rows[3]) + (p_lanes[0] + p_lanes[3])
    bend = (4.0 / 3.0) * near - (1.0 / 12.0) * far - 5.0 * p
    rate_e = bend - (slope(e_rows) * p_x + slope(e_lanes) * p_y)
    rate_p = 0.5 * (p_x * p_x + p_y * p_y) + e
    return e, p, time_step * rate_e, -time_step * rate_p


def surface(
    group, e, p, seam, outer, north, south,
    new_e, new_p, height, wide_e, wide_p, e0, p0, e1, p1,
):
    rows, width = e.shape
    low = group[0] == 0
    left, right = side_blocks(low, seam[...], outer[...])
    tiles = width // LANES + 2
    inner = slice(SUBS, SUBS + rows)
    for old, source, base in ((e0, e, 0), (p0, p, LANES // 2)):
        half = SUBS if base else 0
        for t in range(tiles):
            part = slice(t * LANES, (t + 1) * LANES)
            old[t, :SUBS, :] = north[half : half + SUBS, part]
            old[t, SUBS + rows : 2 * SUBS + rows, :] = south[half : half + SUBS, part]
            if 0 < t < tiles - 1:
                old[t, inner, :] = source[:, (t - 1) * LANES : t * LANES]
        old[0, inner, :] = left[base : base + rows]
        old[tiles - 1, inner, :] = right[base : base + rows]
    blocks = rows // SUBS + 1

    def first(block, carry):
        row = block * SUBS + SUBS - 3
        for t in range(tiles):
            old_e, old_p, step_e, step_p = tile_rates(neighbourhood(e0, t, row), neighbourhood(p0, t, row))
            e1[t, pl.ds(row, SUBS), :] = old_e + step_e
            p1[t, pl.ds(row, SUBS), :] = old_p + step_p
        return carry

    lax.fori_loop(0, blocks, first, 0)

    def second(block, carry):
        row = block * SUBS + SUBS - 1
        for t in range(tiles):
            one_e, one_p, step_e, step_p = tile_rates(neighbourhood(e1, t, row), neighbourhood(p1, t, row))
            old_e = e0[t, pl.ds(row, SUBS), :]
            old_p = p0[t, pl.ds(row, SUBS), :]
            wide_e[t, pl.ds(row, SUBS), :] = 0.5 * ((old_e + one_e) + step_e)
            wide_p[t, pl.ds(row, SUBS), :] = 0.5 * ((old_p + one_p) + step_p)
        return carry

    lax.fori_loop(0, blocks, second, 0)
    for t in range(1, tiles - 1):
        part = slice((t - 1) * LANES, t * LANES)
        tile_e = wide_e[t, inner, :]
        new_e[:, part] = tile_e
        height[:rows, part] = tile_e
        new_p[:, part] = wide_p[t, inner, :]
        for row, wide in ((0, wide_e), (2, wide_p)):
            height[rows + row : rows + row + 1, part] = wide[t, SUBS - 1 : SUBS, :]
            height[rows + row + 1 : rows + row + 2, part] = wide[t, SUBS + rows : SUBS + rows + 1, :]
        height[rows + 4 :, part] = jnp.zeros((4, LANES), jnp.float32)
    left = jnp.concatenate([wide_e[0, inner, :], wide_p[0, inner, :]], 0).T[LANES - 1 :]
    right = jnp.concatenate([wide_e[tiles - 1, inner, :], wide_p[tiles - 1, inner, :]], 0).T[:1]
    height[rows + 4 : rows + 5, :LANES] = jnp.where(low, left, right)


def rim_pack(group, far_north, far_south, x_left, x_right, rims):
    low = group[0] == 0
    layers = far_north.shape[0]
    width = rims.shape[1]
    pairs = layers // 2
    rims[...] = jnp.zeros_like(rims)
    for row, side in ((0, far_north), (2, far_south)):
        for half in range(2):
            part = slice(half * width, (half + 1) * width)
            rims[row + half : row + half + 1, :] = jnp.where(low, side[layers - 1 : layers, part], side[0:1, part])
    for lane, side in ((0, x_left), (LANES, x_right)):
        top_pair = pltpu.roll(side[...], LANES // 2, 1)[pairs - 1 : pairs]
        rims[4:5, lane : lane + LANES] = jnp.where(low, top_pair, side[0:1, :])


def prepare(v, sea, volume, depth, sems):
    _, rows, tile = v.shape
    inner = slice(SUBS, SUBS + rows)
    copies = []
    for t in range(tile // LANES):
        part = slice(t * LANES, (t + 1) * LANES)
        copies.append(pltpu.make_async_copy(v.at[:, :, part], volume.at[:, t + 1, inner, :], sems.at[t]))
        copies[-1].start()
    for t in range(tile // LANES):
        depth[t + 1, inner, :] = sea[:, t * LANES : (t + 1) * LANES].astype(jnp.float32) * depth_unit
    for copy in copies:
        copy.wait()


def run_all(copies):
    for copy in copies:
        copy.start()
    for copy in copies:
        copy.wait()


def fill_columns(old_volume, old_depth, x_left, x_right, volume, depth, sides, depths, sems):
    del old_volume, old_depth
    layers, tiles, rows = volume.shape[0], volume.shape[1], sides.shape[2]
    inner = slice(SUBS, SUBS + rows)
    left = square(x_left[...], False).T
    right = square(x_right[...], False).T
    half, pairs = LANES // 2, layers // 2
    for k in range(layers):
        base = (k % 2) * half
        sides[0, k] = pltpu.roll(left, LANES - 1 - k // 2, 1)[base : base + rows]
        sides[1, k] = pltpu.roll(right, (LANES - k // 2) % LANES, 1)[base : base + rows]
    depths[0] = pltpu.roll(left, LANES - 1 - pairs, 1)[:rows]
    depths[1] = pltpu.roll(right, LANES - pairs, 1)[:rows]
    copies = []
    for side, t in ((0, 0), (1, tiles - 1)):
        copies.append(pltpu.make_async_copy(sides.at[side], volume.at[:, t, inner, :], sems.at[2 * side]))
        copies.append(pltpu.make_async_copy(depths.at[side], depth.at[t, inner, :], sems.at[2 * side + 1]))
    run_all(copies)


def fill_rows(old_volume, old_depth, token, far_north, far_south, volume, depth, edges, depths, sems):
    del old_volume, old_depth, token
    layers, tiles, tall = volume.shape[0], volume.shape[1], volume.shape[2]
    tile = (tiles - 2) * LANES
    piece = tile // SUBS // LANES
    for end, source, row in ((0, far_north, SUBS - 1), (1, far_south, 0)):
        for t in range(tiles - 2):
            for k in range(layers):
                edges[end, k, t + 1, row : row + 1, :] = source[k : k + 1, t * LANES : (t + 1) * LANES]
            q, start = t // piece, tile + (t % piece) * LANES
            depths[end, t + 1, row : row + 1, :] = source[q : q + 1, start : start + LANES]
    copies = []
    for end, rows in ((0, slice(0, SUBS)), (1, slice(tall - SUBS, tall))):
        copies.append(pltpu.make_async_copy(edges.at[end], volume.at[:, :, rows, :], sems.at[2 * end]))
        copies.append(pltpu.make_async_copy(depths.at[end], depth.at[:, rows, :], sems.at[2 * end + 1]))
    run_all(copies)


def apply_tile(total_layers, group, block, volume, depth, t, heights, local, ghost, spot, mine, write, rest=None):
    low = group == 0
    layers = volume.shape[0]
    spacing = 1.0 / total_layers
    sigma = (group * layers).astype(jnp.float32) * spacing + 0.5 * spacing
    gain = (2 * group).astype(jnp.float32)
    here = pl.multiple_of((block + 1) * SUBS, SUBS)

    def near(ref, t):
        at = lambda column, step: ref[column, pl.ds(here + step, SUBS), :]
        cur = at(t, 0)
        left, right = at(t - 1, 0), at(t + 1, 0)
        return cur, at(t, -1), at(t, 1), shift_lanes(left, cur, right, -1), shift_lanes(left, cur, right, 1)

    def differences(ref, t):
        p, up, down, left, right = near(ref, t)
        return p, down - up, right - left

    d, d_x, d_y = differences(depth, t)
    h, h_x, h_y = differences(heights, local)
    inverse = 1.0 / (d + h)
    scale = (0.25 / spacing) * inverse
    bx, by = scale * (d_x + h_x), scale * (d_y + h_y)
    ux, uy = scale * d_x - sigma * bx, scale * d_y - sigma * by
    bx, by = spacing * bx, spacing * by
    scaled = inverse * (1.0 / spacing)
    weight = 4.0 * (ux * ux + uy * uy) + scaled * scaled
    bend = 4.0 * (bx * bx + by * by)
    step = bend - 8.0 * (ux * bx + uy * by)
    bend = bend + bend

    def level(k):
        p, up, down, left, right = near(volume.at[k], t)
        return p, down - up, right - left, ((down + up) + (right + left)) - 4.0 * p

    far = differences(ghost, spot)
    this = level(0)
    lower = [jnp.where(low, a, b) for a, b in zip(this, far)]
    rise_below = this[0] - lower[0]
    for k in range(layers):
        if k < layers - 1:
            upper = level(k + 1)
        else:
            upper = [jnp.where(low, a, -b) for a, b in zip(far, this)]
            if mine is not None:
                upper = [a + gain * b for a, b in zip(upper, differences(mine, local))]
        rise = upper[0] - this[0]
        value = this[3] + ux * (upper[1] - lower[1]) + uy * (upper[2] - lower[2])
        value = value + weight * (rise - rise_below)
        write(k, value)
        if k < layers - 1:
            ux, uy = ux - bx, uy - by
            weight, step = weight + step, step + bend
        elif rest is not None:
            rest(value, ux, uy, weight)
        lower, this, rise_below = this, upper, rise


def lanes_of(local):
    return pl.ds(pl.multiple_of((local - 1) * LANES, LANES), LANES)


def inside(total_layers, group_ref, volume, depth, far_layer, outer, wide_e, wide_p, out, token, ghost):
    group = group_ref[0]
    low = group == 0
    rows, tile = far_layer.shape
    width = tile // 2
    halves = width // LANES
    inner = slice(SUBS, SUBS + rows)

    @pl.when(pl.program_id(0) == 0)
    def _():
        token[...] = jnp.zeros_like(token)
        edge = square(outer[...], False).T[:rows]
        at_left = pltpu.roll(edge, LANES - 1, 1)
        at_right = pltpu.roll(edge, LANES - (SUBS - 1), 1)
        ghost[0, inner, :] = jnp.where(low, at_left, far_layer[:, width - LANES : width])
        ghost[halves + 1, inner, :] = jnp.where(low, far_layer[:, width : width + LANES], at_right)
        for t in range(halves):
            lanes = pl.ds(pl.multiple_of(group * width + t * LANES, LANES), LANES)
            ghost[t + 1, inner, :] = far_layer[:, lanes]

    def pair(index, carry):
        for step in range(2):
            local = index * 2 + step + 1

            def write(k, value):
                out[k, :, lanes_of(local)] = value

            apply_tile(
                total_layers, group, pl.program_id(0) + 1, volume, depth, group * halves + local,
                wide_e, local, ghost, local, wide_p, write,
            )
        return carry

    lax.fori_loop(0, halves // 2, pair, 0)


def outside(
    total_layers, group_ref, before, volume, depth, far_layer, rims, wide_e, wide_p, height,
    out, part, coefficients, ghost, other_e,
):
    del before
    index = pl.program_id(0)
    group = group_ref[0]
    low = group == 0
    rows, tile = far_layer.shape
    width = tile // 2
    tiles, halves = tile // LANES, width // LANES
    last = rows // SUBS - 1
    inner = slice(SUBS, SUBS + rows)

    @pl.when(index == 0)
    def _():
        far_left = pltpu.roll(square(rims[:, :LANES], False).T, LANES - 5, 1)[:rows]
        far_right = pltpu.roll(square(rims[:, LANES : 2 * LANES], False).T, LANES - 4, 1)[:rows]
        ghost[0, inner, :] = far_left
        ghost[tiles + 1, inner, :] = far_right
        for t in range(tiles):
            ghost[t + 1, inner, :] = far_layer[:, t * LANES : (t + 1) * LANES]
            half, spot = t // halves, slice((t % halves) * LANES, (t % halves + 1) * LANES)
            ghost[t + 1, SUBS - 1 : SUBS, :] = rims[half : half + 1, spot]
            ghost[t + 1, SUBS + rows : SUBS + rows + 1, :] = rims[2 + half : 3 + half, spot]
        for t in range(halves):
            spot = slice(t * LANES, (t + 1) * LANES)
            other_e[t + 1, inner, :] = height[:rows, spot]
            other_e[t + 1, SUBS - 1 : SUBS, :] = height[rows : rows + 1, spot]
            other_e[t + 1, SUBS + rows : SUBS + rows + 1, :] = height[rows + 1 : rows + 2, spot]
        edge = square(height[rows:, :LANES], False).T[:rows]
        at_right, at_left = pltpu.roll(edge, LANES - 4, 1), pltpu.roll(edge, LANES - 5, 1)
        other_e[0, inner, :] = jnp.where(low, wide_e[halves, inner, :], at_left)
        other_e[halves + 1, inner, :] = jnp.where(low, at_right, wide_e[1, inner, :])

    def own_pair(pair, carry):
        for step in range(2):
            local = pair * 2 + step + 1
            t = group * halves + local

            def write(k, value):
                out[k, :, lanes_of(local)] = value

            apply_tile(
                total_layers, group, index * last, volume, depth, t, wide_e, local, ghost, t, wide_p, write
            )
        return carry

    def other_pair(pair, carry):
        for step in range(2):
            local = pair * 2 + step + 1
            t = (1 - group) * halves + local

            def write(k, value):
                out[k, :, lanes_of(local)] = value

            def rest(value, ux, uy, weight):
                part[:, lanes_of(local)] = value
                coefficients[0, :, lanes_of(local)] = ux
                coefficients[1, :, lanes_of(local)] = uy
                coefficients[2, :, lanes_of(local)] = weight

            apply_tile(
                total_layers, group, index - 2, volume, depth, t, other_e, local, ghost, t, None, write, rest
            )
        return carry

    @pl.when(index < 2)
    def _():
        lax.fori_loop(0, halves // 2, own_pair, 0)

    @pl.when(index >= 2)
    def _():
        lax.fori_loop(0, halves // 2, other_pair, 0)


def top(group_ref, before, part, coefficients, height, wide_p, other_p, out, potential):
    del before
    low = group_ref[0] == 0
    rows, width = other_p.shape
    halves = width // LANES
    inner = slice(SUBS, SUBS + rows)
    edge = square(height[rows:, :LANES], False).T[LANES // 2 : LANES // 2 + rows]
    potential[0, inner, :] = pltpu.roll(edge, LANES - 5, 1)
    potential[halves + 1, inner, :] = wide_p[1, inner, :]
    for t in range(halves):
        spot = slice(t * LANES, (t + 1) * LANES)
        potential[t + 1, inner, :] = other_p[:, spot]
        potential[t + 1, SUBS - 1 : SUBS, :] = height[rows + 2 : rows + 3, spot]
        potential[t + 1, SUBS + rows : SUBS + rows + 1, :] = height[rows + 3 : rows + 4, spot]

    def body(block, carry):
        here = pl.multiple_of((block + 1) * SUBS, SUBS)
        to = pl.ds(pl.multiple_of(block * SUBS, SUBS), SUBS)
        for t in range(1, halves + 1):
            at = lambda column, step: potential[column, pl.ds(here + step, SUBS), :]
            cur, left, right = at(t, 0), at(t - 1, 0), at(t + 1, 0)
            east = shift_lanes(left, cur, right, 1) - shift_lanes(left, cur, right, -1)
            spot = slice((t - 1) * LANES, t * LANES)
            value = coefficients[0, to, spot] * (at(t, 1) - at(t, -1)) + coefficients[1, to, spot] * east
            value = value + coefficients[2, to, spot] * cur
            partial = part[to, spot]
            out[0, to, spot] = jnp.where(low, partial, partial + 2.0 * value)
        return carry

    lax.fori_loop(0, rows // SUBS, body, 0)


def ring(axis, step):
    count = lax.axis_size(axis)
    return [(i, (i + step) % count) for i in range(count)]


def shards(elevation, surface_potential, seabed, interior_potential):
    rows, width = elevation.shape
    layers, _, tile = interior_potential.shape
    assert 2 * rows == LANES and tile == 2 * width and layers == SUBS
    assert lax.axis_size("gz") == 2
    total_layers = layers * lax.axis_size("gz")
    f32 = jnp.float32
    shape = lambda *dims: jax.ShapeDtypeStruct(dims, f32)
    whole = lambda *dims: pl.BlockSpec(dims, lambda *_: (0,) * len(dims))
    group = lax.axis_index("gz").astype(jnp.int32).reshape((1,))
    scalar = pl.BlockSpec(memory_space=pltpu.SMEM)
    last_row, last_tile = rows // SUBS - 1, tile // LANES - 1

    def block(dims, *index):
        return pl.BlockSpec(dims, lambda *_: index)

    params = pltpu.CompilerParams(vmem_limit_bytes=24 * 1024 * 1024)
    vmem = pl.BlockSpec(memory_space=pltpu.VMEM)
    hbm = pl.BlockSpec(memory_space=pltpu.HBM)
    seam, outer, layer = pl.pallas_call(
        first_pack,
        out_shape=(shape(SUBS, LANES), shape(SUBS, LANES), shape(rows, tile)),
        in_specs=[scalar, hbm, hbm, hbm],
        out_specs=[vmem] * 3,
        scratch_shapes=[pltpu.VMEM((2, LANES, LANES), f32), pltpu.SemaphoreType.DMA((5,))],
        compiler_params=params,
        name="first_pack",
    )(group, *(pltpu.with_memory_space_constraint(x, pltpu.HBM) for x in (elevation, surface_potential, interior_potential)))

    flat = ("gy", "gz")
    count = lax.axis_size("gy")
    partner = [(2 * i + g, 2 * i + 1 - g) for i in range(count) for g in range(2)]
    across = [(2 * i + 1, (2 * i + 2) % (2 * count)) for i in range(count)]
    across = across + [(b, a) for a, b in across]
    seam = lax.ppermute(seam, flat, partner)
    far_layer = lax.ppermute(layer, flat, partner)
    outer = lax.ppermute(outer, flat, across)

    tiles = tile // LANES
    tall = rows + 2 * SUBS
    tables = (shape(layers, tiles + 2, tall, LANES), shape(tiles + 2, tall, LANES))
    anywhere = pl.BlockSpec(memory_space=pl.ANY)
    volume, depth = pl.pallas_call(
        prepare,
        out_shape=tables,
        in_specs=[hbm, vmem],
        out_specs=[vmem] * 2,
        scratch_shapes=[pltpu.SemaphoreType.DMA((tiles,))],
        compiler_params=params,
        name="prepare",
    )(pltpu.with_memory_space_constraint(interior_potential, pltpu.HBM), seabed)

    up, down, to_right, to_left = pl.pallas_call(
        lazy_pack,
        out_shape=(shape(SUBS, tile + tile // SUBS),) * 2 + (shape(SUBS, LANES),) * 2,
        grid=(1,),
        in_specs=[
            block((layers, SUBS, tile), 0, 0, 0),
            block((layers, SUBS, tile), 0, last_row, 0),
            block((layers, rows, LANES), 0, 0, 0),
            block((layers, rows, LANES), 0, 0, last_tile),
            block((SUBS, tile), 0, 0),
            block((SUBS, tile), last_row, 0),
            block((rows, LANES), 0, 0),
            block((rows, LANES), 0, last_tile),
        ],
        out_specs=[whole(SUBS, tile + tile // SUBS)] * 2 + [whole(SUBS, LANES)] * 2,
        compiler_params=params,
        name="lazy_pack",
    )(*(interior_potential,) * 4, *(seabed,) * 4)

    wide = width + 2 * LANES
    row_up, row_down = pl.pallas_call(
        row_pack,
        out_shape=(shape(2 * SUBS, wide),) * 2,
        grid=(1,),
        in_specs=[
            scalar,
            block((SUBS, width), 0, 0),
            block((SUBS, width), last_row, 0),
            block((SUBS, width), 0, 0),
            block((SUBS, width), last_row, 0),
            whole(SUBS, LANES),
            whole(SUBS, LANES),
        ],
        out_specs=[whole(2 * SUBS, wide)] * 2,
        compiler_params=params,
        name="row_pack",
    )(group, elevation, elevation, surface_potential, surface_potential, seam, outer)
    north = lax.ppermute(row_up, "gx", ring("gx", 1))
    south = lax.ppermute(row_down, "gx", ring("gx", -1))

    deep = rows + 3 * SUBS
    padded = (width // LANES + 2, deep, LANES)
    new_e, new_p, height, wide_e, wide_p = pl.pallas_call(
        surface,
        out_shape=(shape(rows, width),) * 2 + (shape(rows + SUBS, width),) + (shape(*padded),) * 2,
        in_specs=[scalar] + [vmem] * 6,
        out_specs=[vmem] * 5,
        scratch_shapes=[pltpu.VMEM(padded, f32)] * 4,
        compiler_params=params,
        name="surface",
    )(group, elevation, surface_potential, seam, outer, north, south)
    far_height = lax.ppermute(height, flat, partner)
    far_north = lax.ppermute(up, "gx", ring("gx", 1))
    far_south = lax.ppermute(down, "gx", ring("gx", -1))
    x_left = lax.ppermute(to_right, "gy", ring("gy", 1))
    x_right = lax.ppermute(to_left, "gy", ring("gy", -1))
    volume, depth = pl.pallas_call(
        fill_columns,
        out_shape=tables,
        in_specs=[anywhere] * 2 + [vmem] * 2,
        out_specs=[anywhere] * 2,
        scratch_shapes=[
            pltpu.VMEM((2, layers, rows, LANES), f32),
            pltpu.VMEM((2, rows, LANES), f32),
            pltpu.SemaphoreType.DMA((4,)),
        ],
        input_output_aliases={0: 0, 1: 1},
        compiler_params=params,
        name="fill_columns",
    )(volume, depth, x_left, x_right)
    blocks = rows // SUBS
    partial, token = pl.pallas_call(
        functools.partial(inside, total_layers),
        out_shape=(shape(layers, rows, tile), shape(SUBS, LANES)),
        grid_spec=pltpu.PrefetchScalarGridSpec(
            num_scalar_prefetch=1,
            grid=(blocks - 2,),
            in_specs=[vmem] * 6,
            out_specs=[
                pl.BlockSpec((layers, SUBS, width), lambda i, g: (0, i + 1, g[0])),
                pl.BlockSpec((SUBS, LANES), lambda i, g: (0, 0)),
            ],
            scratch_shapes=[pltpu.VMEM((width // LANES + 2, tall, LANES), f32)],
        ),
        compiler_params=params,
        name="inside",
    )(group, volume, depth, far_layer, outer, wide_e, wide_p)
    rims = pl.pallas_call(
        rim_pack,
        out_shape=shape(SUBS, width),
        in_specs=[scalar] + [vmem] * 4,
        out_specs=vmem,
        compiler_params=params,
        name="rim_pack",
    )(group, far_north, far_south, x_left, x_right)
    far_rims = lax.ppermute(rims, flat, partner)
    other_p = lax.ppermute(new_p, flat, partner)

    volume, depth = pl.pallas_call(
        fill_rows,
        out_shape=tables,
        in_specs=[anywhere] * 2 + [vmem] * 3,
        out_specs=[anywhere] * 2,
        scratch_shapes=[
            pltpu.VMEM((2, layers, tiles + 2, SUBS, LANES), f32),
            pltpu.VMEM((2, tiles + 2, SUBS, LANES), f32),
            pltpu.SemaphoreType.DMA((4,)),
        ],
        input_output_aliases={0: 0, 1: 1},
        compiler_params=params,
        name="fill_rows",
    )(volume, depth, token, far_north, far_south)

    def place(i, g):
        own = i < 2
        return 0, jnp.where(own, i * (blocks - 1), i - 2), jnp.where(own, g[0], 1 - g[0])

    partial, part, coefficients = pl.pallas_call(
        functools.partial(outside, total_layers),
        out_shape=(shape(layers, rows, tile), shape(rows, width), shape(3, rows, width)),
        grid_spec=pltpu.PrefetchScalarGridSpec(
            num_scalar_prefetch=1,
            grid=(blocks + 2,),
            in_specs=[hbm] + [vmem] * 7,
            out_specs=[
                pl.BlockSpec((layers, SUBS, width), place),
                pl.BlockSpec((SUBS, width), lambda i, g: (jnp.maximum(i - 2, 0), 0)),
                pl.BlockSpec((3, SUBS, width), lambda i, g: (0, jnp.maximum(i - 2, 0), 0)),
            ],
            scratch_shapes=[
                pltpu.VMEM((tiles + 2, tall, LANES), f32),
                pltpu.VMEM((width // LANES + 2, tall, LANES), f32),
            ],
        ),
        input_output_aliases={1: 0},
        compiler_params=params,
        name="outside",
    )(group, partial, volume, depth, far_layer, far_rims, wide_e, wide_p, far_height)
    result = pl.pallas_call(
        top,
        out_shape=shape(layers, rows, tile),
        grid_spec=pltpu.PrefetchScalarGridSpec(
            num_scalar_prefetch=1,
            grid=(1,),
            in_specs=[hbm] + [vmem] * 5,
            out_specs=pl.BlockSpec((1, rows, width), lambda i, g: (layers - 1, 0, 1 - g[0])),
            scratch_shapes=[pltpu.VMEM((width // LANES + 2, tall, LANES), f32)],
        ),
        input_output_aliases={1: 0},
        compiler_params=params,
        name="top",
    )(group, partial, part, coefficients, far_height, wide_p, other_p)
    return new_e, new_p, result


def solution(mesh):
    return jax.shard_map(
        shards,
        mesh=mesh,
        in_specs=(P("gx", ("gy", "gz")), P("gx", ("gy", "gz")), P("gx", "gy"), P("gz", "gx", "gy")),
        out_specs=(P("gx", ("gy", "gz")), P("gx", ("gy", "gz")), P("gz", "gx", "gy")),
        check_vma=False,
    )
```

```python
import functools

import jax
import jax.numpy as jnp
from jax import lax
from jax.experimental import pallas as pl
from jax.experimental.pallas import tpu as pltpu
from jax.sharding import PartitionSpec as P

time_step = 0.05
depth_unit = 0.015625
LANES = 128
SUBS = 8


def shift_lanes(left, cur, right, step):
    lane = lax.broadcasted_iota(jnp.int32, cur.shape, 1)
    if step < 0:
        return pltpu.roll(jnp.where(lane >= LANES + step, left, cur), -step, 1)
    return pltpu.roll(jnp.where(lane < step, right, cur), LANES - step, 1)


def square(tile, at_end):
    rest = jnp.zeros((LANES - tile.shape[0], LANES), tile.dtype)
    return jnp.concatenate([rest, tile] if at_end else [tile, rest], 0)


def first_pack(group, e, p, v, seam, outer, layer, edges, sems):
    rows, width = e.shape
    low = group[0] == 0
    source = jnp.where(low, v.shape[0] - 1, 0)
    whole = pltpu.make_async_copy(v.at[source], layer, sems.at[4])
    copies = []
    for index, (field, start) in enumerate(((e, 0), (p, 0), (e, width - LANES), (p, width - LANES))):
        into = edges.at[index // 2, (index % 2) * rows : (index % 2 + 1) * rows, :]
        copies.append(pltpu.make_async_copy(field.at[:, start : start + LANES], into, sems.at[index]))
    for copy in copies:
        copy.start()
    whole.start()
    for copy in copies:
        copy.wait()
    left = edges[0].T[:SUBS]
    right = edges[1].T[LANES - SUBS :]
    seam[...] = jnp.where(low, right, left)
    outer[...] = jnp.where(low, left, right)
    whole.wait()


def lazy_pack(v_top, v_bottom, v_left, v_right, s_top, s_bottom, s_left, s_right, up, down, to_right, to_left):
    layers, _, width = v_top.shape
    piece = width // SUBS
    for k in range(layers):
        up[k : k + 1, :width] = v_bottom[k, SUBS - 1 : SUBS, :]
        down[k : k + 1, :width] = v_top[k, 0:1, :]
    for q in range(SUBS):
        part = slice(q * piece, (q + 1) * piece)
        up[q : q + 1, width:] = s_bottom[SUBS - 1 : SUBS, part].astype(jnp.float32) * depth_unit
        down[q : q + 1, width:] = s_top[0:1, part].astype(jnp.float32) * depth_unit
    to_right[...] = jnp.zeros_like(to_right)
    to_left[...] = jnp.zeros_like(to_left)
    for j in range(layers // 2):
        both = jnp.concatenate([v_right[2 * j], v_right[2 * j + 1]], 0).T
        to_right[j : j + 1, :] = both[LANES - 1 :]
        both = jnp.concatenate([v_left[2 * j], v_left[2 * j + 1]], 0).T
        to_left[j : j + 1, :] = both[:1]
    j = layers // 2
    both = jnp.concatenate([s_right[...], s_right[...]], 0).astype(jnp.float32) * depth_unit
    to_right[j : j + 1, :] = both.T[LANES - 1 :]
    both = jnp.concatenate([s_left[...], s_left[...]], 0).astype(jnp.float32) * depth_unit
    to_left[j : j + 1, :] = both.T[:1]


def side_blocks(low, seam, outer):
    left = square(jnp.where(low, outer, seam), True).T
    right = square(jnp.where(low, seam, outer), False).T
    return left, right


def row_pack(group, e_top, e_bottom, p_top, p_bottom, seam, outer, up, down):
    left, right = side_blocks(group[0] == 0, seam[...], outer[...])
    rows = LANES // 2
    width = e_top.shape[1]
    for row, tops, bottoms in ((0, e_top, e_bottom), (SUBS, p_top, p_bottom)):
        base = 0 if row == 0 else rows
        up[row : row + SUBS, :LANES] = left[base + rows - SUBS : base + rows]
        up[row : row + SUBS, LANES : LANES + width] = bottoms[...]
        up[row : row + SUBS, LANES + width :] = right[base + rows - SUBS : base + rows]
        down[row : row + SUBS, :LANES] = left[base : base + SUBS]
        down[row : row + SUBS, LANES : LANES + width] = tops[...]
        down[row : row + SUBS, LANES + width :] = right[base : base + SUBS]


def neighbourhood(ref, lane_tile, row):
    last = ref.shape[0] - 1
    at = lambda column, step: ref[column, pl.ds(row + step, SUBS), :]
    cur = at(lane_tile, 0)
    left, right = at(max(lane_tile - 1, 0), 0), at(min(lane_tile + 1, last), 0)
    rows = [at(lane_tile, step) for step in (-2, -1, 1, 2)]
    lanes = [shift_lanes(left, cur, right, step) for step in (-2, -1, 1, 2)]
    return cur, rows, lanes


def slope(values):
    return (2.0 / 3.0) * (values[2] - values[1]) - (1.0 / 12.0) * (values[3] - values[0])


def tile_rates(e_near, p_near):
    e, e_rows, e_lanes = e_near
    p, p_rows, p_lanes = p_near
    p_x, p_y = slope(p_rows), slope(p_lanes)
    near = (p_rows[1] + p_rows[2]) + (p_lanes[1] + p_lanes[2])
    far = (p_rows[0] + p_rows[3]) + (p_lanes[0] + p_lanes[3])
    bend = (4.0 / 3.0) * near - (1.0 / 12.0) * far - 5.0 * p
    rate_e = bend - (slope(e_rows) * p_x + slope(e_lanes) * p_y)
    rate_p = 0.5 * (p_x * p_x + p_y * p_y) + e
    return e, p, time_step * rate_e, -time_step * rate_p


def surface(
    group, e, p, seam, outer, north, south, v, sea,
    new_e, new_p, height, wide_e, wide_p, volume, depth, e0, p0, e1, p1, sems,
):
    rows, width = e.shape
    low = group[0] == 0
    copies = []
    for t in range(v.shape[2] // LANES):
        part = slice(t * LANES, (t + 1) * LANES)
        into = volume.at[:, t + 1, SUBS : SUBS + rows, :]
        copies.append(pltpu.make_async_copy(v.at[:, :, part], into, sems.at[t]))
        copies[-1].start()
    left, right = side_blocks(low, seam[...], outer[...])
    tiles = width // LANES + 2
    inner = slice(SUBS, SUBS + rows)
    for old, source, base in ((e0, e, 0), (p0, p, LANES // 2)):
        half = SUBS if base else 0
        for t in range(tiles):
            part = slice(t * LANES, (t + 1) * LANES)
            old[t, :SUBS, :] = north[half : half + SUBS, part]
            old[t, SUBS + rows : 2 * SUBS + rows, :] = south[half : half + SUBS, part]
            if 0 < t < tiles - 1:
                old[t, inner, :] = source[:, (t - 1) * LANES : t * LANES]
        old[0, inner, :] = left[base : base + rows]
        old[tiles - 1, inner, :] = right[base : base + rows]
    blocks = rows // SUBS + 1

    def first(block, carry):
        row = block * SUBS + SUBS - 3
        for t in range(tiles):
            old_e, old_p, step_e, step_p = tile_rates(neighbourhood(e0, t, row), neighbourhood(p0, t, row))
            e1[t, pl.ds(row, SUBS), :] = old_e + step_e
            p1[t, pl.ds(row, SUBS), :] = old_p + step_p
        return carry

    lax.fori_loop(0, blocks, first, 0)

    def second(block, carry):
        row = block * SUBS + SUBS - 1
        for t in range(tiles):
            one_e, one_p, step_e, step_p = tile_rates(neighbourhood(e1, t, row), neighbourhood(p1, t, row))
            old_e = e0[t, pl.ds(row, SUBS), :]
            old_p = p0[t, pl.ds(row, SUBS), :]
            wide_e[t, pl.ds(row, SUBS), :] = 0.5 * ((old_e + one_e) + step_e)
            wide_p[t, pl.ds(row, SUBS), :] = 0.5 * ((old_p + one_p) + step_p)
        return carry

    lax.fori_loop(0, blocks, second, 0)
    for t in range(1, tiles - 1):
        part = slice((t - 1) * LANES, t * LANES)
        tile_e = wide_e[t, inner, :]
        new_e[:, part] = tile_e
        height[:rows, part] = tile_e
        new_p[:, part] = wide_p[t, inner, :]
        for row, wide in ((0, wide_e), (2, wide_p)):
            height[rows + row : rows + row + 1, part] = wide[t, SUBS - 1 : SUBS, :]
            height[rows + row + 1 : rows + row + 2, part] = wide[t, SUBS + rows : SUBS + rows + 1, :]
        height[rows + 4 :, part] = jnp.zeros((4, LANES), jnp.float32)
    left = jnp.concatenate([wide_e[0, inner, :], wide_p[0, inner, :]], 0).T[LANES - 1 :]
    right = jnp.concatenate([wide_e[tiles - 1, inner, :], wide_p[tiles - 1, inner, :]], 0).T[:1]
    height[rows + 4 : rows + 5, :LANES] = jnp.where(low, left, right)
    for t in range(v.shape[2] // LANES):
        depth[t + 1, inner, :] = sea[:, t * LANES : (t + 1) * LANES].astype(jnp.float32) * depth_unit
    for copy in copies:
        copy.wait()


def rim_pack(group, far_north, far_south, x_left, x_right, rims):
    low = group[0] == 0
    layers = far_north.shape[0]
    width = rims.shape[1]
    pairs = layers // 2
    rims[...] = jnp.zeros_like(rims)
    for row, side in ((0, far_north), (2, far_south)):
        for half in range(2):
            part = slice(half * width, (half + 1) * width)
            rims[row + half : row + half + 1, :] = jnp.where(low, side[layers - 1 : layers, part], side[0:1, part])
    for lane, side in ((0, x_left), (LANES, x_right)):
        top_pair = pltpu.roll(side[...], LANES // 2, 1)[pairs - 1 : pairs]
        rims[4:5, lane : lane + LANES] = jnp.where(low, top_pair, side[0:1, :])


def run_all(copies):
    for copy in copies:
        copy.start()
    for copy in copies:
        copy.wait()


def spread(volume, depth, x_left, x_right, east, around, depth_y, left_sides, right_sides):
    layers, tiles = volume.shape[0], volume.shape[1] - 2
    rows = east.shape[2]
    left = square(x_left[...], False).T
    right = square(x_right[...], False).T
    half = LANES // 2
    for k in range(layers + 1):
        base = (k % 2) * half
        left_sides[k] = pltpu.roll(left, LANES - 1 - k // 2, 1)[base : base + rows]
        right_sides[k] = pltpu.roll(right, (LANES - k // 2) % LANES, 1)[base : base + rows]

    def both(at, sides, t):
        cur = at(t)
        before = sides[0] if t == 0 else at(t - 1)
        after = sides[1] if t == tiles - 1 else at(t + 1)
        return cur, shift_lanes(before, cur, after, -1), shift_lanes(before, cur, after, 1)

    def layer(k, carry):
        def part(quarter, inner_carry):
            for step in range(4):
                row = pl.multiple_of((quarter * 4 + step) * SUBS, SUBS)
                here = pl.ds(pl.multiple_of(row + SUBS, SUBS), SUBS)
                spot = pl.ds(row, SUBS)
                sides = left_sides[k, spot, :], right_sides[k, spot, :]
                for t in range(tiles):
                    cur, west, far = both(lambda c: volume[k, c + 1, here, :], sides, t)
                    east[k, t, spot, :] = far - west
                    around[k, t, spot, :] = (far + west) - 4.0 * cur
            return inner_carry

        return lax.fori_loop(0, rows // SUBS // 4, part, carry)

    lax.fori_loop(0, layers, layer, 0)

    def floor(block, carry):
        row = pl.multiple_of(block * SUBS, SUBS)
        here = pl.ds(pl.multiple_of(row + SUBS, SUBS), SUBS)
        spot = pl.ds(row, SUBS)
        sides = left_sides[layers, spot, :], right_sides[layers, spot, :]
        for t in range(tiles):
            _, west, far = both(lambda c: depth[c + 1, here, :], sides, t)
            depth_y[t, spot, :] = far - west
        return carry

    lax.fori_loop(0, rows // SUBS, floor, 0)


def fill_rows(old_volume, old_depth, token, far_north, far_south, volume, depth, edges, depths, sems):
    del old_volume, old_depth, token
    layers, tiles, tall = volume.shape[0], volume.shape[1], volume.shape[2]
    tile = (tiles - 2) * LANES
    piece = tile // SUBS // LANES
    for end, source, row in ((0, far_north, SUBS - 1), (1, far_south, 0)):
        for t in range(tiles - 2):
            for k in range(layers):
                edges[end, k, t + 1, row : row + 1, :] = source[k : k + 1, t * LANES : (t + 1) * LANES]
            q, start = t // piece, tile + (t % piece) * LANES
            depths[end, t + 1, row : row + 1, :] = source[q : q + 1, start : start + LANES]
    copies = []
    for end, rows in ((0, slice(0, SUBS)), (1, slice(tall - SUBS, tall))):
        copies.append(pltpu.make_async_copy(edges.at[end], volume.at[:, :, rows, :], sems.at[2 * end]))
        copies.append(pltpu.make_async_copy(depths.at[end], depth.at[:, rows, :], sems.at[2 * end + 1]))
    run_all(copies)


def lanes_of(tile):
    return pl.ds(pl.multiple_of((tile - 1) * LANES, LANES), LANES)


def laplace(
    total_layers, group_ref, volume, depth, east, around, depth_y, far_layer, rims, wide_e, wide_p, height,
    out, part, coefficients, ghost, other_e,
):
    block = pl.program_id(0)
    group = group_ref[0]
    low = group == 0
    layers = volume.shape[0]
    rows, tile = far_layer.shape
    width = tile // 2
    tiles, halves = tile // LANES, width // LANES
    inner = slice(SUBS, SUBS + rows)

    @pl.when(block == 0)
    def _():
        far_left = pltpu.roll(square(rims[:, :LANES], False).T, LANES - 5, 1)[:rows]
        far_right = pltpu.roll(square(rims[:, LANES : 2 * LANES], False).T, LANES - 4, 1)[:rows]
        ghost[0, inner, :] = far_left
        ghost[tiles + 1, inner, :] = far_right
        for t in range(tiles):
            ghost[t + 1, inner, :] = far_layer[:, t * LANES : (t + 1) * LANES]
            half, spot = t // halves, slice((t % halves) * LANES, (t % halves + 1) * LANES)
            ghost[t + 1, SUBS - 1 : SUBS, :] = rims[half : half + 1, spot]
            ghost[t + 1, SUBS + rows : SUBS + rows + 1, :] = rims[2 + half : 3 + half, spot]
        for t in range(halves):
            spot = slice(t * LANES, (t + 1) * LANES)
            other_e[t + 1, inner, :] = height[:rows, spot]
            other_e[t + 1, SUBS - 1 : SUBS, :] = height[rows : rows + 1, spot]
            other_e[t + 1, SUBS + rows : SUBS + rows + 1, :] = height[rows + 1 : rows + 2, spot]
        edge = square(height[rows:, :LANES], False).T[:rows]
        at_right, at_left = pltpu.roll(edge, LANES - 4, 1), pltpu.roll(edge, LANES - 5, 1)
        other_e[0, inner, :] = jnp.where(low, wide_e[halves, inner, :], at_left)
        other_e[halves + 1, inner, :] = jnp.where(low, at_right, wide_e[1, inner, :])

    spacing = 1.0 / total_layers
    sigma = (group * layers).astype(jnp.float32) * spacing + 0.5 * spacing
    gain = (2 * group).astype(jnp.float32)
    row = pl.multiple_of(block * SUBS, SUBS)
    here = pl.multiple_of((block + 1) * SUBS, SUBS)
    spot = pl.ds(row, SUBS)

    def differences(ref, t):
        at = lambda column, step: ref[column, pl.ds(here + step, SUBS), :]
        cur, left, right = at(t, 0), at(t - 1, 0), at(t + 1, 0)
        return cur, at(t, 1) - at(t, -1), shift_lanes(left, cur, right, 1) - shift_lanes(left, cur, right, -1)

    def apply_tile(t, heights, local, mine):
        at = lambda ref, step: ref[t, pl.ds(here + step, SUBS), :]
        d, d_x, d_y = at(depth, 0), at(depth, 1) - at(depth, -1), depth_y[t - 1, spot, :]
        h, h_x, h_y = differences(heights, local)
        inverse = 1.0 / (d + h)
        scale = (0.25 / spacing) * inverse
        bx, by = scale * (d_x + h_x), scale * (d_y + h_y)
        ux, uy = scale * d_x - sigma * bx, scale * d_y - sigma * by
        bx, by = spacing * bx, spacing * by
        scaled = inverse * (1.0 / spacing)
        weight = 4.0 * (ux * ux + uy * uy) + scaled * scaled
        bend = 4.0 * (bx * bx + by * by)
        step = bend - 8.0 * (ux * bx + uy * by)
        bend = bend + bend

        def level(k):
            at = lambda step: volume[k, t, pl.ds(here + step, SUBS), :]
            up, down = at(-1), at(1)
            return at(0), down - up, east[k, t - 1, spot, :], (down + up) + around[k, t - 1, spot, :]

        far = differences(ghost, t)
        this = level(0)
        lower = [jnp.where(low, a, b) for a, b in zip(this, far)]
        rise_below = this[0] - lower[0]
        for k in range(layers):
            if k < layers - 1:
                upper = level(k + 1)
            else:
                upper = [jnp.where(low, a, -b) for a, b in zip(far, this)]
                if mine is not None:
                    upper = [a + gain * b for a, b in zip(upper, differences(mine, local))]
            rise = upper[0] - this[0]
            value = this[3] + ux * (upper[1] - lower[1]) + uy * (upper[2] - lower[2])
            value = value + weight * (rise - rise_below)
            out[k, :, lanes_of(t)] = value
            if k < layers - 1:
                ux, uy = ux - bx, uy - by
                weight, step = weight + step, step + bend
            elif mine is None:
                part[:, lanes_of(local)] = value
                coefficients[0, :, lanes_of(local)] = ux
                coefficients[1, :, lanes_of(local)] = uy
                coefficients[2, :, lanes_of(local)] = weight
            lower, this, rise_below = this, upper, rise

    def own_pair(pair, carry):
        for step in range(2):
            local = pair * 2 + step + 1
            apply_tile(group * halves + local, wide_e, local, wide_p)
        return carry

    def other_pair(pair, carry):
        for step in range(2):
            local = pair * 2 + step + 1
            apply_tile((1 - group) * halves + local, other_e, local, None)
        return carry

    lax.fori_loop(0, halves // 2, own_pair, 0)
    lax.fori_loop(0, halves // 2, other_pair, 0)


def top(group_ref, before, part, coefficients, height, wide_p, other_p, out, potential):
    del before
    low = group_ref[0] == 0
    rows, width = other_p.shape
    halves = width // LANES
    inner = slice(SUBS, SUBS + rows)
    edge = square(height[rows:, :LANES], False).T[LANES // 2 : LANES // 2 + rows]
    potential[0, inner, :] = pltpu.roll(edge, LANES - 5, 1)
    potential[halves + 1, inner, :] = wide_p[1, inner, :]
    for t in range(halves):
        spot = slice(t * LANES, (t + 1) * LANES)
        potential[t + 1, inner, :] = other_p[:, spot]
        potential[t + 1, SUBS - 1 : SUBS, :] = height[rows + 2 : rows + 3, spot]
        potential[t + 1, SUBS + rows : SUBS + rows + 1, :] = height[rows + 3 : rows + 4, spot]

    def body(block, carry):
        here = pl.multiple_of((block + 1) * SUBS, SUBS)
        to = pl.ds(pl.multiple_of(block * SUBS, SUBS), SUBS)
        for t in range(1, halves + 1):
            at = lambda column, step: potential[column, pl.ds(here + step, SUBS), :]
            cur, left, right = at(t, 0), at(t - 1, 0), at(t + 1, 0)
            east = shift_lanes(left, cur, right, 1) - shift_lanes(left, cur, right, -1)
            spot = slice((t - 1) * LANES, t * LANES)
            value = coefficients[0, to, spot] * (at(t, 1) - at(t, -1)) + coefficients[1, to, spot] * east
            value = value + coefficients[2, to, spot] * cur
            partial = part[to, spot]
            out[0, to, spot] = jnp.where(low, partial, partial + 2.0 * value)
        return carry

    lax.fori_loop(0, rows // SUBS, body, 0)


def ring(axis, step):
    count = lax.axis_size(axis)
    return [(i, (i + step) % count) for i in range(count)]


def shards(elevation, surface_potential, seabed, interior_potential):
    rows, width = elevation.shape
    layers, _, tile = interior_potential.shape
    assert 2 * rows == LANES and tile == 2 * width and layers == SUBS
    assert lax.axis_size("gz") == 2
    total_layers = layers * lax.axis_size("gz")
    f32 = jnp.float32
    shape = lambda *dims: jax.ShapeDtypeStruct(dims, f32)
    whole = lambda *dims: pl.BlockSpec(dims, lambda *_: (0,) * len(dims))
    group = lax.axis_index("gz").astype(jnp.int32).reshape((1,))
    scalar = pl.BlockSpec(memory_space=pltpu.SMEM)
    last_row, last_tile = rows // SUBS - 1, tile // LANES - 1

    def block(dims, *index):
        return pl.BlockSpec(dims, lambda *_: index)

    params = pltpu.CompilerParams(vmem_limit_bytes=24 * 1024 * 1024)
    vmem = pl.BlockSpec(memory_space=pltpu.VMEM)
    hbm = pl.BlockSpec(memory_space=pltpu.HBM)
    seam, outer, layer = pl.pallas_call(
        first_pack,
        out_shape=(shape(SUBS, LANES), shape(SUBS, LANES), shape(rows, tile)),
        in_specs=[scalar, hbm, hbm, hbm],
        out_specs=[vmem] * 3,
        scratch_shapes=[pltpu.VMEM((2, LANES, LANES), f32), pltpu.SemaphoreType.DMA((5,))],
        compiler_params=params,
        name="first_pack",
    )(group, *(pltpu.with_memory_space_constraint(x, pltpu.HBM) for x in (elevation, surface_potential, interior_potential)))

    flat = ("gy", "gz")
    count = lax.axis_size("gy")
    partner = [(2 * i + g, 2 * i + 1 - g) for i in range(count) for g in range(2)]
    across = [(2 * i + 1, (2 * i + 2) % (2 * count)) for i in range(count)]
    across = across + [(b, a) for a, b in across]
    seam = lax.ppermute(seam, flat, partner)
    far_layer = lax.ppermute(layer, flat, partner)
    outer = lax.ppermute(outer, flat, across)

    tiles = tile // LANES
    tall = rows + 2 * SUBS
    tables = (shape(layers, tiles + 2, tall, LANES), shape(tiles + 2, tall, LANES))
    anywhere = pl.BlockSpec(memory_space=pl.ANY)
    up, down, to_right, to_left = pl.pallas_call(
        lazy_pack,
        out_shape=(shape(SUBS, tile + tile // SUBS),) * 2 + (shape(SUBS, LANES),) * 2,
        grid=(1,),
        in_specs=[
            block((layers, SUBS, tile), 0, 0, 0),
            block((layers, SUBS, tile), 0, last_row, 0),
            block((layers, rows, LANES), 0, 0, 0),
            block((layers, rows, LANES), 0, 0, last_tile),
            block((SUBS, tile), 0, 0),
            block((SUBS, tile), last_row, 0),
            block((rows, LANES), 0, 0),
            block((rows, LANES), 0, last_tile),
        ],
        out_specs=[whole(SUBS, tile + tile // SUBS)] * 2 + [whole(SUBS, LANES)] * 2,
        compiler_params=params,
        name="lazy_pack",
    )(*(interior_potential,) * 4, *(seabed,) * 4)

    wide = width + 2 * LANES
    row_up, row_down = pl.pallas_call(
        row_pack,
        out_shape=(shape(2 * SUBS, wide),) * 2,
        grid=(1,),
        in_specs=[
            scalar,
            block((SUBS, width), 0, 0),
            block((SUBS, width), last_row, 0),
            block((SUBS, width), 0, 0),
            block((SUBS, width), last_row, 0),
            whole(SUBS, LANES),
            whole(SUBS, LANES),
        ],
        out_specs=[whole(2 * SUBS, wide)] * 2,
        compiler_params=params,
        name="row_pack",
    )(group, elevation, elevation, surface_potential, surface_potential, seam, outer)
    north = lax.ppermute(row_up, "gx", ring("gx", 1))
    south = lax.ppermute(row_down, "gx", ring("gx", -1))

    tiles = tile // LANES
    tall = rows + 2 * SUBS
    tables = (shape(layers, tiles + 2, tall, LANES), shape(tiles + 2, tall, LANES))
    anywhere = pl.BlockSpec(memory_space=pl.ANY)
    deep = rows + 3 * SUBS
    padded = (width // LANES + 2, deep, LANES)
    new_e, new_p, height, wide_e, wide_p, volume, depth = pl.pallas_call(
        surface,
        out_shape=(shape(rows, width),) * 2 + (shape(rows + SUBS, width),) + (shape(*padded),) * 2 + tables,
        in_specs=[scalar] + [vmem] * 6 + [hbm, vmem],
        out_specs=[vmem] * 7,
        scratch_shapes=[pltpu.VMEM(padded, f32)] * 4 + [pltpu.SemaphoreType.DMA((tiles,))],
        compiler_params=params,
        name="surface",
    )(
        group, elevation, surface_potential, seam, outer, north, south,
        pltpu.with_memory_space_constraint(interior_potential, pltpu.HBM), seabed,
    )
    far_height = lax.ppermute(height, flat, partner)
    far_north = lax.ppermute(up, "gx", ring("gx", 1))
    far_south = lax.ppermute(down, "gx", ring("gx", -1))
    x_left = lax.ppermute(to_right, "gy", ring("gy", 1))
    x_right = lax.ppermute(to_left, "gy", ring("gy", -1))
    east, around, depth_y = pl.pallas_call(
        spread,
        out_shape=(shape(layers, tiles, rows, LANES),) * 2 + (shape(tiles, rows, LANES),),
        in_specs=[vmem] * 4,
        out_specs=[vmem] * 3,
        scratch_shapes=[pltpu.VMEM((layers + 1, rows, LANES), f32)] * 2,
        compiler_params=params,
        name="spread",
    )(volume, depth, x_left, x_right)
    blocks = rows // SUBS
    rims = pl.pallas_call(
        rim_pack,
        out_shape=shape(SUBS, width),
        in_specs=[scalar] + [vmem] * 4,
        out_specs=vmem,
        compiler_params=params,
        name="rim_pack",
    )(group, far_north, far_south, x_left, x_right)
    far_rims = lax.ppermute(rims, flat, partner)
    other_p = lax.ppermute(new_p, flat, partner)

    volume, depth = pl.pallas_call(
        fill_rows,
        out_shape=tables,
        in_specs=[anywhere] * 3 + [vmem] * 2,
        out_specs=[anywhere] * 2,
        scratch_shapes=[
            pltpu.VMEM((2, layers, tiles + 2, SUBS, LANES), f32),
            pltpu.VMEM((2, tiles + 2, SUBS, LANES), f32),
            pltpu.SemaphoreType.DMA((4,)),
        ],
        input_output_aliases={0: 0, 1: 1},
        compiler_params=params,
        name="fill_rows",
    )(volume, depth, east, far_north, far_south)

    partial, part, coefficients = pl.pallas_call(
        functools.partial(laplace, total_layers),
        out_shape=(shape(layers, rows, tile), shape(rows, width), shape(3, rows, width)),
        grid=(blocks,),
        in_specs=[scalar] + [vmem] * 10,
        out_specs=[
            pl.BlockSpec((layers, SUBS, tile), lambda i: (0, i, 0)),
            pl.BlockSpec((SUBS, width), lambda i: (i, 0)),
            pl.BlockSpec((3, SUBS, width), lambda i: (0, i, 0)),
        ],
        scratch_shapes=[
            pltpu.VMEM((tiles + 2, tall, LANES), f32),
            pltpu.VMEM((width // LANES + 2, tall, LANES), f32),
        ],
        compiler_params=params,
        name="laplace",
    )(
        group, volume, depth, east, around, depth_y, far_layer, far_rims, wide_e, wide_p, far_height,
    )
    result = pl.pallas_call(
        top,
        out_shape=shape(layers, rows, tile),
        grid_spec=pltpu.PrefetchScalarGridSpec(
            num_scalar_prefetch=1,
            grid=(1,),
            in_specs=[hbm] + [vmem] * 5,
            out_specs=pl.BlockSpec((1, rows, width), lambda i, g: (layers - 1, 0, 1 - g[0])),
            scratch_shapes=[pltpu.VMEM((width // LANES + 2, tall, LANES), f32)],
        ),
        input_output_aliases={1: 0},
        compiler_params=params,
        name="top",
    )(group, partial, part, coefficients, far_height, wide_p, other_p)
    return new_e, new_p, result


def solution(mesh):
    return jax.shard_map(
        shards,
        mesh=mesh,
        in_specs=(P("gx", ("gy", "gz")), P("gx", ("gy", "gz")), P("gx", "gy"), P("gz", "gx", "gy")),
        out_specs=(P("gx", ("gy", "gz")), P("gx", ("gy", "gz")), P("gz", "gx", "gy")),
        check_vma=False,
    )
```

```python
import functools

import jax
import jax.numpy as jnp
from jax import lax
from jax.experimental import pallas as pl
from jax.experimental.pallas import tpu as pltpu
from jax.sharding import PartitionSpec as P

time_step = 0.05
depth_unit = 0.015625
LANES = 128
SUBS = 8


def shift_lanes(left, cur, right, step):
    lane = lax.broadcasted_iota(jnp.int32, cur.shape, 1)
    if step < 0:
        return pltpu.roll(jnp.where(lane >= LANES + step, left, cur), -step, 1)
    return pltpu.roll(jnp.where(lane < step, right, cur), LANES - step, 1)


def square(tile, at_end):
    rest = jnp.zeros((LANES - tile.shape[0], LANES), tile.dtype)
    return jnp.concatenate([rest, tile] if at_end else [tile, rest], 0)


def first_pack(group, e, p, v, seam, outer, layer, edges, sems):
    rows, width = e.shape
    low = group[0] == 0
    source = jnp.where(low, v.shape[0] - 1, 0)
    whole = pltpu.make_async_copy(v.at[source], layer, sems.at[4])
    copies = []
    for index, (field, start) in enumerate(((e, 0), (p, 0), (e, width - LANES), (p, width - LANES))):
        into = edges.at[index // 2, (index % 2) * rows : (index % 2 + 1) * rows, :]
        copies.append(pltpu.make_async_copy(field.at[:, start : start + LANES], into, sems.at[index]))
    for copy in copies:
        copy.start()
    whole.start()
    for copy in copies:
        copy.wait()
    left = edges[0].T[:SUBS]
    right = edges[1].T[LANES - SUBS :]
    seam[...] = jnp.where(low, right, left)
    outer[...] = jnp.where(low, left, right)
    whole.wait()


def by_parity(odd, fill, first, second):
    @pl.when(odd[0] == 0)
    def _():
        fill(first, second)

    @pl.when(odd[0] == 1)
    def _():
        fill(second, first)


def lazy_pack(
    odd_x, odd_y, v_top, v_bottom, v_left, v_right, s_top, s_bottom, s_left, s_right, row_a, row_b, column_a, column_b
):
    by_parity(odd_x, functools.partial(pack_rows, v_top, v_bottom, s_top, s_bottom), row_a, row_b)
    by_parity(odd_y, functools.partial(pack_columns, v_left, v_right, s_left, s_right), column_a, column_b)


def pack_rows(v_top, v_bottom, s_top, s_bottom, up, down):
    layers, _, width = v_top.shape
    piece = width // SUBS
    for k in range(layers):
        up[k : k + 1, :width] = v_bottom[k, SUBS - 1 : SUBS, :]
        down[k : k + 1, :width] = v_top[k, 0:1, :]
    for q in range(SUBS):
        part = slice(q * piece, (q + 1) * piece)
        up[q : q + 1, width:] = s_bottom[SUBS - 1 : SUBS, part].astype(jnp.float32) * depth_unit
        down[q : q + 1, width:] = s_top[0:1, part].astype(jnp.float32) * depth_unit


def pack_columns(v_left, v_right, s_left, s_right, to_right, to_left):
    layers = v_left.shape[0]
    to_right[...] = jnp.zeros_like(to_right)
    to_left[...] = jnp.zeros_like(to_left)
    for j in range(layers // 2):
        both = jnp.concatenate([v_right[2 * j], v_right[2 * j + 1]], 0).T
        to_right[j : j + 1, :] = both[LANES - 1 :]
        both = jnp.concatenate([v_left[2 * j], v_left[2 * j + 1]], 0).T
        to_left[j : j + 1, :] = both[:1]
    j = layers // 2
    both = jnp.concatenate([s_right[...], s_right[...]], 0).astype(jnp.float32) * depth_unit
    to_right[j : j + 1, :] = both.T[LANES - 1 :]
    both = jnp.concatenate([s_left[...], s_left[...]], 0).astype(jnp.float32) * depth_unit
    to_left[j : j + 1, :] = both.T[:1]


def side_blocks(low, seam, outer):
    left = square(jnp.where(low, outer, seam), True).T
    right = square(jnp.where(low, seam, outer), False).T
    return left, right


def row_pack(group, odd_x, e_top, e_bottom, p_top, p_bottom, seam, outer, row_a, row_b):
    left, right = side_blocks(group[0] == 0, seam[...], outer[...])
    by_parity(odd_x, functools.partial(pack_surface_rows, left, right, e_top, e_bottom, p_top, p_bottom), row_a, row_b)


def pack_surface_rows(left, right, e_top, e_bottom, p_top, p_bottom, up, down):
    rows = LANES // 2
    width = e_top.shape[1]
    for row, tops, bottoms in ((0, e_top, e_bottom), (SUBS, p_top, p_bottom)):
        base = 0 if row == 0 else rows
        up[row : row + SUBS, :LANES] = left[base + rows - SUBS : base + rows]
        up[row : row + SUBS, LANES : LANES + width] = bottoms[...]
        up[row : row + SUBS, LANES + width :] = right[base + rows - SUBS : base + rows]
        down[row : row + SUBS, :LANES] = left[base : base + SUBS]
        down[row : row + SUBS, LANES : LANES + width] = tops[...]
        down[row : row + SUBS, LANES + width :] = right[base : base + SUBS]


def neighbourhood(ref, lane_tile, row):
    last = ref.shape[0] - 1
    at = lambda column, step: ref[column, pl.ds(row + step, SUBS), :]
    cur = at(lane_tile, 0)
    left, right = at(max(lane_tile - 1, 0), 0), at(min(lane_tile + 1, last), 0)
    rows = [at(lane_tile, step) for step in (-2, -1, 1, 2)]
    lanes = [shift_lanes(left, cur, right, step) for step in (-2, -1, 1, 2)]
    return cur, rows, lanes


def slope(values):
    return (2.0 / 3.0) * (values[2] - values[1]) - (1.0 / 12.0) * (values[3] - values[0])


def tile_rates(e_near, p_near):
    e, e_rows, e_lanes = e_near
    p, p_rows, p_lanes = p_near
    p_x, p_y = slope(p_rows), slope(p_lanes)
    near = (p_rows[1] + p_rows[2]) + (p_lanes[1] + p_lanes[2])
    far = (p_rows[0] + p_rows[3]) + (p_lanes[0] + p_lanes[3])
    bend = (4.0 / 3.0) * near - (1.0 / 12.0) * far - 5.0 * p
    rate_e = bend - (slope(e_rows) * p_x + slope(e_lanes) * p_y)
    rate_p = 0.5 * (p_x * p_x + p_y * p_y) + e
    return e, p, time_step * rate_e, -time_step * rate_p


def surface(
    group, odd_x, e, p, seam, outer, row_a, row_b,
    new_e, new_p, height, wide_e, wide_p, e0, p0, e1, p1,
):
    rows, width = e.shape
    low = group[0] == 0
    left, right = side_blocks(low, seam[...], outer[...])
    tiles = width // LANES + 2
    inner = slice(SUBS, SUBS + rows)
    fields = ((e0, e, 0), (p0, p, LANES // 2))

    def ends(south, north):
        for old, _, base in fields:
            half = SUBS if base else 0
            for t in range(tiles):
                part = slice(t * LANES, (t + 1) * LANES)
                old[t, :SUBS, :] = north[half : half + SUBS, part]
                old[t, SUBS + rows : 2 * SUBS + rows, :] = south[half : half + SUBS, part]

    by_parity(odd_x, ends, row_a, row_b)
    for old, source, base in fields:
        for t in range(1, tiles - 1):
            old[t, inner, :] = source[:, (t - 1) * LANES : t * LANES]
        old[0, inner, :] = left[base : base + rows]
        old[tiles - 1, inner, :] = right[base : base + rows]
    blocks = rows // SUBS + 1

    def first(block, carry):
        row = block * SUBS + SUBS - 3
        for t in range(tiles):
            old_e, old_p, step_e, step_p = tile_rates(neighbourhood(e0, t, row), neighbourhood(p0, t, row))
            e1[t, pl.ds(row, SUBS), :] = old_e + step_e
            p1[t, pl.ds(row, SUBS), :] = old_p + step_p
        return carry

    lax.fori_loop(0, blocks, first, 0)

    def second(block, carry):
        row = block * SUBS + SUBS - 1
        for t in range(tiles):
            one_e, one_p, step_e, step_p = tile_rates(neighbourhood(e1, t, row), neighbourhood(p1, t, row))
            old_e = e0[t, pl.ds(row, SUBS), :]
            old_p = p0[t, pl.ds(row, SUBS), :]
            wide_e[t, pl.ds(row, SUBS), :] = 0.5 * ((old_e + one_e) + step_e)
            wide_p[t, pl.ds(row, SUBS), :] = 0.5 * ((old_p + one_p) + step_p)
        return carry

    lax.fori_loop(0, blocks, second, 0)
    for t in range(1, tiles - 1):
        part = slice((t - 1) * LANES, t * LANES)
        tile_e = wide_e[t, inner, :]
        new_e[:, part] = tile_e
        height[:rows, part] = tile_e
        new_p[:, part] = wide_p[t, inner, :]
        for row, wide in ((0, wide_e), (2, wide_p)):
            height[rows + row : rows + row + 1, part] = wide[t, SUBS - 1 : SUBS, :]
            height[rows + row + 1 : rows + row + 2, part] = wide[t, SUBS + rows : SUBS + rows + 1, :]
        height[rows + 4 :, part] = jnp.zeros((4, LANES), jnp.float32)
    left = jnp.concatenate([wide_e[0, inner, :], wide_p[0, inner, :]], 0).T[LANES - 1 :]
    right = jnp.concatenate([wide_e[tiles - 1, inner, :], wide_p[tiles - 1, inner, :]], 0).T[:1]
    height[rows + 4 : rows + 5, :LANES] = jnp.where(low, left, right)


def rim_pack(group, odd_x, odd_y, far_a, far_b, x_a, x_b, after, rims):
    del after
    low = group[0] == 0
    layers = far_a.shape[0]
    width = rims.shape[1]
    pairs = layers // 2
    rims[...] = jnp.zeros_like(rims)

    def rows(far_south, far_north):
        for row, side in ((0, far_north), (2, far_south)):
            for half in range(2):
                part = slice(half * width, (half + 1) * width)
                rims[row + half : row + half + 1, :] = jnp.where(low, side[layers - 1 : layers, part], side[0:1, part])

    by_parity(odd_x, rows, far_a, far_b)

    def columns(x_right, x_left):
        for lane, side in ((0, x_left), (LANES, x_right)):
            top_pair = pltpu.roll(side[...], LANES // 2, 1)[pairs - 1 : pairs]
            rims[4:5, lane : lane + LANES] = jnp.where(low, top_pair, side[0:1, :])

    by_parity(odd_y, columns, x_a, x_b)


def spread(
    odd_x, odd_y, v, sea, far_a, far_b, x_a, x_b, volume, depth, east, around, depth_y, left_sides, right_sides
):
    layers, rows, tile = v.shape
    tiles = tile // LANES
    even = odd_y[0] == 0
    left = square(jnp.where(even, x_b[...], x_a[...]), False).T
    right = square(jnp.where(even, x_a[...], x_b[...]), False).T
    half = LANES // 2
    for k in range(layers + 1):
        base = (k % 2) * half
        left_sides[k] = pltpu.roll(left, LANES - 1 - k // 2, 1)[base : base + rows]
        right_sides[k] = pltpu.roll(right, (LANES - k // 2) % LANES, 1)[base : base + rows]
    piece = tile // SUBS // LANES

    def ends(far_south, far_north):
        for side, row in ((far_north, SUBS - 1), (far_south, SUBS + rows)):
            for t in range(tiles):
                for k in range(layers):
                    volume[k, t, row : row + 1, :] = side[k : k + 1, t * LANES : (t + 1) * LANES]
                q, start = t // piece, tile + (t % piece) * LANES
                depth[t, row : row + 1, :] = side[q : q + 1, start : start + LANES]

    by_parity(odd_x, ends, far_a, far_b)

    def both(at, sides):
        tile_of = [at(t) for t in range(tiles)]
        padded = [sides[0]] + tile_of + [sides[1]]
        for t in range(tiles):
            before, cur, after = padded[t : t + 3]
            yield t, cur, shift_lanes(before, cur, after, -1), shift_lanes(before, cur, after, 1)

    def layer(k, carry):
        def part(quarter, inner_carry):
            for step in range(4):
                row = pl.multiple_of((quarter * 4 + step) * SUBS, SUBS)
                here = pl.ds(pl.multiple_of(row + SUBS, SUBS), SUBS)
                spot = pl.ds(row, SUBS)
                sides = left_sides[k, spot, :], right_sides[k, spot, :]
                for t, cur, west, far in both(lambda c: v[k, spot, c * LANES : (c + 1) * LANES], sides):
                    volume[k, t, here, :] = cur
                    east[k, t, spot, :] = far - west
                    around[k, t, spot, :] = (far + west) - 4.0 * cur
            return inner_carry

        return lax.fori_loop(0, rows // SUBS // 4, part, carry)

    lax.fori_loop(0, layers, layer, 0)

    def floor(pair, carry):
        for step in range(2):
            row = pl.multiple_of((pair * 2 + step) * SUBS, SUBS)
            here = pl.ds(pl.multiple_of(row + SUBS, SUBS), SUBS)
            spot = pl.ds(row, SUBS)
            sides = left_sides[layers, spot, :], right_sides[layers, spot, :]
            value = lambda c: sea[spot, c * LANES : (c + 1) * LANES].astype(jnp.float32) * depth_unit
            for t, cur, west, far in both(value, sides):
                depth[t, here, :] = cur
                depth_y[t, spot, :] = far - west
        return carry

    lax.fori_loop(0, rows // SUBS // 2, floor, 0)


def own_half(
    total_layers, group_ref, volume, depth, east, around, depth_y, far_layer, rims, wide_e, wide_p, out, ghost
):
    group = group_ref[0]

    @pl.when(pl.program_id(0) == 0)
    def _():
        fill_ghost(group == 0, group, far_layer, rims, ghost)

    apply_half(
        total_layers, group, group, volume, depth, east, around, depth_y, wide_e, wide_p, ghost, out, None, None
    )


def other_half(
    total_layers, group_ref, before, volume, depth, east, around, depth_y, far_layer, rims, wide_e, height,
    out, part, coefficients, ghost, other_e,
):
    del before
    group = group_ref[0]
    low = group == 0
    rows, width = other_e.shape[1] - 2 * SUBS, height.shape[1]
    halves = width // LANES
    inner = slice(SUBS, SUBS + rows)

    @pl.when(pl.program_id(0) == 0)
    def _():
        fill_ghost(group == 1, 1 - group, far_layer, rims, ghost)
        for t in range(halves):
            spot = slice(t * LANES, (t + 1) * LANES)
            other_e[t + 1, inner, :] = height[:rows, spot]
            other_e[t + 1, SUBS - 1 : SUBS, :] = height[rows : rows + 1, spot]
            other_e[t + 1, SUBS + rows : SUBS + rows + 1, :] = height[rows + 1 : rows + 2, spot]
        edge = square(height[rows:, :LANES], False).T[:rows]
        at_right, at_left = pltpu.roll(edge, LANES - 4, 1), pltpu.roll(edge, LANES - 5, 1)
        other_e[0, inner, :] = jnp.where(low, wide_e[halves, inner, :], at_left)
        other_e[halves + 1, inner, :] = jnp.where(low, at_right, wide_e[1, inner, :])

    apply_half(
        total_layers, group, 1 - group, volume, depth, east, around, depth_y, other_e, None, ghost, out, part,
        coefficients,
    )


def fill_ghost(first, half, far_layer, rims, ghost):
    rows, tile = far_layer.shape
    width = tile // 2
    halves = width // LANES
    inner = slice(SUBS, SUBS + rows)
    far_left = pltpu.roll(square(rims[:, :LANES], False).T, LANES - 5, 1)[:rows]
    far_right = pltpu.roll(square(rims[:, LANES : 2 * LANES], False).T, LANES - 4, 1)[:rows]
    ghost[0, inner, :] = jnp.where(first, far_left, far_layer[:, width - LANES : width])
    ghost[halves + 1, inner, :] = jnp.where(first, far_layer[:, width : width + LANES], far_right)
    for t in range(halves):
        spot = slice(t * LANES, (t + 1) * LANES)
        lanes = pl.ds(pl.multiple_of(half * width + t * LANES, LANES), LANES)
        ghost[t + 1, inner, :] = far_layer[:, lanes]
        ghost[t + 1, SUBS - 1 : SUBS, :] = jnp.where(first, rims[0:1, spot], rims[1:2, spot])
        ghost[t + 1, SUBS + rows : SUBS + rows + 1, :] = jnp.where(first, rims[2:3, spot], rims[3:4, spot])


def apply_half(
    total_layers, group, half, volume, depth, east, around, depth_y, heights, mine, ghost, out, part, coefficients
):
    block = pl.program_id(0)
    low = group == 0
    layers = volume.shape[0]
    halves = volume.shape[1] // 2
    spacing = 1.0 / total_layers
    sigma = (group * layers).astype(jnp.float32) * spacing + 0.5 * spacing
    gain = (2 * group).astype(jnp.float32)
    row = pl.multiple_of(block * SUBS, SUBS)
    here = pl.multiple_of((block + 1) * SUBS, SUBS)
    spot = pl.ds(row, SUBS)

    def differences(ref, t):
        at = lambda column, step: ref[column, pl.ds(here + step, SUBS), :]
        cur, left, right = at(t, 0), at(t - 1, 0), at(t + 1, 0)
        return cur, at(t, 1) - at(t, -1), shift_lanes(left, cur, right, 1) - shift_lanes(left, cur, right, -1)

    def apply_tile(t, heights, local, mine):
        at = lambda ref, step: ref[t, pl.ds(here + step, SUBS), :]
        local_lanes = pl.ds(pl.multiple_of((local - 1) * LANES, LANES), LANES)
        d, d_x, d_y = at(depth, 0), at(depth, 1) - at(depth, -1), depth_y[t, spot, :]
        h, h_x, h_y = differences(heights, local)
        inverse = 1.0 / (d + h)
        scale = (0.25 / spacing) * inverse
        bx, by = scale * (d_x + h_x), scale * (d_y + h_y)
        ux, uy = scale * d_x - sigma * bx, scale * d_y - sigma * by
        bx, by = spacing * bx, spacing * by
        scaled = inverse * (1.0 / spacing)
        weight = 4.0 * (ux * ux + uy * uy) + scaled * scaled
        bend = 4.0 * (bx * bx + by * by)
        step = bend - 8.0 * (ux * bx + uy * by)
        bend = bend + bend

        def level(k):
            at = lambda step: volume[k, t, pl.ds(here + step, SUBS), :]
            up, down = at(-1), at(1)
            return at(0), down - up, east[k, t, spot, :], (down + up) + around[k, t, spot, :]

        far = differences(ghost, local)
        this = level(0)
        lower = [jnp.where(low, a, b) for a, b in zip(this, far)]
        rise_below = this[0] - lower[0]
        for k in range(layers):
            if k < layers - 1:
                upper = level(k + 1)
            else:
                upper = [jnp.where(low, a, -b) for a, b in zip(far, this)]
                if mine is not None:
                    upper = [a + gain * b for a, b in zip(upper, differences(mine, local))]
            rise = upper[0] - this[0]
            value = this[3] + ux * (upper[1] - lower[1]) + uy * (upper[2] - lower[2])
            value = value + weight * (rise - rise_below)
            out[k, :, local_lanes] = value
            if k < layers - 1:
                ux, uy = ux - bx, uy - by
                weight, step = weight + step, step + bend
            elif mine is None:
                part[:, local_lanes] = value
                coefficients[0, :, local_lanes] = ux
                coefficients[1, :, local_lanes] = uy
                coefficients[2, :, local_lanes] = weight
            lower, this, rise_below = this, upper, rise

    def pair(index, carry):
        for step in range(2):
            local = index * 2 + step + 1
            apply_tile(half * halves + local - 1, heights, local, mine)
        return carry

    lax.fori_loop(0, halves // 2, pair, 0)


def top(group_ref, before, part, coefficients, height, wide_p, other_p, out, potential):
    del before
    low = group_ref[0] == 0
    rows, width = other_p.shape
    halves = width // LANES
    inner = slice(SUBS, SUBS + rows)
    edge = square(height[rows:, :LANES], False).T[LANES // 2 : LANES // 2 + rows]
    potential[0, inner, :] = pltpu.roll(edge, LANES - 5, 1)
    potential[halves + 1, inner, :] = wide_p[1, inner, :]
    for t in range(halves):
        spot = slice(t * LANES, (t + 1) * LANES)
        potential[t + 1, inner, :] = other_p[:, spot]
        potential[t + 1, SUBS - 1 : SUBS, :] = height[rows + 2 : rows + 3, spot]
        potential[t + 1, SUBS + rows : SUBS + rows + 1, :] = height[rows + 3 : rows + 4, spot]

    def body(block, carry):
        here = pl.multiple_of((block + 1) * SUBS, SUBS)
        to = pl.ds(pl.multiple_of(block * SUBS, SUBS), SUBS)
        for t in range(1, halves + 1):
            at = lambda column, step: potential[column, pl.ds(here + step, SUBS), :]
            cur, left, right = at(t, 0), at(t - 1, 0), at(t + 1, 0)
            east = shift_lanes(left, cur, right, 1) - shift_lanes(left, cur, right, -1)
            spot = slice((t - 1) * LANES, t * LANES)
            value = coefficients[0, to, spot] * (at(t, 1) - at(t, -1)) + coefficients[1, to, spot] * east
            value = value + coefficients[2, to, spot] * cur
            partial = part[to, spot]
            out[0, to, spot] = jnp.where(low, partial, partial + 2.0 * value)
        return carry

    lax.fori_loop(0, rows // SUBS, body, 0)


def couples(axis, shifted):
    count = lax.axis_size(axis)
    start = 1 if shifted else 0
    one_way = [((i + start) % count, (i + start + 1) % count) for i in range(0, count, 2)]
    return one_way + [(b, a) for a, b in one_way]


def shards(elevation, surface_potential, seabed, interior_potential):
    rows, width = elevation.shape
    layers, _, tile = interior_potential.shape
    assert 2 * rows == LANES and tile == 2 * width and layers == SUBS
    assert lax.axis_size("gz") == 2
    total_layers = layers * lax.axis_size("gz")
    f32 = jnp.float32
    shape = lambda *dims: jax.ShapeDtypeStruct(dims, f32)
    whole = lambda *dims: pl.BlockSpec(dims, lambda *_: (0,) * len(dims))
    group = lax.axis_index("gz").astype(jnp.int32).reshape((1,))
    odd_x = (lax.axis_index("gx") & 1).astype(jnp.int32).reshape((1,))
    odd_y = (lax.axis_index("gy") & 1).astype(jnp.int32).reshape((1,))
    assert lax.axis_size("gx") % 2 == 0 and lax.axis_size("gy") % 2 == 0
    scalar = pl.BlockSpec(memory_space=pltpu.SMEM)
    last_row, last_tile = rows // SUBS - 1, tile // LANES - 1

    def block(dims, *index):
        return pl.BlockSpec(dims, lambda *_: index)

    params = pltpu.CompilerParams(vmem_limit_bytes=24 * 1024 * 1024)
    vmem = pl.BlockSpec(memory_space=pltpu.VMEM)
    hbm = pl.BlockSpec(memory_space=pltpu.HBM)
    seam, outer, layer = pl.pallas_call(
        first_pack,
        out_shape=(shape(SUBS, LANES), shape(SUBS, LANES), shape(rows, tile)),
        in_specs=[scalar, hbm, hbm, hbm],
        out_specs=[vmem] * 3,
        scratch_shapes=[pltpu.VMEM((2, LANES, LANES), f32), pltpu.SemaphoreType.DMA((5,))],
        compiler_params=params,
        name="first_pack",
    )(group, *(pltpu.with_memory_space_constraint(x, pltpu.HBM) for x in (elevation, surface_potential, interior_potential)))

    flat = ("gy", "gz")
    count = lax.axis_size("gy")
    partner = [(2 * i + g, 2 * i + 1 - g) for i in range(count) for g in range(2)]
    across = [(2 * i + 1, (2 * i + 2) % (2 * count)) for i in range(count)]
    across = across + [(b, a) for a, b in across]
    seam = lax.ppermute(seam, flat, partner)
    far_layer = lax.ppermute(layer, flat, partner)
    outer = lax.ppermute(outer, flat, across)

    tiles = tile // LANES
    tall = rows + 2 * SUBS
    tables = (shape(layers, tiles + 2, tall, LANES), shape(tiles + 2, tall, LANES))
    anywhere = pl.BlockSpec(memory_space=pl.ANY)
    far_a, far_b, x_a, x_b = pl.pallas_call(
        lazy_pack,
        out_shape=(shape(SUBS, tile + tile // SUBS),) * 2 + (shape(SUBS, LANES),) * 2,
        grid=(1,),
        in_specs=[
            scalar,
            scalar,
            block((layers, SUBS, tile), 0, 0, 0),
            block((layers, SUBS, tile), 0, last_row, 0),
            block((layers, rows, LANES), 0, 0, 0),
            block((layers, rows, LANES), 0, 0, last_tile),
            block((SUBS, tile), 0, 0),
            block((SUBS, tile), last_row, 0),
            block((rows, LANES), 0, 0),
            block((rows, LANES), 0, last_tile),
        ],
        out_specs=[whole(SUBS, tile + tile // SUBS)] * 2 + [whole(SUBS, LANES)] * 2,
        compiler_params=params,
        name="lazy_pack",
    )(odd_x, odd_y, *(pltpu.with_memory_space_constraint(interior_potential, pltpu.HBM),) * 4, *(seabed,) * 4)

    wide = width + 2 * LANES
    row_a, row_b = pl.pallas_call(
        row_pack,
        out_shape=(shape(2 * SUBS, wide),) * 2,
        grid=(1,),
        in_specs=[
            scalar,
            scalar,
            block((SUBS, width), 0, 0),
            block((SUBS, width), last_row, 0),
            block((SUBS, width), 0, 0),
            block((SUBS, width), last_row, 0),
            whole(SUBS, LANES),
            whole(SUBS, LANES),
        ],
        out_specs=[whole(2 * SUBS, wide)] * 2,
        compiler_params=params,
        name="row_pack",
    )(group, odd_x, elevation, elevation, surface_potential, surface_potential, seam, outer)
    sides = {}
    for name, value, axis, shifted in (
        ("row_b", row_b, "gx", True), ("row_a", row_a, "gx", False), ("x_b", x_b, "gy", True),
        ("x_a", x_a, "gy", False), ("far_b", far_b, "gx", True), ("far_a", far_a, "gx", False),
    ):
        sides[name] = lax.ppermute(value, axis, couples(axis, shifted))

    tiles = tile // LANES
    tall = rows + 2 * SUBS
    anywhere = pl.BlockSpec(memory_space=pl.ANY)
    deep = rows + 3 * SUBS
    padded = (width // LANES + 2, deep, LANES)
    new_e, new_p, height, wide_e, wide_p = pl.pallas_call(
        surface,
        out_shape=(shape(rows, width),) * 2 + (shape(rows + SUBS, width),) + (shape(*padded),) * 2,
        in_specs=[scalar] * 2 + [vmem] * 6,
        out_specs=[vmem] * 5,
        scratch_shapes=[pltpu.VMEM(padded, f32)] * 4,
        compiler_params=params,
        name="surface",
    )(group, odd_x, elevation, surface_potential, seam, outer, sides["row_a"], sides["row_b"])
    far_sides = [sides[name] for name in ("far_a", "far_b", "x_a", "x_b")]
    rims = pl.pallas_call(
        rim_pack,
        out_shape=shape(SUBS, width),
        in_specs=[scalar] * 3 + [vmem] * 4 + [anywhere],
        out_specs=vmem,
        compiler_params=params,
        name="rim_pack",
    )(group, odd_x, odd_y, *far_sides, height)
    far_rims = lax.ppermute(rims, flat, partner)
    far_height = lax.ppermute(height, flat, partner)
    other_p = lax.ppermute(new_p, flat, partner)
    spread_shapes = (shape(layers, tiles, tall, LANES), shape(tiles, tall, LANES))
    spread_shapes = spread_shapes + (shape(layers, tiles, rows, LANES),) * 2 + (shape(tiles, rows, LANES),)
    volume, depth, east, around, depth_y = pl.pallas_call(
        spread,
        out_shape=spread_shapes,
        in_specs=[scalar] * 2 + [vmem] * 6,
        out_specs=[vmem] * 5,
        scratch_shapes=[pltpu.VMEM((layers + 1, rows, LANES), f32)] * 2,
        compiler_params=params,
        name="spread",
    )(odd_x, odd_y, interior_potential, seabed, *far_sides)
    blocks = rows // SUBS
    tables = (volume, depth, east, around, depth_y, far_layer, far_rims, wide_e)
    ghost = pltpu.VMEM((width // LANES + 2, tall, LANES), f32)
    partial = pl.pallas_call(
        functools.partial(own_half, total_layers),
        out_shape=shape(layers, rows, tile),
        grid_spec=pltpu.PrefetchScalarGridSpec(
            num_scalar_prefetch=1,
            grid=(blocks,),
            in_specs=[vmem] * 9,
            out_specs=pl.BlockSpec((layers, SUBS, width), lambda i, g: (0, i, g[0])),
            scratch_shapes=[ghost],
        ),
        compiler_params=params,
        name="own_half",
    )(group, *tables, wide_p)
    partial, part, coefficients = pl.pallas_call(
        functools.partial(other_half, total_layers),
        out_shape=(shape(layers, rows, tile), shape(rows, width), shape(3, rows, width)),
        grid_spec=pltpu.PrefetchScalarGridSpec(
            num_scalar_prefetch=1,
            grid=(blocks,),
            in_specs=[hbm] + [vmem] * 9,
            out_specs=[
                pl.BlockSpec((layers, SUBS, width), lambda i, g: (0, i, 1 - g[0])),
                pl.BlockSpec((SUBS, width), lambda i, g: (i, 0)),
                pl.BlockSpec((3, SUBS, width), lambda i, g: (0, i, 0)),
            ],
            scratch_shapes=[ghost] * 2,
        ),
        input_output_aliases={1: 0},
        compiler_params=params,
        name="other_half",
    )(group, partial, *tables, far_height)
    result = pl.pallas_call(
        top,
        out_shape=shape(layers, rows, tile),
        grid_spec=pltpu.PrefetchScalarGridSpec(
            num_scalar_prefetch=1,
            grid=(1,),
            in_specs=[hbm] + [vmem] * 5,
            out_specs=pl.BlockSpec((1, rows, width), lambda i, g: (layers - 1, 0, 1 - g[0])),
            scratch_shapes=[pltpu.VMEM((width // LANES + 2, tall, LANES), f32)],
        ),
        input_output_aliases={1: 0},
        compiler_params=params,
        name="top",
    )(group, partial, part, coefficients, far_height, wide_p, other_p)
    return new_e, new_p, result


def solution(mesh):
    return jax.shard_map(
        shards,
        mesh=mesh,
        in_specs=(P("gx", ("gy", "gz")), P("gx", ("gy", "gz")), P("gx", "gy"), P("gz", "gx", "gy")),
        out_specs=(P("gx", ("gy", "gz")), P("gx", ("gy", "gz")), P("gz", "gx", "gy")),
        check_vma=False,
    )
```

```python
import functools

import jax
import jax.numpy as jnp
from jax import lax
from jax.experimental import pallas as pl
from jax.experimental.pallas import tpu as pltpu
from jax.sharding import PartitionSpec as P

time_step = 0.05
depth_unit = 0.015625
LANES = 128
SUBS = 8


def shift_lanes(left, cur, right, step):
    lane = lax.broadcasted_iota(jnp.int32, cur.shape, 1)
    if step < 0:
        return pltpu.roll(jnp.where(lane >= LANES + step, left, cur), -step, 1)
    return pltpu.roll(jnp.where(lane < step, right, cur), LANES - step, 1)


def square(tile, at_end):
    rest = jnp.zeros((LANES - tile.shape[0], LANES), tile.dtype)
    return jnp.concatenate([rest, tile] if at_end else [tile, rest], 0)


def first_pack(group, e, p, v, seam, outer, layer, edges, sems):
    rows, width = e.shape
    low = group[0] == 0
    source = jnp.where(low, v.shape[0] - 1, 0)
    whole = pltpu.make_async_copy(v.at[source], layer, sems.at[4])
    copies = []
    for index, (field, start) in enumerate(((e, 0), (p, 0), (e, width - LANES), (p, width - LANES))):
        into = edges.at[index // 2, (index % 2) * rows : (index % 2 + 1) * rows, :]
        copies.append(pltpu.make_async_copy(field.at[:, start : start + LANES], into, sems.at[index]))
    for copy in copies:
        copy.start()
    whole.start()
    for copy in copies:
        copy.wait()
    left = edges[0].T[:SUBS]
    right = edges[1].T[LANES - SUBS :]
    seam[...] = jnp.where(low, right, left)
    outer[...] = jnp.where(low, left, right)
    whole.wait()


def by_parity(odd, fill, first, second):
    @pl.when(odd[0] == 0)
    def _():
        fill(first, second)

    @pl.when(odd[0] == 1)
    def _():
        fill(second, first)


def lazy_pack(
    odd_x, odd_y, v_top, v_bottom, v_left, v_right, s_top, s_bottom, s_left, s_right, row_a, row_b, column_a, column_b
):
    by_parity(odd_x, functools.partial(pack_rows, v_top, v_bottom, s_top, s_bottom), row_a, row_b)
    by_parity(odd_y, functools.partial(pack_columns, v_left, v_right, s_left, s_right), column_a, column_b)


def pack_rows(v_top, v_bottom, s_top, s_bottom, up, down):
    layers, _, width = v_top.shape
    piece = width // SUBS
    for k in range(layers):
        up[k : k + 1, :width] = v_bottom[k, SUBS - 1 : SUBS, :]
        down[k : k + 1, :width] = v_top[k, 0:1, :]
    for q in range(SUBS):
        part = slice(q * piece, (q + 1) * piece)
        up[q : q + 1, width:] = s_bottom[SUBS - 1 : SUBS, part].astype(jnp.float32) * depth_unit
        down[q : q + 1, width:] = s_top[0:1, part].astype(jnp.float32) * depth_unit


def pack_columns(v_left, v_right, s_left, s_right, to_right, to_left):
    layers = v_left.shape[0]
    to_right[...] = jnp.zeros_like(to_right)
    to_left[...] = jnp.zeros_like(to_left)
    for j in range(layers // 2):
        both = jnp.concatenate([v_right[2 * j], v_right[2 * j + 1]], 0).T
        to_right[j : j + 1, :] = both[LANES - 1 :]
        both = jnp.concatenate([v_left[2 * j], v_left[2 * j + 1]], 0).T
        to_left[j : j + 1, :] = both[:1]
    j = layers // 2
    both = jnp.concatenate([s_right[...], s_right[...]], 0).astype(jnp.float32) * depth_unit
    to_right[j : j + 1, :] = both.T[LANES - 1 :]
    both = jnp.concatenate([s_left[...], s_left[...]], 0).astype(jnp.float32) * depth_unit
    to_left[j : j + 1, :] = both.T[:1]


def side_blocks(low, seam, outer):
    left = square(jnp.where(low, outer, seam), True).T
    right = square(jnp.where(low, seam, outer), False).T
    return left, right


def row_pack(group, odd_x, e_top, e_bottom, p_top, p_bottom, seam, outer, row_a, row_b):
    left, right = side_blocks(group[0] == 0, seam[...], outer[...])
    by_parity(odd_x, functools.partial(pack_surface_rows, left, right, e_top, e_bottom, p_top, p_bottom), row_a, row_b)


def pack_surface_rows(left, right, e_top, e_bottom, p_top, p_bottom, up, down):
    rows = LANES // 2
    width = e_top.shape[1]
    for row, tops, bottoms in ((0, e_top, e_bottom), (SUBS, p_top, p_bottom)):
        base = 0 if row == 0 else rows
        up[row : row + SUBS, :LANES] = left[base + rows - SUBS : base + rows]
        up[row : row + SUBS, LANES : LANES + width] = bottoms[...]
        up[row : row + SUBS, LANES + width :] = right[base + rows - SUBS : base + rows]
        down[row : row + SUBS, :LANES] = left[base : base + SUBS]
        down[row : row + SUBS, LANES : LANES + width] = tops[...]
        down[row : row + SUBS, LANES + width :] = right[base : base + SUBS]


def neighbourhood(ref, lane_tile, row):
    last = ref.shape[0] - 1
    at = lambda column, step: ref[column, pl.ds(row + step, SUBS), :]
    cur = at(lane_tile, 0)
    left, right = at(max(lane_tile - 1, 0), 0), at(min(lane_tile + 1, last), 0)
    rows = [at(lane_tile, step) for step in (-2, -1, 1, 2)]
    lanes = [shift_lanes(left, cur, right, step) for step in (-2, -1, 1, 2)]
    return cur, rows, lanes


def slope(values):
    return (2.0 / 3.0) * (values[2] - values[1]) - (1.0 / 12.0) * (values[3] - values[0])


def tile_rates(e_near, p_near):
    e, e_rows, e_lanes = e_near
    p, p_rows, p_lanes = p_near
    p_x, p_y = slope(p_rows), slope(p_lanes)
    near = (p_rows[1] + p_rows[2]) + (p_lanes[1] + p_lanes[2])
    far = (p_rows[0] + p_rows[3]) + (p_lanes[0] + p_lanes[3])
    bend = (4.0 / 3.0) * near - (1.0 / 12.0) * far - 5.0 * p
    rate_e = bend - (slope(e_rows) * p_x + slope(e_lanes) * p_y)
    rate_p = 0.5 * (p_x * p_x + p_y * p_y) + e
    return e, p, time_step * rate_e, -time_step * rate_p


def surface(
    group, odd_x, e, p, seam, outer, row_a, row_b, v, sea,
    new_e, new_p, height, wide_e, wide_p, volume, depth, e0, p0, e1, p1, sems,
):
    rows, width = e.shape
    low = group[0] == 0
    copies = []
    for t in range(v.shape[2] // LANES):
        part = slice(t * LANES, (t + 1) * LANES)
        into = volume.at[:, t + 1, SUBS : SUBS + rows, :]
        copies.append(pltpu.make_async_copy(v.at[:, :, part], into, sems.at[t]))
        copies[-1].start()
    left, right = side_blocks(low, seam[...], outer[...])
    tiles = width // LANES + 2
    inner = slice(SUBS, SUBS + rows)
    fields = ((e0, e, 0), (p0, p, LANES // 2))

    def ends(south, north):
        for old, _, base in fields:
            half = SUBS if base else 0
            for t in range(tiles):
                part = slice(t * LANES, (t + 1) * LANES)
                old[t, :SUBS, :] = north[half : half + SUBS, part]
                old[t, SUBS + rows : 2 * SUBS + rows, :] = south[half : half + SUBS, part]

    by_parity(odd_x, ends, row_a, row_b)
    for old, source, base in fields:
        for t in range(1, tiles - 1):
            old[t, inner, :] = source[:, (t - 1) * LANES : t * LANES]
        old[0, inner, :] = left[base : base + rows]
        old[tiles - 1, inner, :] = right[base : base + rows]
    blocks = rows // SUBS + 1

    def first(block, carry):
        row = block * SUBS + SUBS - 3
        for t in range(tiles):
            old_e, old_p, step_e, step_p = tile_rates(neighbourhood(e0, t, row), neighbourhood(p0, t, row))
            e1[t, pl.ds(row, SUBS), :] = old_e + step_e
            p1[t, pl.ds(row, SUBS), :] = old_p + step_p
        return carry

    lax.fori_loop(0, blocks, first, 0, unroll=True)

    def second(block, carry):
        row = block * SUBS + SUBS - 1
        for t in range(tiles):
            one_e, one_p, step_e, step_p = tile_rates(neighbourhood(e1, t, row), neighbourhood(p1, t, row))
            old_e = e0[t, pl.ds(row, SUBS), :]
            old_p = p0[t, pl.ds(row, SUBS), :]
            wide_e[t, pl.ds(row, SUBS), :] = 0.5 * ((old_e + one_e) + step_e)
            wide_p[t, pl.ds(row, SUBS), :] = 0.5 * ((old_p + one_p) + step_p)
        return carry

    lax.fori_loop(0, blocks, second, 0, unroll=True)
    for t in range(1, tiles - 1):
        part = slice((t - 1) * LANES, t * LANES)
        tile_e = wide_e[t, inner, :]
        new_e[:, part] = tile_e
        height[:rows, part] = tile_e
        new_p[:, part] = wide_p[t, inner, :]
        for row, wide in ((0, wide_e), (2, wide_p)):
            height[rows + row : rows + row + 1, part] = wide[t, SUBS - 1 : SUBS, :]
            height[rows + row + 1 : rows + row + 2, part] = wide[t, SUBS + rows : SUBS + rows + 1, :]
        height[rows + 4 :, part] = jnp.zeros((4, LANES), jnp.float32)
    left = jnp.concatenate([wide_e[0, inner, :], wide_p[0, inner, :]], 0).T[LANES - 1 :]
    right = jnp.concatenate([wide_e[tiles - 1, inner, :], wide_p[tiles - 1, inner, :]], 0).T[:1]
    height[rows + 4 : rows + 5, :LANES] = jnp.where(low, left, right)
    for t in range(v.shape[2] // LANES):
        depth[t + 1, inner, :] = sea[:, t * LANES : (t + 1) * LANES].astype(jnp.float32) * depth_unit
    for copy in copies:
        copy.wait()


def rim_pack(group, odd_x, odd_y, far_a, far_b, x_a, x_b, after, rims):
    del after
    low = group[0] == 0
    layers = far_a.shape[0]
    width = rims.shape[1]
    pairs = layers // 2
    rims[...] = jnp.zeros_like(rims)

    def rows(far_south, far_north):
        for row, side in ((0, far_north), (2, far_south)):
            for half in range(2):
                part = slice(half * width, (half + 1) * width)
                rims[row + half : row + half + 1, :] = jnp.where(low, side[layers - 1 : layers, part], side[0:1, part])

    by_parity(odd_x, rows, far_a, far_b)

    def columns(x_right, x_left):
        for lane, side in ((0, x_left), (LANES, x_right)):
            top_pair = pltpu.roll(side[...], LANES // 2, 1)[pairs - 1 : pairs]
            rims[4:5, lane : lane + LANES] = jnp.where(low, top_pair, side[0:1, :])

    by_parity(odd_y, columns, x_a, x_b)


def fill(
    odd_x, odd_y, old_volume, old_depth, far_a, far_b, x_a, x_b, volume, depth, sides, depths, edges, ends, sems
):
    del old_volume, old_depth
    layers, tiles, tall = volume.shape[0], volume.shape[1], volume.shape[2]
    rows, tile = tall - 2 * SUBS, (tiles - 2) * LANES
    inner = slice(SUBS, SUBS + rows)
    even = odd_y[0] == 0
    left = square(jnp.where(even, x_b[...], x_a[...]), False).T
    right = square(jnp.where(even, x_a[...], x_b[...]), False).T
    half, pairs = LANES // 2, layers // 2
    for k in range(layers):
        base = (k % 2) * half
        sides[0, k] = pltpu.roll(left, LANES - 1 - k // 2, 1)[base : base + rows]
        sides[1, k] = pltpu.roll(right, (LANES - k // 2) % LANES, 1)[base : base + rows]
    depths[0] = pltpu.roll(left, LANES - 1 - pairs, 1)[:rows]
    depths[1] = pltpu.roll(right, LANES - pairs, 1)[:rows]
    piece = tile // SUBS // LANES

    def fill_ends(far_south, far_north):
        for end, source, row in ((0, far_north, SUBS - 1), (1, far_south, 0)):
            for t in range(tiles - 2):
                for k in range(layers):
                    edges[end, k, t, row : row + 1, :] = source[k : k + 1, t * LANES : (t + 1) * LANES]
                q, start = t // piece, tile + (t % piece) * LANES
                ends[end, t, row : row + 1, :] = source[q : q + 1, start : start + LANES]

    by_parity(odd_x, fill_ends, far_a, far_b)
    copies = []
    for index, (t, at) in enumerate(((0, slice(0, SUBS)), (tiles - 1, slice(tall - SUBS, tall)))):
        for source, target in (
            (sides.at[index], volume.at[:, t, inner, :]),
            (depths.at[index], depth.at[t, inner, :]),
            (edges.at[index], volume.at[:, 1 : tiles - 1, at, :]),
            (ends.at[index], depth.at[1 : tiles - 1, at, :]),
        ):
            copies.append(pltpu.make_async_copy(source, target, sems.at[len(copies)]))
    for copy in copies:
        copy.start()
    for copy in copies:
        copy.wait()


def apply_tile(total_layers, group, block, volume, depth, t, heights, local, ghost, spot, mine, write, rest=None):
    low = group == 0
    layers = volume.shape[0]
    spacing = 1.0 / total_layers
    sigma = (group * layers).astype(jnp.float32) * spacing + 0.5 * spacing
    gain = (2 * group).astype(jnp.float32)
    here = pl.multiple_of((block + 1) * SUBS, SUBS)

    def near(ref, t):
        at = lambda column, step: ref[column, pl.ds(here + step, SUBS), :]
        cur = at(t, 0)
        left, right = at(t - 1, 0), at(t + 1, 0)
        return cur, at(t, -1), at(t, 1), shift_lanes(left, cur, right, -1), shift_lanes(left, cur, right, 1)

    def differences(ref, t):
        p, up, down, left, right = near(ref, t)
        return p, down - up, right - left

    d, d_x, d_y = differences(depth, t)
    h, h_x, h_y = differences(heights, local)
    inverse = 1.0 / (d + h)
    scale = (0.25 / spacing) * inverse
    bx, by = scale * (d_x + h_x), scale * (d_y + h_y)
    ux, uy = scale * d_x - sigma * bx, scale * d_y - sigma * by
    bx, by = spacing * bx, spacing * by
    scaled = inverse * (1.0 / spacing)
    weight = 4.0 * (ux * ux + uy * uy) + scaled * scaled
    bend = 4.0 * (bx * bx + by * by)
    step = bend - 8.0 * (ux * bx + uy * by)
    bend = bend + bend

    def level(k):
        p, up, down, left, right = near(volume.at[k], t)
        return p, down - up, right - left, ((down + up) + (right + left)) - 4.0 * p

    far = differences(ghost, spot)
    this = level(0)
    lower = [jnp.where(low, a, b) for a, b in zip(this, far)]
    rise_below = this[0] - lower[0]
    for k in range(layers):
        if k < layers - 1:
            upper = level(k + 1)
        else:
            upper = [jnp.where(low, a, -b) for a, b in zip(far, this)]
            if mine is not None:
                upper = [a + gain * b for a, b in zip(upper, differences(mine, local))]
        rise = upper[0] - this[0]
        value = this[3] + ux * (upper[1] - lower[1]) + uy * (upper[2] - lower[2])
        value = value + weight * (rise - rise_below)
        write(k, value)
        if k < layers - 1:
            ux, uy = ux - bx, uy - by
            weight, step = weight + step, step + bend
        elif rest is not None:
            rest(value, ux, uy, weight)
        lower, this, rise_below = this, upper, rise


def own_half(total_layers, group_ref, volume, depth, far_layer, rims, wide_e, wide_p, out, ghost):
    block = pl.program_id(0)
    group = group_ref[0]
    halves = volume.shape[1] // 2 - 1

    @pl.when(block == 0)
    def _():
        fill_ghost(group == 0, group, far_layer, rims, ghost)

    for local in range(1, halves + 1):

        def write(k, value):
            out[k, :, (local - 1) * LANES : local * LANES] = value

        apply_tile(
            total_layers, group, block, volume, depth, group * halves + local, wide_e, local, ghost, local, wide_p,
            write,
        )


def other_half(
    total_layers, group_ref, before, volume, depth, far_layer, rims, wide_e, height,
    out, part, coefficients, ghost, other_e,
):
    del before
    block = pl.program_id(0)
    group = group_ref[0]
    low = group == 0
    rows, width = other_e.shape[1] - 2 * SUBS, height.shape[1]
    halves = width // LANES
    inner = slice(SUBS, SUBS + rows)

    @pl.when(block == 0)
    def _():
        fill_ghost(group == 1, 1 - group, far_layer, rims, ghost)
        for t in range(halves):
            spot = slice(t * LANES, (t + 1) * LANES)
            other_e[t + 1, inner, :] = height[:rows, spot]
            other_e[t + 1, SUBS - 1 : SUBS, :] = height[rows : rows + 1, spot]
            other_e[t + 1, SUBS + rows : SUBS + rows + 1, :] = height[rows + 1 : rows + 2, spot]
        edge = square(height[rows:, :LANES], False).T[:rows]
        at_right, at_left = pltpu.roll(edge, LANES - 4, 1), pltpu.roll(edge, LANES - 5, 1)
        other_e[0, inner, :] = jnp.where(low, wide_e[halves, inner, :], at_left)
        other_e[halves + 1, inner, :] = jnp.where(low, at_right, wide_e[1, inner, :])

    for local in range(1, halves + 1):
        spot = slice((local - 1) * LANES, local * LANES)

        def write(k, value):
            out[k, :, spot] = value

        def rest(value, ux, uy, weight):
            part[:, spot] = value
            coefficients[0, :, spot] = ux
            coefficients[1, :, spot] = uy
            coefficients[2, :, spot] = weight

        apply_tile(
            total_layers, group, block, volume, depth, (1 - group) * halves + local, other_e, local, ghost, local,
            None, write, rest,
        )


def fill_ghost(first, half, far_layer, rims, ghost):
    rows, tile = far_layer.shape
    width = tile // 2
    halves = width // LANES
    inner = slice(SUBS, SUBS + rows)
    far_left = pltpu.roll(square(rims[:, :LANES], False).T, LANES - 5, 1)[:rows]
    far_right = pltpu.roll(square(rims[:, LANES : 2 * LANES], False).T, LANES - 4, 1)[:rows]
    ghost[0, inner, :] = jnp.where(first, far_left, far_layer[:, width - LANES : width])
    ghost[halves + 1, inner, :] = jnp.where(first, far_layer[:, width : width + LANES], far_right)
    for t in range(halves):
        spot = slice(t * LANES, (t + 1) * LANES)
        lanes = pl.ds(pl.multiple_of(half * width + t * LANES, LANES), LANES)
        ghost[t + 1, inner, :] = far_layer[:, lanes]
        ghost[t + 1, SUBS - 1 : SUBS, :] = jnp.where(first, rims[0:1, spot], rims[1:2, spot])
        ghost[t + 1, SUBS + rows : SUBS + rows + 1, :] = jnp.where(first, rims[2:3, spot], rims[3:4, spot])


def top(group_ref, before, part, coefficients, height, wide_p, other_p, out, potential):
    del before
    low = group_ref[0] == 0
    rows, width = other_p.shape
    halves = width // LANES
    inner = slice(SUBS, SUBS + rows)
    edge = square(height[rows:, :LANES], False).T[LANES // 2 : LANES // 2 + rows]
    potential[0, inner, :] = pltpu.roll(edge, LANES - 5, 1)
    potential[halves + 1, inner, :] = wide_p[1, inner, :]
    for t in range(halves):
        spot = slice(t * LANES, (t + 1) * LANES)
        potential[t + 1, inner, :] = other_p[:, spot]
        potential[t + 1, SUBS - 1 : SUBS, :] = height[rows + 2 : rows + 3, spot]
        potential[t + 1, SUBS + rows : SUBS + rows + 1, :] = height[rows + 3 : rows + 4, spot]

    def body(block, carry):
        here = pl.multiple_of((block + 1) * SUBS, SUBS)
        to = pl.ds(pl.multiple_of(block * SUBS, SUBS), SUBS)
        for t in range(1, halves + 1):
            at = lambda column, step: potential[column, pl.ds(here + step, SUBS), :]
            cur, left, right = at(t, 0), at(t - 1, 0), at(t + 1, 0)
            east = shift_lanes(left, cur, right, 1) - shift_lanes(left, cur, right, -1)
            spot = slice((t - 1) * LANES, t * LANES)
            value = coefficients[0, to, spot] * (at(t, 1) - at(t, -1)) + coefficients[1, to, spot] * east
            value = value + coefficients[2, to, spot] * cur
            partial = part[to, spot]
            out[0, to, spot] = jnp.where(low, partial, partial + 2.0 * value)
        return carry

    lax.fori_loop(0, rows // SUBS, body, 0)


def couples(axis, shifted):
    count = lax.axis_size(axis)
    start = 1 if shifted else 0
    one_way = [((i + start) % count, (i + start + 1) % count) for i in range(0, count, 2)]
    return one_way + [(b, a) for a, b in one_way]


def shards(elevation, surface_potential, seabed, interior_potential):
    rows, width = elevation.shape
    layers, _, tile = interior_potential.shape
    assert 2 * rows == LANES and tile == 2 * width and layers == SUBS
    assert lax.axis_size("gz") == 2
    total_layers = layers * lax.axis_size("gz")
    f32 = jnp.float32
    shape = lambda *dims: jax.ShapeDtypeStruct(dims, f32)
    whole = lambda *dims: pl.BlockSpec(dims, lambda *_: (0,) * len(dims))
    group = lax.axis_index("gz").astype(jnp.int32).reshape((1,))
    odd_x = (lax.axis_index("gx") & 1).astype(jnp.int32).reshape((1,))
    odd_y = (lax.axis_index("gy") & 1).astype(jnp.int32).reshape((1,))
    assert lax.axis_size("gx") % 2 == 0 and lax.axis_size("gy") % 2 == 0
    scalar = pl.BlockSpec(memory_space=pltpu.SMEM)
    last_row, last_tile = rows // SUBS - 1, tile // LANES - 1

    def block(dims, *index):
        return pl.BlockSpec(dims, lambda *_: index)

    params = pltpu.CompilerParams(vmem_limit_bytes=24 * 1024 * 1024)
    vmem = pl.BlockSpec(memory_space=pltpu.VMEM)
    hbm = pl.BlockSpec(memory_space=pltpu.HBM)
    seam, outer, layer = pl.pallas_call(
        first_pack,
        out_shape=(shape(SUBS, LANES), shape(SUBS, LANES), shape(rows, tile)),
        in_specs=[scalar, hbm, hbm, hbm],
        out_specs=[vmem] * 3,
        scratch_shapes=[pltpu.VMEM((2, LANES, LANES), f32), pltpu.SemaphoreType.DMA((5,))],
        compiler_params=params,
        name="first_pack",
    )(group, *(pltpu.with_memory_space_constraint(x, pltpu.HBM) for x in (elevation, surface_potential, interior_potential)))

    flat = ("gy", "gz")
    count = lax.axis_size("gy")
    partner = [(2 * i + g, 2 * i + 1 - g) for i in range(count) for g in range(2)]
    across = [(2 * i + 1, (2 * i + 2) % (2 * count)) for i in range(count)]
    across = across + [(b, a) for a, b in across]
    seam = lax.ppermute(seam, flat, partner)
    far_layer = lax.ppermute(layer, flat, partner)
    outer = lax.ppermute(outer, flat, across)

    tiles = tile // LANES
    tall = rows + 2 * SUBS
    tables = (shape(layers, tiles + 2, tall, LANES), shape(tiles + 2, tall, LANES))
    anywhere = pl.BlockSpec(memory_space=pl.ANY)
    far_a, far_b, x_a, x_b = pl.pallas_call(
        lazy_pack,
        out_shape=(shape(SUBS, tile + tile // SUBS),) * 2 + (shape(SUBS, LANES),) * 2,
        grid=(1,),
        in_specs=[
            scalar,
            scalar,
            block((layers, SUBS, tile), 0, 0, 0),
            block((layers, SUBS, tile), 0, last_row, 0),
            block((layers, rows, LANES), 0, 0, 0),
            block((layers, rows, LANES), 0, 0, last_tile),
            block((SUBS, tile), 0, 0),
            block((SUBS, tile), last_row, 0),
            block((rows, LANES), 0, 0),
            block((rows, LANES), 0, last_tile),
        ],
        out_specs=[whole(SUBS, tile + tile // SUBS)] * 2 + [whole(SUBS, LANES)] * 2,
        compiler_params=params,
        name="lazy_pack",
    )(odd_x, odd_y, *(pltpu.with_memory_space_constraint(interior_potential, pltpu.HBM),) * 4, *(seabed,) * 4)

    wide = width + 2 * LANES
    row_a, row_b = pl.pallas_call(
        row_pack,
        out_shape=(shape(2 * SUBS, wide),) * 2,
        grid=(1,),
        in_specs=[
            scalar,
            scalar,
            block((SUBS, width), 0, 0),
            block((SUBS, width), last_row, 0),
            block((SUBS, width), 0, 0),
            block((SUBS, width), last_row, 0),
            whole(SUBS, LANES),
            whole(SUBS, LANES),
        ],
        out_specs=[whole(2 * SUBS, wide)] * 2,
        compiler_params=params,
        name="row_pack",
    )(group, odd_x, elevation, elevation, surface_potential, surface_potential, seam, outer)
    sides = {}
    for name, value, axis, shifted in (
        ("row_b", row_b, "gx", True), ("row_a", row_a, "gx", False), ("x_b", x_b, "gy", True),
        ("x_a", x_a, "gy", False), ("far_b", far_b, "gx", True), ("far_a", far_a, "gx", False),
    ):
        sides[name] = lax.ppermute(value, axis, couples(axis, shifted))

    tiles = tile // LANES
    tall = rows + 2 * SUBS
    anywhere = pl.BlockSpec(memory_space=pl.ANY)
    tables = (shape(layers, tiles + 2, tall, LANES), shape(tiles + 2, tall, LANES))
    deep = rows + 3 * SUBS
    padded = (width // LANES + 2, deep, LANES)
    new_e, new_p, height, wide_e, wide_p, volume, depth = pl.pallas_call(
        surface,
        out_shape=(shape(rows, width),) * 2 + (shape(rows + SUBS, width),) + (shape(*padded),) * 2 + tables,
        in_specs=[scalar] * 2 + [vmem] * 6 + [hbm, vmem],
        out_specs=[vmem] * 7,
        scratch_shapes=[pltpu.VMEM(padded, f32)] * 4 + [pltpu.SemaphoreType.DMA((tiles,))],
        compiler_params=params,
        name="surface",
    )(
        group, odd_x, elevation, surface_potential, seam, outer, sides["row_a"], sides["row_b"],
        pltpu.with_memory_space_constraint(interior_potential, pltpu.HBM), seabed,
    )
    far_sides = [sides[name] for name in ("far_a", "far_b", "x_a", "x_b")]
    rims = pl.pallas_call(
        rim_pack,
        out_shape=shape(SUBS, width),
        in_specs=[scalar] * 3 + [vmem] * 4 + [anywhere],
        out_specs=vmem,
        compiler_params=params,
        name="rim_pack",
    )(group, odd_x, odd_y, *far_sides, height)
    far_rims = lax.ppermute(rims, flat, partner)
    far_height = lax.ppermute(height, flat, partner)
    other_p = lax.ppermute(new_p, flat, partner)
    volume, depth = pl.pallas_call(
        fill,
        out_shape=tables,
        in_specs=[scalar] * 2 + [anywhere] * 2 + [vmem] * 4,
        out_specs=[anywhere] * 2,
        scratch_shapes=[
            pltpu.VMEM((2, layers, rows, LANES), f32),
            pltpu.VMEM((2, rows, LANES), f32),
            pltpu.VMEM((2, layers, tiles, SUBS, LANES), f32),
            pltpu.VMEM((2, tiles, SUBS, LANES), f32),
            pltpu.SemaphoreType.DMA((8,)),
        ],
        input_output_aliases={2: 0, 3: 1},
        compiler_params=params,
        name="fill",
    )(odd_x, odd_y, volume, depth, *far_sides)
    blocks = rows // SUBS
    tables = (volume, depth, far_layer, far_rims, wide_e)
    ghost = pltpu.VMEM((width // LANES + 2, tall, LANES), f32)
    partial = pl.pallas_call(
        functools.partial(own_half, total_layers),
        out_shape=shape(layers, rows, tile),
        grid_spec=pltpu.PrefetchScalarGridSpec(
            num_scalar_prefetch=1,
            grid=(blocks,),
            in_specs=[vmem] * 6,
            out_specs=pl.BlockSpec((layers, SUBS, width), lambda i, g: (0, i, g[0])),
            scratch_shapes=[ghost],
        ),
        compiler_params=params,
        name="own_half",
    )(group, *tables, wide_p)
    partial, part, coefficients = pl.pallas_call(
        functools.partial(other_half, total_layers),
        out_shape=(shape(layers, rows, tile), shape(rows, width), shape(3, rows, width)),
        grid_spec=pltpu.PrefetchScalarGridSpec(
            num_scalar_prefetch=1,
            grid=(blocks,),
            in_specs=[hbm] + [vmem] * 6,
            out_specs=[
                pl.BlockSpec((layers, SUBS, width), lambda i, g: (0, i, 1 - g[0])),
                pl.BlockSpec((SUBS, width), lambda i, g: (i, 0)),
                pl.BlockSpec((3, SUBS, width), lambda i, g: (0, i, 0)),
            ],
            scratch_shapes=[ghost] * 2,
        ),
        input_output_aliases={1: 0},
        compiler_params=params,
        name="other_half",
    )(group, partial, *tables, far_height)
    result = pl.pallas_call(
        top,
        out_shape=shape(layers, rows, tile),
        grid_spec=pltpu.PrefetchScalarGridSpec(
            num_scalar_prefetch=1,
            grid=(1,),
            in_specs=[hbm] + [vmem] * 5,
            out_specs=pl.BlockSpec((1, rows, width), lambda i, g: (layers - 1, 0, 1 - g[0])),
            scratch_shapes=[pltpu.VMEM((width // LANES + 2, tall, LANES), f32)],
        ),
        input_output_aliases={1: 0},
        compiler_params=params,
        name="top",
    )(group, partial, part, coefficients, far_height, wide_p, other_p)
    return new_e, new_p, result


def solution(mesh):
    return jax.shard_map(
        shards,
        mesh=mesh,
        in_specs=(P("gx", ("gy", "gz")), P("gx", ("gy", "gz")), P("gx", "gy"), P("gz", "gx", "gy")),
        out_specs=(P("gx", ("gy", "gz")), P("gx", ("gy", "gz")), P("gz", "gx", "gy")),
        check_vma=False,
    )
```

```python
import functools

import jax
import jax.numpy as jnp
from jax import lax
from jax.experimental import pallas as pl
from jax.experimental.pallas import tpu as pltpu
from jax.sharding import PartitionSpec as P

time_step = 0.05
depth_unit = 0.015625
LANES = 128
SUBS = 8


def shift_lanes(left, cur, right, step):
    lane = lax.broadcasted_iota(jnp.int32, cur.shape, 1)
    if step < 0:
        return pltpu.roll(jnp.where(lane >= LANES + step, left, cur), -step, 1)
    return pltpu.roll(jnp.where(lane < step, right, cur), LANES - step, 1)


def square(tile, at_end):
    rest = jnp.zeros((LANES - tile.shape[0], LANES), tile.dtype)
    return jnp.concatenate([rest, tile] if at_end else [tile, rest], 0)


def first_pack(group, e, p, v, seam, outer, layer, edges, sems):
    rows, width = e.shape
    low = group[0] == 0
    source = jnp.where(low, v.shape[0] - 1, 0)
    whole = pltpu.make_async_copy(v.at[source], layer, sems.at[4])
    copies = []
    for index, (field, start) in enumerate(((e, 0), (p, 0), (e, width - LANES), (p, width - LANES))):
        into = edges.at[index // 2, (index % 2) * rows : (index % 2 + 1) * rows, :]
        copies.append(pltpu.make_async_copy(field.at[:, start : start + LANES], into, sems.at[index]))
    for copy in copies:
        copy.start()
    whole.start()
    for copy in copies:
        copy.wait()
    left = edges[0].T[:SUBS]
    right = edges[1].T[LANES - SUBS :]
    seam[...] = jnp.where(low, right, left)
    outer[...] = jnp.where(low, left, right)
    whole.wait()


def by_parity(odd, fill, first, second):
    @pl.when(odd[0] == 0)
    def _():
        fill(first, second)

    @pl.when(odd[0] == 1)
    def _():
        fill(second, first)


def lazy_pack(
    odd_x, odd_y, v_top, v_bottom, v_left, v_right, s_top, s_bottom, s_left, s_right, row_a, row_b, column_a, column_b
):
    by_parity(odd_x, functools.partial(pack_rows, v_top, v_bottom, s_top, s_bottom), row_a, row_b)
    by_parity(odd_y, functools.partial(pack_columns, v_left, v_right, s_left, s_right), column_a, column_b)


def pack_rows(v_top, v_bottom, s_top, s_bottom, up, down):
    layers, _, width = v_top.shape
    piece = width // SUBS
    for k in range(layers):
        up[k : k + 1, :width] = v_bottom[k, SUBS - 1 : SUBS, :]
        down[k : k + 1, :width] = v_top[k, 0:1, :]
    for q in range(SUBS):
        part = slice(q * piece, (q + 1) * piece)
        up[q : q + 1, width:] = s_bottom[SUBS - 1 : SUBS, part].astype(jnp.float32) * depth_unit
        down[q : q + 1, width:] = s_top[0:1, part].astype(jnp.float32) * depth_unit


def pack_columns(v_left, v_right, s_left, s_right, to_right, to_left):
    layers = v_left.shape[0]
    to_right[...] = jnp.zeros_like(to_right)
    to_left[...] = jnp.zeros_like(to_left)
    for j in range(layers // 2):
        both = jnp.concatenate([v_right[2 * j], v_right[2 * j + 1]], 0).T
        to_right[j : j + 1, :] = both[LANES - 1 :]
        both = jnp.concatenate([v_left[2 * j], v_left[2 * j + 1]], 0).T
        to_left[j : j + 1, :] = both[:1]
    j = layers // 2
    both = jnp.concatenate([s_right[...], s_right[...]], 0).astype(jnp.float32) * depth_unit
    to_right[j : j + 1, :] = both.T[LANES - 1 :]
    both = jnp.concatenate([s_left[...], s_left[...]], 0).astype(jnp.float32) * depth_unit
    to_left[j : j + 1, :] = both.T[:1]


def side_blocks(low, seam, outer):
    left = square(jnp.where(low, outer, seam), True).T
    right = square(jnp.where(low, seam, outer), False).T
    return left, right


def row_pack(group, odd_x, e_top, e_bottom, p_top, p_bottom, seam, outer, row_a, row_b):
    left, right = side_blocks(group[0] == 0, seam[...], outer[...])
    by_parity(odd_x, functools.partial(pack_surface_rows, left, right, e_top, e_bottom, p_top, p_bottom), row_a, row_b)


REACH = 5


def spare_piece(index, tiles):
    start = (tiles + index // SUBS) * LANES
    return slice(index % SUBS, index % SUBS + 1), slice(start, start + LANES)


def pack_surface_rows(left, right, e_top, e_bottom, p_top, p_bottom, up, down):
    rows = LANES // 2
    tiles = e_top.shape[1] // LANES + 2
    fit = SUBS - REACH
    for into, first, e_rows, p_rows in ((up, rows - REACH, e_bottom, p_bottom), (down, 0, e_top, p_top)):
        start = first % SUBS
        for t in range(tiles):
            part = slice(t * LANES, (t + 1) * LANES)
            if 0 < t < tiles - 1:
                own = slice((t - 1) * LANES, t * LANES)
                e_part = e_rows[start : start + REACH, own]
                p_part = p_rows[start : start + REACH, own]
            else:
                side = left if t == 0 else right
                e_part = side[first : first + REACH]
                p_part = side[rows + first : rows + first + REACH]
            into[:REACH, part] = e_part
            into[REACH:, part] = p_part[:fit]
            for extra in range(REACH - fit):
                row, lanes = spare_piece(extra * tiles + t, tiles)
                into[row, lanes] = p_part[fit + extra : fit + extra + 1]


def neighbourhood(ref, lane_tile, row):
    last = ref.shape[0] - 1
    at = lambda column, step: ref[column, pl.ds(row + step, SUBS), :]
    cur = at(lane_tile, 0)
    left, right = at(max(lane_tile - 1, 0), 0), at(min(lane_tile + 1, last), 0)
    rows = [at(lane_tile, step) for step in (-2, -1, 1, 2)]
    lanes = [shift_lanes(left, cur, right, step) for step in (-2, -1, 1, 2)]
    return cur, rows, lanes


def slope(values):
    return (2.0 / 3.0) * (values[2] - values[1]) - (1.0 / 12.0) * (values[3] - values[0])


def tile_rates(e_near, p_near):
    e, e_rows, e_lanes = e_near
    p, p_rows, p_lanes = p_near
    p_x, p_y = slope(p_rows), slope(p_lanes)
    near = (p_rows[1] + p_rows[2]) + (p_lanes[1] + p_lanes[2])
    far = (p_rows[0] + p_rows[3]) + (p_lanes[0] + p_lanes[3])
    bend = (4.0 / 3.0) * near - (1.0 / 12.0) * far - 5.0 * p
    rate_e = bend - (slope(e_rows) * p_x + slope(e_lanes) * p_y)
    rate_p = 0.5 * (p_x * p_x + p_y * p_y) + e
    return e, p, time_step * rate_e, -time_step * rate_p


def surface(
    group, odd_x, e, p, seam, outer, row_a, row_b, v, sea,
    new_e, new_p, height, wide_e, wide_p, volume, depth, e0, p0, e1, p1, sems,
):
    rows, width = e.shape
    low = group[0] == 0
    copies = []
    for t in range(v.shape[2] // LANES):
        part = slice(t * LANES, (t + 1) * LANES)
        into = volume.at[:, t + 1, SUBS : SUBS + rows, :]
        copies.append(pltpu.make_async_copy(v.at[:, :, part], into, sems.at[t]))
        copies[-1].start()
    left, right = side_blocks(low, seam[...], outer[...])
    tiles = width // LANES + 2
    inner = slice(SUBS, SUBS + rows)
    fields = ((e0, e, 0), (p0, p, LANES // 2))
    fit = SUBS - REACH

    def ends(south, north):
        for source, first in ((north, SUBS - REACH), (south, SUBS + rows)):
            for t in range(tiles):
                part = slice(t * LANES, (t + 1) * LANES)
                e0[t, first : first + REACH, :] = source[:REACH, part]
                p0[t, first : first + fit, :] = source[REACH:, part]
                for extra in range(REACH - fit):
                    row = first + fit + extra
                    p0[t, row : row + 1, :] = source[spare_piece(extra * tiles + t, tiles)]

    by_parity(odd_x, ends, row_a, row_b)
    for old, source, base in fields:
        for t in range(1, tiles - 1):
            old[t, inner, :] = source[:, (t - 1) * LANES : t * LANES]
        old[0, inner, :] = left[base : base + rows]
        old[tiles - 1, inner, :] = right[base : base + rows]
    blocks = rows // SUBS + 1

    def first(block, carry):
        row = block * SUBS + SUBS - 3
        for t in range(tiles):
            old_e, old_p, step_e, step_p = tile_rates(neighbourhood(e0, t, row), neighbourhood(p0, t, row))
            e1[t, pl.ds(row, SUBS), :] = old_e + step_e
            p1[t, pl.ds(row, SUBS), :] = old_p + step_p
        return carry

    lax.fori_loop(0, blocks, first, 0, unroll=True)

    def second(block, carry):
        row = block * SUBS + SUBS - 1
        for t in range(tiles):
            one_e, one_p, step_e, step_p = tile_rates(neighbourhood(e1, t, row), neighbourhood(p1, t, row))
            old_e = e0[t, pl.ds(row, SUBS), :]
            old_p = p0[t, pl.ds(row, SUBS), :]
            wide_e[t, pl.ds(row, SUBS), :] = 0.5 * ((old_e + one_e) + step_e)
            wide_p[t, pl.ds(row, SUBS), :] = 0.5 * ((old_p + one_p) + step_p)
        return carry

    lax.fori_loop(0, blocks, second, 0, unroll=True)
    for t in range(1, tiles - 1):
        part = slice((t - 1) * LANES, t * LANES)
        tile_e = wide_e[t, inner, :]
        new_e[:, part] = tile_e
        height[:rows, part] = tile_e
        new_p[:, part] = wide_p[t, inner, :]
        for row, wide in ((0, wide_e), (2, wide_p)):
            height[rows + row : rows + row + 1, part] = wide[t, SUBS - 1 : SUBS, :]
            height[rows + row + 1 : rows + row + 2, part] = wide[t, SUBS + rows : SUBS + rows + 1, :]
        height[rows + 4 :, part] = jnp.zeros((4, LANES), jnp.float32)
    left = jnp.concatenate([wide_e[0, inner, :], wide_p[0, inner, :]], 0).T[LANES - 1 :]
    right = jnp.concatenate([wide_e[tiles - 1, inner, :], wide_p[tiles - 1, inner, :]], 0).T[:1]
    height[rows + 4 : rows + 5, :LANES] = jnp.where(low, left, right)
    for t in range(v.shape[2] // LANES):
        depth[t + 1, inner, :] = sea[:, t * LANES : (t + 1) * LANES].astype(jnp.float32) * depth_unit
    for copy in copies:
        copy.wait()


def rim_pack(group, odd_x, odd_y, far_a, far_b, x_a, x_b, after, rims):
    del after
    low = group[0] == 0
    layers = far_a.shape[0]
    width = rims.shape[1]
    pairs = layers // 2
    rims[...] = jnp.zeros_like(rims)

    def rows(far_south, far_north):
        for row, side in ((0, far_north), (2, far_south)):
            for half in range(2):
                part = slice(half * width, (half + 1) * width)
                rims[row + half : row + half + 1, :] = jnp.where(low, side[layers - 1 : layers, part], side[0:1, part])

    by_parity(odd_x, rows, far_a, far_b)

    def columns(x_right, x_left):
        for lane, side in ((0, x_left), (LANES, x_right)):
            top_pair = pltpu.roll(side[...], LANES // 2, 1)[pairs - 1 : pairs]
            rims[4:5, lane : lane + LANES] = jnp.where(low, top_pair, side[0:1, :])

    by_parity(odd_y, columns, x_a, x_b)


def fill(
    odd_x, odd_y, old_volume, old_depth, far_a, far_b, x_a, x_b, volume, depth, sides, depths, edges, ends, sems
):
    del old_volume, old_depth
    layers, tiles, tall = volume.shape[0], volume.shape[1], volume.shape[2]
    rows, tile = tall - 2 * SUBS, (tiles - 2) * LANES
    inner = slice(SUBS, SUBS + rows)
    even = odd_y[0] == 0
    left = square(jnp.where(even, x_b[...], x_a[...]), False).T
    right = square(jnp.where(even, x_a[...], x_b[...]), False).T
    half, pairs = LANES // 2, layers // 2
    for k in range(layers):
        base = (k % 2) * half
        sides[0, k] = pltpu.roll(left, LANES - 1 - k // 2, 1)[base : base + rows]
        sides[1, k] = pltpu.roll(right, (LANES - k // 2) % LANES, 1)[base : base + rows]
    depths[0] = pltpu.roll(left, LANES - 1 - pairs, 1)[:rows]
    depths[1] = pltpu.roll(right, LANES - pairs, 1)[:rows]
    piece = tile // SUBS // LANES

    def fill_ends(far_south, far_north):
        for end, source, row in ((0, far_north, SUBS - 1), (1, far_south, 0)):
            for t in range(tiles - 2):
                for k in range(layers):
                    edges[end, k, t, row : row + 1, :] = source[k : k + 1, t * LANES : (t + 1) * LANES]
                q, start = t // piece, tile + (t % piece) * LANES
                ends[end, t, row : row + 1, :] = source[q : q + 1, start : start + LANES]

    by_parity(odd_x, fill_ends, far_a, far_b)
    copies = []
    for index, (t, at) in enumerate(((0, slice(0, SUBS)), (tiles - 1, slice(tall - SUBS, tall)))):
        for source, target in (
            (sides.at[index], volume.at[:, t, inner, :]),
            (depths.at[index], depth.at[t, inner, :]),
            (edges.at[index], volume.at[:, 1 : tiles - 1, at, :]),
            (ends.at[index], depth.at[1 : tiles - 1, at, :]),
        ):
            copies.append(pltpu.make_async_copy(source, target, sems.at[len(copies)]))
    for copy in copies:
        copy.start()
    for copy in copies:
        copy.wait()


def apply_tile(total_layers, group, block, volume, depth, t, heights, local, ghost, spot, mine, write, rest=None):
    low = group == 0
    layers = volume.shape[0]
    spacing = 1.0 / total_layers
    sigma = (group * layers).astype(jnp.float32) * spacing + 0.5 * spacing
    gain = (2 * group).astype(jnp.float32)
    here = pl.multiple_of((block + 1) * SUBS, SUBS)

    def near(ref, t):
        at = lambda column, step: ref[column, pl.ds(here + step, SUBS), :]
        cur = at(t, 0)
        left, right = at(t - 1, 0), at(t + 1, 0)
        return cur, at(t, -1), at(t, 1), shift_lanes(left, cur, right, -1), shift_lanes(left, cur, right, 1)

    def differences(ref, t):
        p, up, down, left, right = near(ref, t)
        return p, down - up, right - left

    d, d_x, d_y = differences(depth, t)
    h, h_x, h_y = differences(heights, local)
    inverse = 1.0 / (d + h)
    scale = (0.25 / spacing) * inverse
    bx, by = scale * (d_x + h_x), scale * (d_y + h_y)
    ux, uy = scale * d_x - sigma * bx, scale * d_y - sigma * by
    bx, by = spacing * bx, spacing * by
    scaled = inverse * (1.0 / spacing)
    weight = 4.0 * (ux * ux + uy * uy) + scaled * scaled
    bend = 4.0 * (bx * bx + by * by)
    step = bend - 8.0 * (ux * bx + uy * by)
    bend = bend + bend

    def level(k):
        p, up, down, left, right = near(volume.at[k], t)
        return p, down - up, right - left, ((down + up) + (right + left)) - 4.0 * p

    far = differences(ghost, spot)
    this = level(0)
    lower = [jnp.where(low, a, b) for a, b in zip(this, far)]
    rise_below = this[0] - lower[0]
    for k in range(layers):
        if k < layers - 1:
            upper = level(k + 1)
        else:
            upper = [jnp.where(low, a, -b) for a, b in zip(far, this)]
            if mine is not None:
                upper = [a + gain * b for a, b in zip(upper, differences(mine, local))]
        rise = upper[0] - this[0]
        value = this[3] + ux * (upper[1] - lower[1]) + uy * (upper[2] - lower[2])
        value = value + weight * (rise - rise_below)
        write(k, value)
        if k < layers - 1:
            ux, uy = ux - bx, uy - by
            weight, step = weight + step, step + bend
        elif rest is not None:
            rest(value, ux, uy, weight)
        lower, this, rise_below = this, upper, rise


def own_half(total_layers, group_ref, volume, depth, far_layer, rims, wide_e, wide_p, out, ghost):
    block = pl.program_id(0)
    group = group_ref[0]
    halves = volume.shape[1] // 2 - 1

    @pl.when(block == 0)
    def _():
        fill_ghost(group == 0, group, far_layer, rims, ghost)

    for local in range(1, halves + 1):

        def write(k, value):
            out[k, :, (local - 1) * LANES : local * LANES] = value

        apply_tile(
            total_layers, group, block, volume, depth, group * halves + local, wide_e, local, ghost, local, wide_p,
            write,
        )


def other_half(
    total_layers, group_ref, before, volume, depth, far_layer, rims, wide_e, height,
    out, part, coefficients, ghost, other_e,
):
    del before
    block = pl.program_id(0)
    group = group_ref[0]
    low = group == 0
    rows, width = other_e.shape[1] - 2 * SUBS, height.shape[1]
    halves = width // LANES
    inner = slice(SUBS, SUBS + rows)

    @pl.when(block == 0)
    def _():
        fill_ghost(group == 1, 1 - group, far_layer, rims, ghost)
        for t in range(halves):
            spot = slice(t * LANES, (t + 1) * LANES)
            other_e[t + 1, inner, :] = height[:rows, spot]
            other_e[t + 1, SUBS - 1 : SUBS, :] = height[rows : rows + 1, spot]
            other_e[t + 1, SUBS + rows : SUBS + rows + 1, :] = height[rows + 1 : rows + 2, spot]
        edge = square(height[rows:, :LANES], False).T[:rows]
        at_right, at_left = pltpu.roll(edge, LANES - 4, 1), pltpu.roll(edge, LANES - 5, 1)
        other_e[0, inner, :] = jnp.where(low, wide_e[halves, inner, :], at_left)
        other_e[halves + 1, inner, :] = jnp.where(low, at_right, wide_e[1, inner, :])

    for local in range(1, halves + 1):
        spot = slice((local - 1) * LANES, local * LANES)

        def write(k, value):
            out[k, :, spot] = value

        def rest(value, ux, uy, weight):
            part[:, spot] = value
            coefficients[0, :, spot] = ux
            coefficients[1, :, spot] = uy
            coefficients[2, :, spot] = weight

        apply_tile(
            total_layers, group, block, volume, depth, (1 - group) * halves + local, other_e, local, ghost, local,
            None, write, rest,
        )


def fill_ghost(first, half, far_layer, rims, ghost):
    rows, tile = far_layer.shape
    width = tile // 2
    halves = width // LANES
    inner = slice(SUBS, SUBS + rows)
    far_left = pltpu.roll(square(rims[:, :LANES], False).T, LANES - 5, 1)[:rows]
    far_right = pltpu.roll(square(rims[:, LANES : 2 * LANES], False).T, LANES - 4, 1)[:rows]
    ghost[0, inner, :] = jnp.where(first, far_left, far_layer[:, width - LANES : width])
    ghost[halves + 1, inner, :] = jnp.where(first, far_layer[:, width : width + LANES], far_right)
    for t in range(halves):
        spot = slice(t * LANES, (t + 1) * LANES)
        lanes = pl.ds(pl.multiple_of(half * width + t * LANES, LANES), LANES)
        ghost[t + 1, inner, :] = far_layer[:, lanes]
        ghost[t + 1, SUBS - 1 : SUBS, :] = jnp.where(first, rims[0:1, spot], rims[1:2, spot])
        ghost[t + 1, SUBS + rows : SUBS + rows + 1, :] = jnp.where(first, rims[2:3, spot], rims[3:4, spot])


def top(group_ref, before, part, coefficients, height, wide_p, other_p, out, potential):
    del before
    low = group_ref[0] == 0
    rows, width = other_p.shape
    halves = width // LANES
    inner = slice(SUBS, SUBS + rows)
    edge = square(height[rows:, :LANES], False).T[LANES // 2 : LANES // 2 + rows]
    potential[0, inner, :] = pltpu.roll(edge, LANES - 5, 1)
    potential[halves + 1, inner, :] = wide_p[1, inner, :]
    for t in range(halves):
        spot = slice(t * LANES, (t + 1) * LANES)
        potential[t + 1, inner, :] = other_p[:, spot]
        potential[t + 1, SUBS - 1 : SUBS, :] = height[rows + 2 : rows + 3, spot]
        potential[t + 1, SUBS + rows : SUBS + rows + 1, :] = height[rows + 3 : rows + 4, spot]

    def body(block, carry):
        here = pl.multiple_of((block + 1) * SUBS, SUBS)
        to = pl.ds(pl.multiple_of(block * SUBS, SUBS), SUBS)
        for t in range(1, halves + 1):
            at = lambda column, step: potential[column, pl.ds(here + step, SUBS), :]
            cur, left, right = at(t, 0), at(t - 1, 0), at(t + 1, 0)
            east = shift_lanes(left, cur, right, 1) - shift_lanes(left, cur, right, -1)
            spot = slice((t - 1) * LANES, t * LANES)
            value = coefficients[0, to, spot] * (at(t, 1) - at(t, -1)) + coefficients[1, to, spot] * east
            value = value + coefficients[2, to, spot] * cur
            partial = part[to, spot]
            out[0, to, spot] = jnp.where(low, partial, partial + 2.0 * value)
        return carry

    lax.fori_loop(0, rows // SUBS, body, 0)


def couples(axis, shifted):
    count = lax.axis_size(axis)
    start = 1 if shifted else 0
    one_way = [((i + start) % count, (i + start + 1) % count) for i in range(0, count, 2)]
    return one_way + [(b, a) for a, b in one_way]


def shards(elevation, surface_potential, seabed, interior_potential):
    rows, width = elevation.shape
    layers, _, tile = interior_potential.shape
    assert 2 * rows == LANES and tile == 2 * width and layers == SUBS
    assert lax.axis_size("gz") == 2
    total_layers = layers * lax.axis_size("gz")
    f32 = jnp.float32
    shape = lambda *dims: jax.ShapeDtypeStruct(dims, f32)
    whole = lambda *dims: pl.BlockSpec(dims, lambda *_: (0,) * len(dims))
    group = lax.axis_index("gz").astype(jnp.int32).reshape((1,))
    odd_x = (lax.axis_index("gx") & 1).astype(jnp.int32).reshape((1,))
    odd_y = (lax.axis_index("gy") & 1).astype(jnp.int32).reshape((1,))
    assert lax.axis_size("gx") % 2 == 0 and lax.axis_size("gy") % 2 == 0
    scalar = pl.BlockSpec(memory_space=pltpu.SMEM)
    last_row, last_tile = rows // SUBS - 1, tile // LANES - 1

    def block(dims, *index):
        return pl.BlockSpec(dims, lambda *_: index)

    params = pltpu.CompilerParams(vmem_limit_bytes=24 * 1024 * 1024)
    vmem = pl.BlockSpec(memory_space=pltpu.VMEM)
    hbm = pl.BlockSpec(memory_space=pltpu.HBM)
    seam, outer, layer = pl.pallas_call(
        first_pack,
        out_shape=(shape(SUBS, LANES), shape(SUBS, LANES), shape(rows, tile)),
        in_specs=[scalar, hbm, hbm, hbm],
        out_specs=[vmem] * 3,
        scratch_shapes=[pltpu.VMEM((2, LANES, LANES), f32), pltpu.SemaphoreType.DMA((5,))],
        compiler_params=params,
        name="first_pack",
    )(group, *(pltpu.with_memory_space_constraint(x, pltpu.HBM) for x in (elevation, surface_potential, interior_potential)))

    flat = ("gy", "gz")
    count = lax.axis_size("gy")
    partner = [(2 * i + g, 2 * i + 1 - g) for i in range(count) for g in range(2)]
    across = [(2 * i + 1, (2 * i + 2) % (2 * count)) for i in range(count)]
    across = across + [(b, a) for a, b in across]
    seam = lax.ppermute(seam, flat, partner)
    far_layer = lax.ppermute(layer, flat, partner)
    outer = lax.ppermute(outer, flat, across)

    tiles = tile // LANES
    tall = rows + 2 * SUBS
    tables = (shape(layers, tiles + 2, tall, LANES), shape(tiles + 2, tall, LANES))
    anywhere = pl.BlockSpec(memory_space=pl.ANY)
    far_a, far_b, x_a, x_b = pl.pallas_call(
        lazy_pack,
        out_shape=(shape(SUBS, tile + tile // SUBS),) * 2 + (shape(SUBS, LANES),) * 2,
        grid=(1,),
        in_specs=[
            scalar,
            scalar,
            block((layers, SUBS, tile), 0, 0, 0),
            block((layers, SUBS, tile), 0, last_row, 0),
            block((layers, rows, LANES), 0, 0, 0),
            block((layers, rows, LANES), 0, 0, last_tile),
            block((SUBS, tile), 0, 0),
            block((SUBS, tile), last_row, 0),
            block((rows, LANES), 0, 0),
            block((rows, LANES), 0, last_tile),
        ],
        out_specs=[whole(SUBS, tile + tile // SUBS)] * 2 + [whole(SUBS, LANES)] * 2,
        compiler_params=params,
        name="lazy_pack",
    )(odd_x, odd_y, *(pltpu.with_memory_space_constraint(interior_potential, pltpu.HBM),) * 4, *(seabed,) * 4)

    wide = width + 2 * LANES
    packed = wide + pl.cdiv((2 * REACH - SUBS) * (wide // LANES), SUBS) * LANES
    row_a, row_b = pl.pallas_call(
        row_pack,
        out_shape=(shape(SUBS, packed),) * 2,
        grid=(1,),
        in_specs=[
            scalar,
            scalar,
            block((SUBS, width), 0, 0),
            block((SUBS, width), last_row, 0),
            block((SUBS, width), 0, 0),
            block((SUBS, width), last_row, 0),
            whole(SUBS, LANES),
            whole(SUBS, LANES),
        ],
        out_specs=[whole(SUBS, packed)] * 2,
        compiler_params=params,
        name="row_pack",
    )(group, odd_x, elevation, elevation, surface_potential, surface_potential, seam, outer)
    sides = {}
    for name, value, axis, shifted in (
        ("row_b", row_b, "gx", True), ("row_a", row_a, "gx", False), ("x_b", x_b, "gy", True),
        ("x_a", x_a, "gy", False), ("far_b", far_b, "gx", True), ("far_a", far_a, "gx", False),
    ):
        sides[name] = lax.ppermute(value, axis, couples(axis, shifted))

    tiles = tile // LANES
    tall = rows + 2 * SUBS
    anywhere = pl.BlockSpec(memory_space=pl.ANY)
    tables = (shape(layers, tiles + 2, tall, LANES), shape(tiles + 2, tall, LANES))
    deep = rows + 3 * SUBS
    padded = (width // LANES + 2, deep, LANES)
    new_e, new_p, height, wide_e, wide_p, volume, depth = pl.pallas_call(
        surface,
        out_shape=(shape(rows, width),) * 2 + (shape(rows + SUBS, width),) + (shape(*padded),) * 2 + tables,
        in_specs=[scalar] * 2 + [vmem] * 6 + [hbm, vmem],
        out_specs=[vmem] * 7,
        scratch_shapes=[pltpu.VMEM(padded, f32)] * 4 + [pltpu.SemaphoreType.DMA((tiles,))],
        compiler_params=params,
        name="surface",
    )(
        group, odd_x, elevation, surface_potential, seam, outer, sides["row_a"], sides["row_b"],
        pltpu.with_memory_space_constraint(interior_potential, pltpu.HBM), seabed,
    )
    far_sides = [sides[name] for name in ("far_a", "far_b", "x_a", "x_b")]
    rims = pl.pallas_call(
        rim_pack,
        out_shape=shape(SUBS, width),
        in_specs=[scalar] * 3 + [vmem] * 4 + [anywhere],
        out_specs=vmem,
        compiler_params=params,
        name="rim_pack",
    )(group, odd_x, odd_y, *far_sides, height)
    far_rims = lax.ppermute(rims, flat, partner)
    far_height = lax.ppermute(height, flat, partner)
    other_p = lax.ppermute(new_p, flat, partner)
    volume, depth = pl.pallas_call(
        fill,
        out_shape=tables,
        in_specs=[scalar] * 2 + [anywhere] * 2 + [vmem] * 4,
        out_specs=[anywhere] * 2,
        scratch_shapes=[
            pltpu.VMEM((2, layers, rows, LANES), f32),
            pltpu.VMEM((2, rows, LANES), f32),
            pltpu.VMEM((2, layers, tiles, SUBS, LANES), f32),
            pltpu.VMEM((2, tiles, SUBS, LANES), f32),
            pltpu.SemaphoreType.DMA((8,)),
        ],
        input_output_aliases={2: 0, 3: 1},
        compiler_params=params,
        name="fill",
    )(odd_x, odd_y, volume, depth, *far_sides)
    blocks = rows // SUBS
    tables = (volume, depth, far_layer, far_rims, wide_e)
    ghost = pltpu.VMEM((width // LANES + 2, tall, LANES), f32)
    partial = pl.pallas_call(
        functools.partial(own_half, total_layers),
        out_shape=shape(layers, rows, tile),
        grid_spec=pltpu.PrefetchScalarGridSpec(
            num_scalar_prefetch=1,
            grid=(blocks,),
            in_specs=[vmem] * 6,
            out_specs=pl.BlockSpec((layers, SUBS, width), lambda i, g: (0, i, g[0])),
            scratch_shapes=[ghost],
        ),
        compiler_params=params,
        name="own_half",
    )(group, *tables, wide_p)
    partial, part, coefficients = pl.pallas_call(
        functools.partial(other_half, total_layers),
        out_shape=(shape(layers, rows, tile), shape(rows, width), shape(3, rows, width)),
        grid_spec=pltpu.PrefetchScalarGridSpec(
            num_scalar_prefetch=1,
            grid=(blocks,),
            in_specs=[hbm] + [vmem] * 6,
            out_specs=[
                pl.BlockSpec((layers, SUBS, width), lambda i, g: (0, i, 1 - g[0])),
                pl.BlockSpec((SUBS, width), lambda i, g: (i, 0)),
                pl.BlockSpec((3, SUBS, width), lambda i, g: (0, i, 0)),
            ],
            scratch_shapes=[ghost] * 2,
        ),
        input_output_aliases={1: 0},
        compiler_params=params,
        name="other_half",
    )(group, partial, *tables, far_height)
    result = pl.pallas_call(
        top,
        out_shape=shape(layers, rows, tile),
        grid_spec=pltpu.PrefetchScalarGridSpec(
            num_scalar_prefetch=1,
            grid=(1,),
            in_specs=[hbm] + [vmem] * 5,
            out_specs=pl.BlockSpec((1, rows, width), lambda i, g: (layers - 1, 0, 1 - g[0])),
            scratch_shapes=[pltpu.VMEM((width // LANES + 2, tall, LANES), f32)],
        ),
        input_output_aliases={1: 0},
        compiler_params=params,
        name="top",
    )(group, partial, part, coefficients, far_height, wide_p, other_p)
    return new_e, new_p, result


def solution(mesh):
    return jax.shard_map(
        shards,
        mesh=mesh,
        in_specs=(P("gx", ("gy", "gz")), P("gx", ("gy", "gz")), P("gx", "gy"), P("gz", "gx", "gy")),
        out_specs=(P("gx", ("gy", "gz")), P("gx", ("gy", "gz")), P("gz", "gx", "gy")),
        check_vma=False,
    )
```

```python
import functools

import jax
import jax.numpy as jnp
from jax import lax
from jax.experimental import pallas as pl
from jax.experimental.pallas import tpu as pltpu
from jax.sharding import PartitionSpec as P

time_step = 0.05
depth_unit = 0.015625
LANES = 128
SUBS = 8


def shift_lanes(left, cur, right, step):
    lane = lax.broadcasted_iota(jnp.int32, cur.shape, 1)
    if step < 0:
        return pltpu.roll(jnp.where(lane >= LANES + step, left, cur), -step, 1)
    return pltpu.roll(jnp.where(lane < step, right, cur), LANES - step, 1)


def square(tile, at_end):
    rest = jnp.zeros((LANES - tile.shape[0], LANES), tile.dtype)
    return jnp.concatenate([rest, tile] if at_end else [tile, rest], 0)


def first_pack(group, e, p, v, seam, outer, layer, edges, sems):
    rows, width = e.shape
    low = group[0] == 0
    source = jnp.where(low, v.shape[0] - 1, 0)
    whole = pltpu.make_async_copy(v.at[source], layer, sems.at[4])
    copies = []
    for index, (field, start) in enumerate(((e, 0), (p, 0), (e, width - LANES), (p, width - LANES))):
        into = edges.at[index // 2, (index % 2) * rows : (index % 2 + 1) * rows, :]
        copies.append(pltpu.make_async_copy(field.at[:, start : start + LANES], into, sems.at[index]))
    for copy in copies:
        copy.start()
    whole.start()
    for copy in copies:
        copy.wait()
    left = edges[0].T[:SUBS]
    right = edges[1].T[LANES - SUBS :]
    seam[...] = jnp.where(low, right, left)
    outer[...] = jnp.where(low, left, right)
    whole.wait()


def by_parity(odd, fill, first, second):
    @pl.when(odd[0] == 0)
    def _():
        fill(first, second)

    @pl.when(odd[0] == 1)
    def _():
        fill(second, first)


def lazy_pack(
    odd_x, odd_y, v_top, v_bottom, v_left, v_right, s_top, s_bottom, s_left, s_right, row_a, row_b, column_a, column_b
):
    by_parity(odd_x, functools.partial(pack_rows, v_top, v_bottom, s_top, s_bottom), row_a, row_b)
    by_parity(odd_y, functools.partial(pack_columns, v_left, v_right, s_left, s_right), column_a, column_b)


def pack_rows(v_top, v_bottom, s_top, s_bottom, up, down):
    layers, _, width = v_top.shape
    piece = width // SUBS
    for k in range(layers):
        up[k : k + 1, :width] = v_bottom[k, SUBS - 1 : SUBS, :]
        down[k : k + 1, :width] = v_top[k, 0:1, :]
    for q in range(SUBS):
        part = slice(q * piece, (q + 1) * piece)
        up[q : q + 1, width:] = s_bottom[SUBS - 1 : SUBS, part].astype(jnp.float32) * depth_unit
        down[q : q + 1, width:] = s_top[0:1, part].astype(jnp.float32) * depth_unit


def pack_columns(v_left, v_right, s_left, s_right, to_right, to_left):
    layers = v_left.shape[0]
    to_right[...] = jnp.zeros_like(to_right)
    to_left[...] = jnp.zeros_like(to_left)
    for j in range(layers // 2):
        both = jnp.concatenate([v_right[2 * j], v_right[2 * j + 1]], 0).T
        to_right[j : j + 1, :] = both[LANES - 1 :]
        both = jnp.concatenate([v_left[2 * j], v_left[2 * j + 1]], 0).T
        to_left[j : j + 1, :] = both[:1]
    j = layers // 2
    both = jnp.concatenate([s_right[...], s_right[...]], 0).astype(jnp.float32) * depth_unit
    to_right[j : j + 1, :] = both.T[LANES - 1 :]
    both = jnp.concatenate([s_left[...], s_left[...]], 0).astype(jnp.float32) * depth_unit
    to_left[j : j + 1, :] = both.T[:1]


def side_blocks(low, seam, outer):
    left = square(jnp.where(low, outer, seam), True).T
    right = square(jnp.where(low, seam, outer), False).T
    return left, right


def block_pack(group, seam, outer, blocks):
    blocks[0], blocks[1] = side_blocks(group[0] == 0, seam[...], outer[...])


def row_pack(group, odd_x, e_top, e_bottom, p_top, p_bottom, seam, outer, row_a, row_b):
    left, right = side_blocks(group[0] == 0, seam[...], outer[...])
    by_parity(odd_x, functools.partial(pack_surface_rows, left, right, e_top, e_bottom, p_top, p_bottom), row_a, row_b)


REACH = 5


def spare_piece(index, tiles):
    start = (tiles + index // SUBS) * LANES
    return slice(index % SUBS, index % SUBS + 1), slice(start, start + LANES)


def pack_surface_rows(left, right, e_top, e_bottom, p_top, p_bottom, up, down):
    rows = LANES // 2
    tiles = e_top.shape[1] // LANES + 2
    fit = SUBS - REACH
    for into, first, e_rows, p_rows in ((up, rows - REACH, e_bottom, p_bottom), (down, 0, e_top, p_top)):
        start = first % SUBS
        for t in range(tiles):
            part = slice(t * LANES, (t + 1) * LANES)
            if 0 < t < tiles - 1:
                own = slice((t - 1) * LANES, t * LANES)
                e_part = e_rows[start : start + REACH, own]
                p_part = p_rows[start : start + REACH, own]
            else:
                side = left if t == 0 else right
                e_part = side[first : first + REACH]
                p_part = side[rows + first : rows + first + REACH]
            into[:REACH, part] = e_part
            into[REACH:, part] = p_part[:fit]
            for extra in range(REACH - fit):
                row, lanes = spare_piece(extra * tiles + t, tiles)
                into[row, lanes] = p_part[fit + extra : fit + extra + 1]


def neighbourhood(ref, lane_tile, row):
    last = ref.shape[0] - 1
    at = lambda column, step: ref[column, pl.ds(row + step, SUBS), :]
    cur = at(lane_tile, 0)
    left, right = at(max(lane_tile - 1, 0), 0), at(min(lane_tile + 1, last), 0)
    rows = [at(lane_tile, step) for step in (-2, -1, 1, 2)]
    lanes = [shift_lanes(left, cur, right, step) for step in (-2, -1, 1, 2)]
    return cur, rows, lanes


def slope(values):
    return (2.0 / 3.0) * (values[2] - values[1]) - (1.0 / 12.0) * (values[3] - values[0])


def tile_rates(e_near, p_near):
    e, e_rows, e_lanes = e_near
    p, p_rows, p_lanes = p_near
    p_x, p_y = slope(p_rows), slope(p_lanes)
    near = (p_rows[1] + p_rows[2]) + (p_lanes[1] + p_lanes[2])
    far = (p_rows[0] + p_rows[3]) + (p_lanes[0] + p_lanes[3])
    bend = (4.0 / 3.0) * near - (1.0 / 12.0) * far - 5.0 * p
    rate_e = bend - (slope(e_rows) * p_x + slope(e_lanes) * p_y)
    rate_p = 0.5 * (p_x * p_x + p_y * p_y) + e
    return e, p, time_step * rate_e, -time_step * rate_p


def surface(
    odd_x, e, p, side_tiles, group, row_a, row_b, v, sea,
    new_e, new_p, height, wide_e, wide_p, volume, depth, e0, p0, e1, p1, sems,
):
    rows, width = e.shape
    low = group[0] == 0
    left, right = side_tiles[0], side_tiles[1]
    copies = []
    for t in range(v.shape[2] // LANES):
        part = slice(t * LANES, (t + 1) * LANES)
        into = volume.at[:, t + 1, SUBS : SUBS + rows, :]
        copies.append(pltpu.make_async_copy(v.at[:, :, part], into, sems.at[t]))
        copies[-1].start()
    tiles = width // LANES + 2
    inner = slice(SUBS, SUBS + rows)
    fields = ((e0, e, 0), (p0, p, LANES // 2))
    fit = SUBS - REACH

    def ends(south, north):
        for source, first in ((north, SUBS - REACH), (south, SUBS + rows)):
            for t in range(tiles):
                part = slice(t * LANES, (t + 1) * LANES)
                e0[t, first : first + REACH, :] = source[:REACH, part]
                p0[t, first : first + fit, :] = source[REACH:, part]
                for extra in range(REACH - fit):
                    row = first + fit + extra
                    p0[t, row : row + 1, :] = source[spare_piece(extra * tiles + t, tiles)]

    by_parity(odd_x, ends, row_a, row_b)
    for old, source, base in fields:
        for t in range(1, tiles - 1):
            old[t, inner, :] = source[:, (t - 1) * LANES : t * LANES]
        old[0, inner, :] = left[base : base + rows]
        old[tiles - 1, inner, :] = right[base : base + rows]
    blocks = rows // SUBS + 1

    def first(block, carry):
        row = block * SUBS + SUBS - 3
        for t in range(tiles):
            old_e, old_p, step_e, step_p = tile_rates(neighbourhood(e0, t, row), neighbourhood(p0, t, row))
            e1[t, pl.ds(row, SUBS), :] = old_e + step_e
            p1[t, pl.ds(row, SUBS), :] = old_p + step_p
        return carry

    lax.fori_loop(0, blocks, first, 0, unroll=True)

    def second(block, carry):
        row = block * SUBS + SUBS - 1
        for t in range(tiles):
            one_e, one_p, step_e, step_p = tile_rates(neighbourhood(e1, t, row), neighbourhood(p1, t, row))
            old_e = e0[t, pl.ds(row, SUBS), :]
            old_p = p0[t, pl.ds(row, SUBS), :]
            wide_e[t, pl.ds(row, SUBS), :] = 0.5 * ((old_e + one_e) + step_e)
            wide_p[t, pl.ds(row, SUBS), :] = 0.5 * ((old_p + one_p) + step_p)
        return carry

    lax.fori_loop(0, blocks, second, 0, unroll=True)
    for t in range(1, tiles - 1):
        part = slice((t - 1) * LANES, t * LANES)
        tile_e = wide_e[t, inner, :]
        new_e[:, part] = tile_e
        height[:rows, part] = tile_e
        new_p[:, part] = wide_p[t, inner, :]
        for row, wide in ((0, wide_e), (2, wide_p)):
            height[rows + row : rows + row + 1, part] = wide[t, SUBS - 1 : SUBS, :]
            height[rows + row + 1 : rows + row + 2, part] = wide[t, SUBS + rows : SUBS + rows + 1, :]
        height[rows + 4 :, part] = jnp.zeros((4, LANES), jnp.float32)
    left = jnp.concatenate([wide_e[0, inner, :], wide_p[0, inner, :]], 0).T[LANES - 1 :]
    right = jnp.concatenate([wide_e[tiles - 1, inner, :], wide_p[tiles - 1, inner, :]], 0).T[:1]
    height[rows + 4 : rows + 5, :LANES] = jnp.where(low, left, right)
    for t in range(v.shape[2] // LANES):
        depth[t + 1, inner, :] = sea[:, t * LANES : (t + 1) * LANES].astype(jnp.float32) * depth_unit
    for copy in copies:
        copy.wait()


def rim_pack(group, odd_x, odd_y, far_a, far_b, x_a, x_b, after, rims):
    del after
    low = group[0] == 0
    layers = far_a.shape[0]
    width = rims.shape[1]
    pairs = layers // 2
    rims[...] = jnp.zeros_like(rims)

    def rows(far_south, far_north):
        for row, side in ((0, far_north), (2, far_south)):
            for half in range(2):
                part = slice(half * width, (half + 1) * width)
                rims[row + half : row + half + 1, :] = jnp.where(low, side[layers - 1 : layers, part], side[0:1, part])

    by_parity(odd_x, rows, far_a, far_b)

    def columns(x_right, x_left):
        for lane, side in ((0, x_left), (LANES, x_right)):
            top_pair = pltpu.roll(side[...], LANES // 2, 1)[pairs - 1 : pairs]
            rims[4:5, lane : lane + LANES] = jnp.where(low, top_pair, side[0:1, :])

    by_parity(odd_y, columns, x_a, x_b)


def fill(
    odd_x, odd_y, old_volume, old_depth, far_a, far_b, x_a, x_b, volume, depth, sides, depths, edges, ends, sems
):
    del old_volume, old_depth
    layers, tiles, tall = volume.shape[0], volume.shape[1], volume.shape[2]
    rows, tile = tall - 2 * SUBS, (tiles - 2) * LANES
    inner = slice(SUBS, SUBS + rows)
    even = odd_y[0] == 0
    left = square(jnp.where(even, x_b[...], x_a[...]), False).T
    right = square(jnp.where(even, x_a[...], x_b[...]), False).T
    half, pairs = LANES // 2, layers // 2
    for k in range(layers):
        base = (k % 2) * half
        sides[0, k] = pltpu.roll(left, LANES - 1 - k // 2, 1)[base : base + rows]
        sides[1, k] = pltpu.roll(right, (LANES - k // 2) % LANES, 1)[base : base + rows]
    depths[0] = pltpu.roll(left, LANES - 1 - pairs, 1)[:rows]
    depths[1] = pltpu.roll(right, LANES - pairs, 1)[:rows]
    piece = tile // SUBS // LANES

    def fill_ends(far_south, far_north):
        for end, source, row in ((0, far_north, SUBS - 1), (1, far_south, 0)):
            for t in range(tiles - 2):
                for k in range(layers):
                    edges[end, k, t, row : row + 1, :] = source[k : k + 1, t * LANES : (t + 1) * LANES]
                q, start = t // piece, tile + (t % piece) * LANES
                ends[end, t, row : row + 1, :] = source[q : q + 1, start : start + LANES]

    by_parity(odd_x, fill_ends, far_a, far_b)
    copies = []
    for index, (t, at) in enumerate(((0, slice(0, SUBS)), (tiles - 1, slice(tall - SUBS, tall)))):
        for source, target in (
            (sides.at[index], volume.at[:, t, inner, :]),
            (depths.at[index], depth.at[t, inner, :]),
            (edges.at[index], volume.at[:, 1 : tiles - 1, at, :]),
            (ends.at[index], depth.at[1 : tiles - 1, at, :]),
        ):
            copies.append(pltpu.make_async_copy(source, target, sems.at[len(copies)]))
    for copy in copies:
        copy.start()
    for copy in copies:
        copy.wait()


def apply_tile(total_layers, group, block, volume, depth, t, heights, local, ghost, spot, mine, write, rest=None):
    low = group == 0
    layers = volume.shape[0]
    spacing = 1.0 / total_layers
    sigma = (group * layers).astype(jnp.float32) * spacing + 0.5 * spacing
    gain = (2 * group).astype(jnp.float32)
    here = pl.multiple_of((block + 1) * SUBS, SUBS)

    def near(ref, t):
        at = lambda column, step: ref[column, pl.ds(here + step, SUBS), :]
        cur = at(t, 0)
        left, right = at(t - 1, 0), at(t + 1, 0)
        return cur, at(t, -1), at(t, 1), shift_lanes(left, cur, right, -1), shift_lanes(left, cur, right, 1)

    def differences(ref, t):
        p, up, down, left, right = near(ref, t)
        return p, down - up, right - left

    d, d_x, d_y = differences(depth, t)
    h, h_x, h_y = differences(heights, local)
    inverse = 1.0 / (d + h)
    scale = (0.25 / spacing) * inverse
    bx, by = scale * (d_x + h_x), scale * (d_y + h_y)
    ux, uy = scale * d_x - sigma * bx, scale * d_y - sigma * by
    bx, by = spacing * bx, spacing * by
    scaled = inverse * (1.0 / spacing)
    weight = 4.0 * (ux * ux + uy * uy) + scaled * scaled
    bend = 4.0 * (bx * bx + by * by)
    step = bend - 8.0 * (ux * bx + uy * by)
    bend = bend + bend

    def level(k):
        p, up, down, left, right = near(volume.at[k], t)
        return p, down - up, right - left, ((down + up) + (right + left)) - 4.0 * p

    far = differences(ghost, spot)
    this = level(0)
    lower = [jnp.where(low, a, b) for a, b in zip(this, far)]
    rise_below = this[0] - lower[0]
    for k in range(layers):
        if k < layers - 1:
            upper = level(k + 1)
        else:
            upper = [jnp.where(low, a, -b) for a, b in zip(far, this)]
            if mine is not None:
                upper = [a + gain * b for a, b in zip(upper, differences(mine, local))]
        rise = upper[0] - this[0]
        value = this[3] + ux * (upper[1] - lower[1]) + uy * (upper[2] - lower[2])
        value = value + weight * (rise - rise_below)
        write(k, value)
        if k < layers - 1:
            ux, uy = ux - bx, uy - by
            weight, step = weight + step, step + bend
        elif rest is not None:
            rest(value, ux, uy, weight)
        lower, this, rise_below = this, upper, rise


def own_half(total_layers, group_ref, volume, depth, far_layer, rims, wide_e, wide_p, out, ghost):
    block = pl.program_id(0)
    group = group_ref[0]
    halves = volume.shape[1] // 2 - 1

    @pl.when(block == 0)
    def _():
        fill_ghost(group == 0, group, far_layer, rims, ghost)

    for local in range(1, halves + 1):

        def write(k, value):
            out[k, :, (local - 1) * LANES : local * LANES] = value

        apply_tile(
            total_layers, group, block, volume, depth, group * halves + local, wide_e, local, ghost, local, wide_p,
            write,
        )


def other_half(
    total_layers, group_ref, before, volume, depth, far_layer, rims, wide_e, height,
    out, part, coefficients, ghost, other_e,
):
    del before
    block = pl.program_id(0)
    group = group_ref[0]
    low = group == 0
    rows, width = other_e.shape[1] - 2 * SUBS, height.shape[1]
    halves = width // LANES
    inner = slice(SUBS, SUBS + rows)

    @pl.when(block == 0)
    def _():
        fill_ghost(group == 1, 1 - group, far_layer, rims, ghost)
        for t in range(halves):
            spot = slice(t * LANES, (t + 1) * LANES)
            other_e[t + 1, inner, :] = height[:rows, spot]
            other_e[t + 1, SUBS - 1 : SUBS, :] = height[rows : rows + 1, spot]
            other_e[t + 1, SUBS + rows : SUBS + rows + 1, :] = height[rows + 1 : rows + 2, spot]
        edge = square(height[rows:, :LANES], False).T[:rows]
        at_right, at_left = pltpu.roll(edge, LANES - 4, 1), pltpu.roll(edge, LANES - 5, 1)
        other_e[0, inner, :] = jnp.where(low, wide_e[halves, inner, :], at_left)
        other_e[halves + 1, inner, :] = jnp.where(low, at_right, wide_e[1, inner, :])

    for local in range(1, halves + 1):
        spot = slice((local - 1) * LANES, local * LANES)

        def write(k, value):
            out[k, :, spot] = value

        def rest(value, ux, uy, weight):
            part[:, spot] = value
            coefficients[0, :, spot] = ux
            coefficients[1, :, spot] = uy
            coefficients[2, :, spot] = weight

        apply_tile(
            total_layers, group, block, volume, depth, (1 - group) * halves + local, other_e, local, ghost, local,
            None, write, rest,
        )


def fill_ghost(first, half, far_layer, rims, ghost):
    rows, tile = far_layer.shape
    width = tile // 2
    halves = width // LANES
    inner = slice(SUBS, SUBS + rows)
    far_left = pltpu.roll(square(rims[:, :LANES], False).T, LANES - 5, 1)[:rows]
    far_right = pltpu.roll(square(rims[:, LANES : 2 * LANES], False).T, LANES - 4, 1)[:rows]
    ghost[0, inner, :] = jnp.where(first, far_left, far_layer[:, width - LANES : width])
    ghost[halves + 1, inner, :] = jnp.where(first, far_layer[:, width : width + LANES], far_right)
    for t in range(halves):
        spot = slice(t * LANES, (t + 1) * LANES)
        lanes = pl.ds(pl.multiple_of(half * width + t * LANES, LANES), LANES)
        ghost[t + 1, inner, :] = far_layer[:, lanes]
        ghost[t + 1, SUBS - 1 : SUBS, :] = jnp.where(first, rims[0:1, spot], rims[1:2, spot])
        ghost[t + 1, SUBS + rows : SUBS + rows + 1, :] = jnp.where(first, rims[2:3, spot], rims[3:4, spot])


def top(group_ref, before, part, coefficients, height, wide_p, other_p, out, potential):
    del before
    low = group_ref[0] == 0
    rows, width = other_p.shape
    halves = width // LANES
    inner = slice(SUBS, SUBS + rows)
    edge = square(height[rows:, :LANES], False).T[LANES // 2 : LANES // 2 + rows]
    potential[0, inner, :] = pltpu.roll(edge, LANES - 5, 1)
    potential[halves + 1, inner, :] = wide_p[1, inner, :]
    for t in range(halves):
        spot = slice(t * LANES, (t + 1) * LANES)
        potential[t + 1, inner, :] = other_p[:, spot]
        potential[t + 1, SUBS - 1 : SUBS, :] = height[rows + 2 : rows + 3, spot]
        potential[t + 1, SUBS + rows : SUBS + rows + 1, :] = height[rows + 3 : rows + 4, spot]

    def body(block, carry):
        here = pl.multiple_of((block + 1) * SUBS, SUBS)
        to = pl.ds(pl.multiple_of(block * SUBS, SUBS), SUBS)
        for t in range(1, halves + 1):
            at = lambda column, step: potential[column, pl.ds(here + step, SUBS), :]
            cur, left, right = at(t, 0), at(t - 1, 0), at(t + 1, 0)
            east = shift_lanes(left, cur, right, 1) - shift_lanes(left, cur, right, -1)
            spot = slice((t - 1) * LANES, t * LANES)
            value = coefficients[0, to, spot] * (at(t, 1) - at(t, -1)) + coefficients[1, to, spot] * east
            value = value + coefficients[2, to, spot] * cur
            partial = part[to, spot]
            out[0, to, spot] = jnp.where(low, partial, partial + 2.0 * value)
        return carry

    lax.fori_loop(0, rows // SUBS, body, 0)


def couples(axis, shifted):
    count = lax.axis_size(axis)
    start = 1 if shifted else 0
    one_way = [((i + start) % count, (i + start + 1) % count) for i in range(0, count, 2)]
    return one_way + [(b, a) for a, b in one_way]


def shards(elevation, surface_potential, seabed, interior_potential):
    rows, width = elevation.shape
    layers, _, tile = interior_potential.shape
    assert 2 * rows == LANES and tile == 2 * width and layers == SUBS
    assert lax.axis_size("gz") == 2
    total_layers = layers * lax.axis_size("gz")
    f32 = jnp.float32
    shape = lambda *dims: jax.ShapeDtypeStruct(dims, f32)
    whole = lambda *dims: pl.BlockSpec(dims, lambda *_: (0,) * len(dims))
    group = lax.axis_index("gz").astype(jnp.int32).reshape((1,))
    odd_x = (lax.axis_index("gx") & 1).astype(jnp.int32).reshape((1,))
    odd_y = (lax.axis_index("gy") & 1).astype(jnp.int32).reshape((1,))
    assert lax.axis_size("gx") % 2 == 0 and lax.axis_size("gy") % 2 == 0
    scalar = pl.BlockSpec(memory_space=pltpu.SMEM)
    last_row, last_tile = rows // SUBS - 1, tile // LANES - 1

    def block(dims, *index):
        return pl.BlockSpec(dims, lambda *_: index)

    params = pltpu.CompilerParams(vmem_limit_bytes=24 * 1024 * 1024)
    vmem = pl.BlockSpec(memory_space=pltpu.VMEM)
    hbm = pl.BlockSpec(memory_space=pltpu.HBM)
    seam, outer, layer = pl.pallas_call(
        first_pack,
        out_shape=(shape(SUBS, LANES), shape(SUBS, LANES), shape(rows, tile)),
        in_specs=[scalar, hbm, hbm, hbm],
        out_specs=[vmem] * 3,
        scratch_shapes=[pltpu.VMEM((2, LANES, LANES), f32), pltpu.SemaphoreType.DMA((5,))],
        compiler_params=params,
        name="first_pack",
    )(group, *(pltpu.with_memory_space_constraint(x, pltpu.HBM) for x in (elevation, surface_potential, interior_potential)))

    flat = ("gy", "gz")
    count = lax.axis_size("gy")
    partner = [(2 * i + g, 2 * i + 1 - g) for i in range(count) for g in range(2)]
    across = [(2 * i + 1, (2 * i + 2) % (2 * count)) for i in range(count)]
    across = across + [(b, a) for a, b in across]
    seam = lax.ppermute(seam, flat, partner)
    far_layer = lax.ppermute(layer, flat, partner)
    outer = lax.ppermute(outer, flat, across)

    side_tiles = pl.pallas_call(
        block_pack,
        out_shape=shape(2, LANES, LANES),
        in_specs=[scalar] + [vmem] * 2,
        out_specs=vmem,
        compiler_params=params,
        name="block_pack",
    )(group, seam, outer)
    tiles = tile // LANES
    tall = rows + 2 * SUBS
    tables = (shape(layers, tiles + 2, tall, LANES), shape(tiles + 2, tall, LANES))
    anywhere = pl.BlockSpec(memory_space=pl.ANY)
    far_a, far_b, x_a, x_b = pl.pallas_call(
        lazy_pack,
        out_shape=(shape(SUBS, tile + tile // SUBS),) * 2 + (shape(SUBS, LANES),) * 2,
        grid=(1,),
        in_specs=[
            scalar,
            scalar,
            block((layers, SUBS, tile), 0, 0, 0),
            block((layers, SUBS, tile), 0, last_row, 0),
            block((layers, rows, LANES), 0, 0, 0),
            block((layers, rows, LANES), 0, 0, last_tile),
            block((SUBS, tile), 0, 0),
            block((SUBS, tile), last_row, 0),
            block((rows, LANES), 0, 0),
            block((rows, LANES), 0, last_tile),
        ],
        out_specs=[whole(SUBS, tile + tile // SUBS)] * 2 + [whole(SUBS, LANES)] * 2,
        compiler_params=params,
        name="lazy_pack",
    )(odd_x, odd_y, *(pltpu.with_memory_space_constraint(interior_potential, pltpu.HBM),) * 4, *(seabed,) * 4)

    wide = width + 2 * LANES
    packed = wide + pl.cdiv((2 * REACH - SUBS) * (wide // LANES), SUBS) * LANES
    row_a, row_b = pl.pallas_call(
        row_pack,
        out_shape=(shape(SUBS, packed),) * 2,
        grid=(1,),
        in_specs=[
            scalar,
            scalar,
            block((SUBS, width), 0, 0),
            block((SUBS, width), last_row, 0),
            block((SUBS, width), 0, 0),
            block((SUBS, width), last_row, 0),
            whole(SUBS, LANES),
            whole(SUBS, LANES),
        ],
        out_specs=[whole(SUBS, packed)] * 2,
        compiler_params=params,
        name="row_pack",
    )(group, odd_x, elevation, elevation, surface_potential, surface_potential, seam, outer)
    sides = {}
    for name, value, axis, shifted in (
        ("row_b", row_b, "gx", True), ("row_a", row_a, "gx", False), ("x_b", x_b, "gy", True),
        ("x_a", x_a, "gy", False), ("far_b", far_b, "gx", True), ("far_a", far_a, "gx", False),
    ):
        sides[name] = lax.ppermute(value, axis, couples(axis, shifted))

    tiles = tile // LANES
    tall = rows + 2 * SUBS
    anywhere = pl.BlockSpec(memory_space=pl.ANY)
    tables = (shape(layers, tiles + 2, tall, LANES), shape(tiles + 2, tall, LANES))
    deep = rows + 3 * SUBS
    padded = (width // LANES + 2, deep, LANES)
    new_e, new_p, height, wide_e, wide_p, volume, depth = pl.pallas_call(
        surface,
        out_shape=(shape(rows, width),) * 2 + (shape(rows + SUBS, width),) + (shape(*padded),) * 2 + tables,
        in_specs=[scalar] + [vmem] * 3 + [scalar] + [vmem] * 2 + [hbm, vmem],
        out_specs=[vmem] * 7,
        scratch_shapes=[pltpu.VMEM(padded, f32)] * 4 + [pltpu.SemaphoreType.DMA((tiles,))],
        compiler_params=params,
        name="surface",
    )(
        odd_x, elevation, surface_potential, side_tiles, group, sides["row_a"], sides["row_b"],
        pltpu.with_memory_space_constraint(interior_potential, pltpu.HBM), seabed,
    )
    far_sides = [sides[name] for name in ("far_a", "far_b", "x_a", "x_b")]
    rims = pl.pallas_call(
        rim_pack,
        out_shape=shape(SUBS, width),
        in_specs=[scalar] * 3 + [vmem] * 4 + [anywhere],
        out_specs=vmem,
        compiler_params=params,
        name="rim_pack",
    )(group, odd_x, odd_y, *far_sides, height)
    far_rims = lax.ppermute(rims, flat, partner)
    far_height = lax.ppermute(height, flat, partner)
    other_p = lax.ppermute(new_p, flat, partner)
    volume, depth = pl.pallas_call(
        fill,
        out_shape=tables,
        in_specs=[scalar] * 2 + [anywhere] * 2 + [vmem] * 4,
        out_specs=[anywhere] * 2,
        scratch_shapes=[
            pltpu.VMEM((2, layers, rows, LANES), f32),
            pltpu.VMEM((2, rows, LANES), f32),
            pltpu.VMEM((2, layers, tiles, SUBS, LANES), f32),
            pltpu.VMEM((2, tiles, SUBS, LANES), f32),
            pltpu.SemaphoreType.DMA((8,)),
        ],
        input_output_aliases={2: 0, 3: 1},
        compiler_params=params,
        name="fill",
    )(odd_x, odd_y, volume, depth, *far_sides)
    blocks = rows // SUBS
    tables = (volume, depth, far_layer, far_rims, wide_e)
    ghost = pltpu.VMEM((width // LANES + 2, tall, LANES), f32)
    partial = pl.pallas_call(
        functools.partial(own_half, total_layers),
        out_shape=shape(layers, rows, tile),
        grid_spec=pltpu.PrefetchScalarGridSpec(
            num_scalar_prefetch=1,
            grid=(blocks,),
            in_specs=[vmem] * 6,
            out_specs=pl.BlockSpec((layers, SUBS, width), lambda i, g: (0, i, g[0])),
            scratch_shapes=[ghost],
        ),
        compiler_params=params,
        name="own_half",
    )(group, *tables, wide_p)
    partial, part, coefficients = pl.pallas_call(
        functools.partial(other_half, total_layers),
        out_shape=(shape(layers, rows, tile), shape(rows, width), shape(3, rows, width)),
        grid_spec=pltpu.PrefetchScalarGridSpec(
            num_scalar_prefetch=1,
            grid=(blocks,),
            in_specs=[hbm] + [vmem] * 6,
            out_specs=[
                pl.BlockSpec((layers, SUBS, width), lambda i, g: (0, i, 1 - g[0])),
                pl.BlockSpec((SUBS, width), lambda i, g: (i, 0)),
                pl.BlockSpec((3, SUBS, width), lambda i, g: (0, i, 0)),
            ],
            scratch_shapes=[ghost] * 2,
        ),
        input_output_aliases={1: 0},
        compiler_params=params,
        name="other_half",
    )(group, partial, *tables, far_height)
    result = pl.pallas_call(
        top,
        out_shape=shape(layers, rows, tile),
        grid_spec=pltpu.PrefetchScalarGridSpec(
            num_scalar_prefetch=1,
            grid=(1,),
            in_specs=[hbm] + [vmem] * 5,
            out_specs=pl.BlockSpec((1, rows, width), lambda i, g: (layers - 1, 0, 1 - g[0])),
            scratch_shapes=[pltpu.VMEM((width // LANES + 2, tall, LANES), f32)],
        ),
        input_output_aliases={1: 0},
        compiler_params=params,
        name="top",
    )(group, partial, part, coefficients, far_height, wide_p, other_p)
    return new_e, new_p, result


def solution(mesh):
    return jax.shard_map(
        shards,
        mesh=mesh,
        in_specs=(P("gx", ("gy", "gz")), P("gx", ("gy", "gz")), P("gx", "gy"), P("gz", "gx", "gy")),
        out_specs=(P("gx", ("gy", "gz")), P("gx", ("gy", "gz")), P("gz", "gx", "gy")),
        check_vma=False,
    )
```

```python
import functools

import jax
import jax.numpy as jnp
from jax import lax
from jax.experimental import pallas as pl
from jax.experimental.pallas import tpu as pltpu
from jax.sharding import PartitionSpec as P

time_step = 0.05
depth_unit = 0.015625
LANES = 128
SUBS = 8


def shift_lanes(left, cur, right, step):
    lane = lax.broadcasted_iota(jnp.int32, cur.shape, 1)
    if step < 0:
        return pltpu.roll(jnp.where(lane >= LANES + step, left, cur), -step, 1)
    return pltpu.roll(jnp.where(lane < step, right, cur), LANES - step, 1)


def square(tile, at_end):
    rest = jnp.zeros((LANES - tile.shape[0], LANES), tile.dtype)
    return jnp.concatenate([rest, tile] if at_end else [tile, rest], 0)


def first_pack(group, e, p, v, seam, outer, layer, v_top, v_bottom, v_left, v_right, edges, sems):
    rows, width = e.shape
    low = group[0] == 0
    source = jnp.where(low, v.shape[0] - 1, 0)
    whole = pltpu.make_async_copy(v.at[source], layer, sems.at[4])
    copies = []
    for index, (field, start) in enumerate(((e, 0), (p, 0), (e, width - LANES), (p, width - LANES))):
        into = edges.at[index // 2, (index % 2) * rows : (index % 2 + 1) * rows, :]
        copies.append(pltpu.make_async_copy(field.at[:, start : start + LANES], into, sems.at[index]))
    tile = v.shape[2]
    ends = [
        pltpu.make_async_copy(source, into, sems.at[5 + index])
        for index, (source, into) in enumerate(
            (
                (v.at[:, :SUBS, :], v_top),
                (v.at[:, rows - SUBS :, :], v_bottom),
                (v.at[:, :, :LANES], v_left),
                (v.at[:, :, tile - LANES :], v_right),
            )
        )
    ]
    for copy in copies:
        copy.start()
    whole.start()
    for copy in ends:
        copy.start()
    for copy in copies:
        copy.wait()
    left = edges[0].T[:SUBS]
    right = edges[1].T[LANES - SUBS :]
    seam[...] = jnp.where(low, right, left)
    outer[...] = jnp.where(low, left, right)
    whole.wait()
    for copy in ends:
        copy.wait()


def by_parity(odd, fill, first, second):
    @pl.when(odd[0] == 0)
    def _():
        fill(first, second)

    @pl.when(odd[0] == 1)
    def _():
        fill(second, first)


def lazy_pack(
    odd_x, odd_y, v_top, v_bottom, v_left, v_right, s_top, s_bottom, s_left, s_right, row_a, row_b, column_a, column_b
):
    by_parity(odd_x, functools.partial(pack_rows, v_top, v_bottom, s_top, s_bottom), row_a, row_b)
    by_parity(odd_y, functools.partial(pack_columns, v_left, v_right, s_left, s_right), column_a, column_b)


def pack_rows(v_top, v_bottom, s_top, s_bottom, up, down):
    layers, _, width = v_top.shape
    piece = width // SUBS
    for k in range(layers):
        up[k : k + 1, :width] = v_bottom[k, SUBS - 1 : SUBS, :]
        down[k : k + 1, :width] = v_top[k, 0:1, :]
    for q in range(SUBS):
        part = slice(q * piece, (q + 1) * piece)
        up[q : q + 1, width:] = s_bottom[SUBS - 1 : SUBS, part].astype(jnp.float32) * depth_unit
        down[q : q + 1, width:] = s_top[0:1, part].astype(jnp.float32) * depth_unit


def pack_columns(v_left, v_right, s_left, s_right, to_right, to_left):
    layers = v_left.shape[0]
    to_right[...] = jnp.zeros_like(to_right)
    to_left[...] = jnp.zeros_like(to_left)
    for j in range(layers // 2):
        both = jnp.concatenate([v_right[2 * j], v_right[2 * j + 1]], 0).T
        to_right[j : j + 1, :] = both[LANES - 1 :]
        both = jnp.concatenate([v_left[2 * j], v_left[2 * j + 1]], 0).T
        to_left[j : j + 1, :] = both[:1]
    j = layers // 2
    both = jnp.concatenate([s_right[...], s_right[...]], 0).astype(jnp.float32) * depth_unit
    to_right[j : j + 1, :] = both.T[LANES - 1 :]
    both = jnp.concatenate([s_left[...], s_left[...]], 0).astype(jnp.float32) * depth_unit
    to_left[j : j + 1, :] = both.T[:1]


def side_blocks(low, seam, outer):
    left = square(jnp.where(low, outer, seam), True).T
    right = square(jnp.where(low, seam, outer), False).T
    return left, right


def block_pack(group, seam, outer, blocks):
    blocks[0], blocks[1] = side_blocks(group[0] == 0, seam[...], outer[...])


def row_pack(group, odd_x, e_top, e_bottom, p_top, p_bottom, seam, outer, row_a, row_b):
    left, right = side_blocks(group[0] == 0, seam[...], outer[...])
    by_parity(odd_x, functools.partial(pack_surface_rows, left, right, e_top, e_bottom, p_top, p_bottom), row_a, row_b)


REACH = 5


def spare_piece(index, tiles):
    start = (tiles + index // SUBS) * LANES
    return slice(index % SUBS, index % SUBS + 1), slice(start, start + LANES)


def pack_surface_rows(left, right, e_top, e_bottom, p_top, p_bottom, up, down):
    rows = LANES // 2
    tiles = e_top.shape[1] // LANES + 2
    fit = SUBS - REACH
    for into, first, e_rows, p_rows in ((up, rows - REACH, e_bottom, p_bottom), (down, 0, e_top, p_top)):
        start = first % SUBS
        for t in range(tiles):
            part = slice(t * LANES, (t + 1) * LANES)
            if 0 < t < tiles - 1:
                own = slice((t - 1) * LANES, t * LANES)
                e_part = e_rows[start : start + REACH, own]
                p_part = p_rows[start : start + REACH, own]
            else:
                side = left if t == 0 else right
                e_part = side[first : first + REACH]
                p_part = side[rows + first : rows + first + REACH]
            into[:REACH, part] = e_part
            into[REACH:, part] = p_part[:fit]
            for extra in range(REACH - fit):
                row, lanes = spare_piece(extra * tiles + t, tiles)
                into[row, lanes] = p_part[fit + extra : fit + extra + 1]


def neighbourhood(ref, lane_tile, row):
    last = ref.shape[0] - 1
    at = lambda column, step: ref[column, pl.ds(row + step, SUBS), :]
    cur = at(lane_tile, 0)
    left, right = at(max(lane_tile - 1, 0), 0), at(min(lane_tile + 1, last), 0)
    rows = [at(lane_tile, step) for step in (-2, -1, 1, 2)]
    lanes = [shift_lanes(left, cur, right, step) for step in (-2, -1, 1, 2)]
    return cur, rows, lanes


def slope(values):
    return (2.0 / 3.0) * (values[2] - values[1]) - (1.0 / 12.0) * (values[3] - values[0])


def tile_rates(e_near, p_near):
    e, e_rows, e_lanes = e_near
    p, p_rows, p_lanes = p_near
    p_x, p_y = slope(p_rows), slope(p_lanes)
    near = (p_rows[1] + p_rows[2]) + (p_lanes[1] + p_lanes[2])
    far = (p_rows[0] + p_rows[3]) + (p_lanes[0] + p_lanes[3])
    bend = (4.0 / 3.0) * near - (1.0 / 12.0) * far - 5.0 * p
    rate_e = bend - (slope(e_rows) * p_x + slope(e_lanes) * p_y)
    rate_p = 0.5 * (p_x * p_x + p_y * p_y) + e
    return e, p, time_step * rate_e, -time_step * rate_p


def surface(
    odd_x, e, p, side_tiles, group, row_a, row_b, v, sea,
    new_e, new_p, wide_e, wide_p, volume, depth, e0, p0, e1, p1, sems,
):
    rows, width = e.shape
    left, right = side_tiles[0], side_tiles[1]
    copies = []
    for t in range(v.shape[2] // LANES):
        part = slice(t * LANES, (t + 1) * LANES)
        into = volume.at[:, t + 1, SUBS : SUBS + rows, :]
        copies.append(pltpu.make_async_copy(v.at[:, :, part], into, sems.at[t]))
        copies[-1].start()
    tiles = width // LANES + 2
    inner = slice(SUBS, SUBS + rows)
    fields = ((e0, e, 0), (p0, p, LANES // 2))
    fit = SUBS - REACH

    def ends(south, north):
        for source, first in ((north, SUBS - REACH), (south, SUBS + rows)):
            for t in range(tiles):
                part = slice(t * LANES, (t + 1) * LANES)
                e0[t, first : first + REACH, :] = source[:REACH, part]
                p0[t, first : first + fit, :] = source[REACH:, part]
                for extra in range(REACH - fit):
                    row = first + fit + extra
                    p0[t, row : row + 1, :] = source[spare_piece(extra * tiles + t, tiles)]

    by_parity(odd_x, ends, row_a, row_b)
    for old, source, base in fields:
        for t in range(1, tiles - 1):
            old[t, inner, :] = source[:, (t - 1) * LANES : t * LANES]
        old[0, inner, :] = left[base : base + rows]
        old[tiles - 1, inner, :] = right[base : base + rows]
    blocks = rows // SUBS + 1

    def first(block, carry):
        row = block * SUBS + SUBS - 3
        for t in range(tiles):
            old_e, old_p, step_e, step_p = tile_rates(neighbourhood(e0, t, row), neighbourhood(p0, t, row))
            e1[t, pl.ds(row, SUBS), :] = old_e + step_e
            p1[t, pl.ds(row, SUBS), :] = old_p + step_p
        return carry

    lax.fori_loop(0, blocks, first, 0, unroll=True)

    def second(block, carry):
        row = block * SUBS + SUBS - 1
        for t in range(tiles):
            one_e, one_p, step_e, step_p = tile_rates(neighbourhood(e1, t, row), neighbourhood(p1, t, row))
            old_e = e0[t, pl.ds(row, SUBS), :]
            old_p = p0[t, pl.ds(row, SUBS), :]
            wide_e[t, pl.ds(row, SUBS), :] = 0.5 * ((old_e + one_e) + step_e)
            wide_p[t, pl.ds(row, SUBS), :] = 0.5 * ((old_p + one_p) + step_p)
        return carry

    lax.fori_loop(0, blocks, second, 0, unroll=True)
    for t in range(1, tiles - 1):
        part = slice((t - 1) * LANES, t * LANES)
        new_e[:, part] = wide_e[t, inner, :]
        new_p[:, part] = wide_p[t, inner, :]
    for t in range(v.shape[2] // LANES):
        depth[t + 1, inner, :] = sea[:, t * LANES : (t + 1) * LANES].astype(jnp.float32) * depth_unit
    for copy in copies:
        copy.wait()


def rim_pack(group, odd_x, odd_y, far_a, far_b, x_a, x_b, wide_e, wide_p, rims):
    low = group[0] == 0
    layers = far_a.shape[0]
    width = rims.shape[1] - LANES
    pairs = layers // 2
    last = width // LANES + 1
    half_lanes = LANES // 2
    inner = slice(SUBS, SUBS + half_lanes)
    rims[:, width:] = jnp.zeros((SUBS, LANES), jnp.float32)
    for row, wide in ((4, wide_e), (6, wide_p)):
        for t in range(1, last):
            part = slice((t - 1) * LANES, t * LANES)
            rims[row : row + 1, part] = wide[t, SUBS - 1 : SUBS, :]
            rims[row + 1 : row + 2, part] = wide[t, SUBS + half_lanes : SUBS + half_lanes + 1, :]
    left = jnp.concatenate([wide_e[0, inner, :], wide_p[0, inner, :]], 0).T[LANES - 1 :]
    right = jnp.concatenate([wide_e[last, inner, :], wide_p[last, inner, :]], 0).T[:1]
    rims[2:3, width:] = jnp.where(low, left, right)

    def rows(far_south, far_north):
        for row, side in ((0, far_north), (2, far_south)):
            for half in range(2):
                part = slice(half * width, (half + 1) * width)
                rims[row + half : row + half + 1, :width] = jnp.where(low, side[layers - 1 : layers, part], side[0:1, part])

    by_parity(odd_x, rows, far_a, far_b)

    def columns(x_right, x_left):
        for row, side in ((0, x_left), (1, x_right)):
            top_pair = pltpu.roll(side[...], LANES // 2, 1)[pairs - 1 : pairs]
            rims[row : row + 1, width:] = jnp.where(low, top_pair, side[0:1, :])

    by_parity(odd_y, columns, x_a, x_b)


def fill(
    odd_x, odd_y, old_volume, old_depth, far_a, far_b, x_a, x_b, volume, depth, sides, depths, edges, ends, sems
):
    del old_volume, old_depth
    layers, tiles, tall = volume.shape[0], volume.shape[1], volume.shape[2]
    rows, tile = tall - 2 * SUBS, (tiles - 2) * LANES
    inner = slice(SUBS, SUBS + rows)
    even = odd_y[0] == 0
    left = square(jnp.where(even, x_b[...], x_a[...]), False).T
    right = square(jnp.where(even, x_a[...], x_b[...]), False).T
    half, pairs = LANES // 2, layers // 2
    for k in range(layers):
        base = (k % 2) * half
        sides[0, k] = pltpu.roll(left, LANES - 1 - k // 2, 1)[base : base + rows]
        sides[1, k] = pltpu.roll(right, (LANES - k // 2) % LANES, 1)[base : base + rows]
    depths[0] = pltpu.roll(left, LANES - 1 - pairs, 1)[:rows]
    depths[1] = pltpu.roll(right, LANES - pairs, 1)[:rows]
    piece = tile // SUBS // LANES

    def fill_ends(far_south, far_north):
        for end, source, row in ((0, far_north, SUBS - 1), (1, far_south, 0)):
            for t in range(tiles - 2):
                for k in range(layers):
                    edges[end, k, t, row : row + 1, :] = source[k : k + 1, t * LANES : (t + 1) * LANES]
                q, start = t // piece, tile + (t % piece) * LANES
                ends[end, t, row : row + 1, :] = source[q : q + 1, start : start + LANES]

    by_parity(odd_x, fill_ends, far_a, far_b)
    copies = []
    for index, (t, at) in enumerate(((0, slice(0, SUBS)), (tiles - 1, slice(tall - SUBS, tall)))):
        for source, target in (
            (sides.at[index], volume.at[:, t, inner, :]),
            (depths.at[index], depth.at[t, inner, :]),
            (edges.at[index], volume.at[:, 1 : tiles - 1, at, :]),
            (ends.at[index], depth.at[1 : tiles - 1, at, :]),
        ):
            copies.append(pltpu.make_async_copy(source, target, sems.at[len(copies)]))
    for copy in copies:
        copy.start()
    for copy in copies:
        copy.wait()


def apply_tile(total_layers, group, block, volume, depth, t, heights, local, ghost, spot, mine, write, rest=None):
    low = group == 0
    layers = volume.shape[0]
    spacing = 1.0 / total_layers
    sigma = (group * layers).astype(jnp.float32) * spacing + 0.5 * spacing
    gain = (2 * group).astype(jnp.float32)
    here = pl.multiple_of((block + 1) * SUBS, SUBS)

    def near(ref, t):
        at = lambda column, step: ref[column, pl.ds(here + step, SUBS), :]
        cur = at(t, 0)
        left, right = at(t - 1, 0), at(t + 1, 0)
        return cur, at(t, -1), at(t, 1), shift_lanes(left, cur, right, -1), shift_lanes(left, cur, right, 1)

    def differences(ref, t):
        p, up, down, left, right = near(ref, t)
        return p, down - up, right - left

    d, d_x, d_y = differences(depth, t)
    h, h_x, h_y = differences(heights, local)
    inverse = 1.0 / (d + h)
    scale = (0.25 / spacing) * inverse
    bx, by = scale * (d_x + h_x), scale * (d_y + h_y)
    ux, uy = scale * d_x - sigma * bx, scale * d_y - sigma * by
    bx, by = spacing * bx, spacing * by
    scaled = inverse * (1.0 / spacing)
    weight = 4.0 * (ux * ux + uy * uy) + scaled * scaled
    bend = 4.0 * (bx * bx + by * by)
    step = bend - 8.0 * (ux * bx + uy * by)
    bend = bend + bend

    def level(k):
        p, up, down, left, right = near(volume.at[k], t)
        return p, down - up, right - left, ((down + up) + (right + left)) - 4.0 * p

    far = differences(ghost, spot)
    this = level(0)
    lower = [jnp.where(low, a, b) for a, b in zip(this, far)]
    rise_below = this[0] - lower[0]
    for k in range(layers):
        if k < layers - 1:
            upper = level(k + 1)
        else:
            upper = [jnp.where(low, a, -b) for a, b in zip(far, this)]
            if mine is not None:
                upper = [a + gain * b for a, b in zip(upper, differences(mine, local))]
        rise = upper[0] - this[0]
        value = this[3] + ux * (upper[1] - lower[1]) + uy * (upper[2] - lower[2])
        value = value + weight * (rise - rise_below)
        write(k, value)
        if k < layers - 1:
            ux, uy = ux - bx, uy - by
            weight, step = weight + step, step + bend
        elif rest is not None:
            rest(value, ux, uy, weight)
        lower, this, rise_below = this, upper, rise


def own_half(total_layers, group_ref, volume, depth, far_layer, rims, wide_e, wide_p, out, ghost):
    block = pl.program_id(0)
    group = group_ref[0]
    halves = volume.shape[1] // 2 - 1

    @pl.when(block == 0)
    def _():
        fill_ghost(group == 0, group, far_layer, rims, ghost)

    for local in range(1, halves + 1):

        def write(k, value):
            out[k, :, (local - 1) * LANES : local * LANES] = value

        apply_tile(
            total_layers, group, block, volume, depth, group * halves + local, wide_e, local, ghost, local, wide_p,
            write,
        )


def other_half(
    total_layers, group_ref, before, volume, depth, far_layer, rims, wide_e, height,
    out, part, coefficients, ghost, other_e,
):
    del before
    block = pl.program_id(0)
    group = group_ref[0]
    low = group == 0
    rows, width = other_e.shape[1] - 2 * SUBS, height.shape[1]
    halves = width // LANES
    inner = slice(SUBS, SUBS + rows)

    @pl.when(block == 0)
    def _():
        fill_ghost(group == 1, 1 - group, far_layer, rims, ghost)
        for t in range(halves):
            spot = slice(t * LANES, (t + 1) * LANES)
            other_e[t + 1, inner, :] = height[:, spot]
            other_e[t + 1, SUBS - 1 : SUBS, :] = rims[4:5, spot]
            other_e[t + 1, SUBS + rows : SUBS + rows + 1, :] = rims[5:6, spot]
        edge = square(rims[:, width:], False).T[:rows]
        at_right, at_left = pltpu.roll(edge, LANES - 2, 1), pltpu.roll(edge, LANES - 3, 1)
        other_e[0, inner, :] = jnp.where(low, wide_e[halves, inner, :], at_left)
        other_e[halves + 1, inner, :] = jnp.where(low, at_right, wide_e[1, inner, :])

    for local in range(1, halves + 1):
        spot = slice((local - 1) * LANES, local * LANES)

        def write(k, value):
            out[k, :, spot] = value

        def rest(value, ux, uy, weight):
            part[:, spot] = value
            coefficients[0, :, spot] = ux
            coefficients[1, :, spot] = uy
            coefficients[2, :, spot] = weight

        apply_tile(
            total_layers, group, block, volume, depth, (1 - group) * halves + local, other_e, local, ghost, local,
            None, write, rest,
        )


def fill_ghost(first, half, far_layer, rims, ghost):
    rows, tile = far_layer.shape
    width = tile // 2
    halves = width // LANES
    inner = slice(SUBS, SUBS + rows)
    side = pltpu.roll(square(rims[:, width:], False).T, LANES - 1, 1)[:rows]
    ghost[0, inner, :] = jnp.where(first, side, far_layer[:, width - LANES : width])
    ghost[halves + 1, inner, :] = jnp.where(first, far_layer[:, width : width + LANES], side)
    for t in range(halves):
        spot = slice(t * LANES, (t + 1) * LANES)
        lanes = pl.ds(pl.multiple_of(half * width + t * LANES, LANES), LANES)
        ghost[t + 1, inner, :] = far_layer[:, lanes]
        ghost[t + 1, SUBS - 1 : SUBS, :] = jnp.where(first, rims[0:1, spot], rims[1:2, spot])
        ghost[t + 1, SUBS + rows : SUBS + rows + 1, :] = jnp.where(first, rims[2:3, spot], rims[3:4, spot])


def top(group_ref, before, part, coefficients, rims, wide_p, other_p, out, potential):
    del before
    low = group_ref[0] == 0
    rows, width = other_p.shape
    halves = width // LANES
    inner = slice(SUBS, SUBS + rows)
    edge = square(rims[:, width:], False).T[LANES // 2 : LANES // 2 + rows]
    potential[0, inner, :] = pltpu.roll(edge, LANES - 3, 1)
    potential[halves + 1, inner, :] = wide_p[1, inner, :]
    for t in range(halves):
        spot = slice(t * LANES, (t + 1) * LANES)
        potential[t + 1, inner, :] = other_p[:, spot]
        potential[t + 1, SUBS - 1 : SUBS, :] = rims[6:7, spot]
        potential[t + 1, SUBS + rows : SUBS + rows + 1, :] = rims[7:8, spot]

    def body(block, carry):
        here = pl.multiple_of((block + 1) * SUBS, SUBS)
        to = pl.ds(pl.multiple_of(block * SUBS, SUBS), SUBS)
        for t in range(1, halves + 1):
            at = lambda column, step: potential[column, pl.ds(here + step, SUBS), :]
            cur, left, right = at(t, 0), at(t - 1, 0), at(t + 1, 0)
            east = shift_lanes(left, cur, right, 1) - shift_lanes(left, cur, right, -1)
            spot = slice((t - 1) * LANES, t * LANES)
            value = coefficients[0, to, spot] * (at(t, 1) - at(t, -1)) + coefficients[1, to, spot] * east
            value = value + coefficients[2, to, spot] * cur
            partial = part[to, spot]
            out[0, to, spot] = jnp.where(low, partial, partial + 2.0 * value)
        return carry

    lax.fori_loop(0, rows // SUBS, body, 0, unroll=True)


def couples(axis, shifted):
    count = lax.axis_size(axis)
    start = 1 if shifted else 0
    one_way = [((i + start) % count, (i + start + 1) % count) for i in range(0, count, 2)]
    return one_way + [(b, a) for a, b in one_way]


def shards(elevation, surface_potential, seabed, interior_potential):
    rows, width = elevation.shape
    layers, _, tile = interior_potential.shape
    assert 2 * rows == LANES and tile == 2 * width and layers == SUBS
    assert lax.axis_size("gz") == 2
    total_layers = layers * lax.axis_size("gz")
    f32 = jnp.float32
    shape = lambda *dims: jax.ShapeDtypeStruct(dims, f32)
    whole = lambda *dims: pl.BlockSpec(dims, lambda *_: (0,) * len(dims))
    group = lax.axis_index("gz").astype(jnp.int32).reshape((1,))
    odd_x = (lax.axis_index("gx") & 1).astype(jnp.int32).reshape((1,))
    odd_y = (lax.axis_index("gy") & 1).astype(jnp.int32).reshape((1,))
    assert lax.axis_size("gx") % 2 == 0 and lax.axis_size("gy") % 2 == 0
    scalar = pl.BlockSpec(memory_space=pltpu.SMEM)
    last_row, last_tile = rows // SUBS - 1, tile // LANES - 1

    def block(dims, *index):
        return pl.BlockSpec(dims, lambda *_: index)

    params = pltpu.CompilerParams(vmem_limit_bytes=24 * 1024 * 1024)
    vmem = pl.BlockSpec(memory_space=pltpu.VMEM)
    hbm = pl.BlockSpec(memory_space=pltpu.HBM)
    seam, outer, layer, *ends = pl.pallas_call(
        first_pack,
        out_shape=(shape(SUBS, LANES), shape(SUBS, LANES), shape(rows, tile))
        + (shape(layers, SUBS, tile),) * 2
        + (shape(layers, rows, LANES),) * 2,
        in_specs=[scalar, hbm, hbm, hbm],
        out_specs=[vmem] * 7,
        scratch_shapes=[pltpu.VMEM((2, LANES, LANES), f32), pltpu.SemaphoreType.DMA((9,))],
        compiler_params=params,
        name="first_pack",
    )(group, *(pltpu.with_memory_space_constraint(x, pltpu.HBM) for x in (elevation, surface_potential, interior_potential)))

    flat = ("gy", "gz")
    count = lax.axis_size("gy")
    partner = [(2 * i + g, 2 * i + 1 - g) for i in range(count) for g in range(2)]
    across = [(2 * i + 1, (2 * i + 2) % (2 * count)) for i in range(count)]
    across = across + [(b, a) for a, b in across]
    seam = lax.ppermute(seam, flat, partner)
    far_layer = lax.ppermute(layer, flat, partner)
    outer = lax.ppermute(outer, flat, across)

    side_tiles = pl.pallas_call(
        block_pack,
        out_shape=shape(2, LANES, LANES),
        in_specs=[scalar] + [vmem] * 2,
        out_specs=vmem,
        compiler_params=params,
        name="block_pack",
    )(group, seam, outer)
    tiles = tile // LANES
    tall = rows + 2 * SUBS
    tables = (shape(layers, tiles + 2, tall, LANES), shape(tiles + 2, tall, LANES))
    anywhere = pl.BlockSpec(memory_space=pl.ANY)
    far_a, far_b, x_a, x_b = pl.pallas_call(
        lazy_pack,
        out_shape=(shape(SUBS, tile + tile // SUBS),) * 2 + (shape(SUBS, LANES),) * 2,
        grid=(1,),
        in_specs=[
            scalar,
            scalar,
            *[vmem] * 4,
            block((SUBS, tile), 0, 0),
            block((SUBS, tile), last_row, 0),
            block((rows, LANES), 0, 0),
            block((rows, LANES), 0, last_tile),
        ],
        out_specs=[whole(SUBS, tile + tile // SUBS)] * 2 + [whole(SUBS, LANES)] * 2,
        compiler_params=params,
        name="lazy_pack",
    )(odd_x, odd_y, *ends, *(seabed,) * 4)

    wide = width + 2 * LANES
    packed = wide + pl.cdiv((2 * REACH - SUBS) * (wide // LANES), SUBS) * LANES
    row_a, row_b = pl.pallas_call(
        row_pack,
        out_shape=(shape(SUBS, packed),) * 2,
        grid=(1,),
        in_specs=[
            scalar,
            scalar,
            block((SUBS, width), 0, 0),
            block((SUBS, width), last_row, 0),
            block((SUBS, width), 0, 0),
            block((SUBS, width), last_row, 0),
            whole(SUBS, LANES),
            whole(SUBS, LANES),
        ],
        out_specs=[whole(SUBS, packed)] * 2,
        compiler_params=params,
        name="row_pack",
    )(group, odd_x, elevation, elevation, surface_potential, surface_potential, seam, outer)
    sides = {}
    for name, value, axis, shifted in (
        ("row_b", row_b, "gx", True), ("row_a", row_a, "gx", False), ("x_b", x_b, "gy", True),
        ("x_a", x_a, "gy", False), ("far_b", far_b, "gx", True), ("far_a", far_a, "gx", False),
    ):
        sides[name] = lax.ppermute(value, axis, couples(axis, shifted))

    tiles = tile // LANES
    tall = rows + 2 * SUBS
    anywhere = pl.BlockSpec(memory_space=pl.ANY)
    tables = (shape(layers, tiles + 2, tall, LANES), shape(tiles + 2, tall, LANES))
    deep = rows + 3 * SUBS
    padded = (width // LANES + 2, deep, LANES)
    new_e, new_p, wide_e, wide_p, volume, depth = pl.pallas_call(
        surface,
        out_shape=(shape(rows, width),) * 2 + (shape(*padded),) * 2 + tables,
        in_specs=[scalar] + [vmem] * 3 + [scalar] + [vmem] * 2 + [hbm, vmem],
        out_specs=[vmem] * 6,
        scratch_shapes=[pltpu.VMEM(padded, f32)] * 4 + [pltpu.SemaphoreType.DMA((tiles,))],
        compiler_params=params,
        name="surface",
    )(
        odd_x, elevation, surface_potential, side_tiles, group, sides["row_a"], sides["row_b"],
        pltpu.with_memory_space_constraint(interior_potential, pltpu.HBM), seabed,
    )
    far_sides = [sides[name] for name in ("far_a", "far_b", "x_a", "x_b")]
    rims = pl.pallas_call(
        rim_pack,
        out_shape=shape(SUBS, width + LANES),
        in_specs=[scalar] * 3 + [vmem] * 6,
        out_specs=vmem,
        compiler_params=params,
        name="rim_pack",
    )(group, odd_x, odd_y, *far_sides, wide_e, wide_p)
    far_rims = lax.ppermute(rims, flat, partner)
    far_height = lax.ppermute(new_e, flat, partner)
    other_p = lax.ppermute(new_p, flat, partner)
    volume, depth = pl.pallas_call(
        fill,
        out_shape=tables,
        in_specs=[scalar] * 2 + [anywhere] * 2 + [vmem] * 4,
        out_specs=[anywhere] * 2,
        scratch_shapes=[
            pltpu.VMEM((2, layers, rows, LANES), f32),
            pltpu.VMEM((2, rows, LANES), f32),
            pltpu.VMEM((2, layers, tiles, SUBS, LANES), f32),
            pltpu.VMEM((2, tiles, SUBS, LANES), f32),
            pltpu.SemaphoreType.DMA((8,)),
        ],
        input_output_aliases={2: 0, 3: 1},
        compiler_params=params,
        name="fill",
    )(odd_x, odd_y, volume, depth, *far_sides)
    blocks = rows // SUBS
    tables = (volume, depth, far_layer, far_rims, wide_e)
    ghost = pltpu.VMEM((width // LANES + 2, tall, LANES), f32)
    partial = pl.pallas_call(
        functools.partial(own_half, total_layers),
        out_shape=shape(layers, rows, tile),
        grid_spec=pltpu.PrefetchScalarGridSpec(
            num_scalar_prefetch=1,
            grid=(blocks,),
            in_specs=[vmem] * 6,
            out_specs=pl.BlockSpec((layers, SUBS, width), lambda i, g: (0, i, g[0])),
            scratch_shapes=[ghost],
        ),
        compiler_params=params,
        name="own_half",
    )(group, *tables, wide_p)
    partial, part, coefficients = pl.pallas_call(
        functools.partial(other_half, total_layers),
        out_shape=(shape(layers, rows, tile), shape(rows, width), shape(3, rows, width)),
        grid_spec=pltpu.PrefetchScalarGridSpec(
            num_scalar_prefetch=1,
            grid=(blocks,),
            in_specs=[hbm] + [vmem] * 6,
            out_specs=[
                pl.BlockSpec((layers, SUBS, width), lambda i, g: (0, i, 1 - g[0])),
                pl.BlockSpec((SUBS, width), lambda i, g: (i, 0)),
                pl.BlockSpec((3, SUBS, width), lambda i, g: (0, i, 0)),
            ],
            scratch_shapes=[ghost] * 2,
        ),
        input_output_aliases={1: 0},
        compiler_params=params,
        name="other_half",
    )(group, partial, *tables, far_height)
    result = pl.pallas_call(
        top,
        out_shape=shape(layers, rows, tile),
        grid_spec=pltpu.PrefetchScalarGridSpec(
            num_scalar_prefetch=1,
            grid=(1,),
            in_specs=[hbm] + [vmem] * 5,
            out_specs=pl.BlockSpec((1, rows, width), lambda i, g: (layers - 1, 0, 1 - g[0])),
            scratch_shapes=[pltpu.VMEM((width // LANES + 2, tall, LANES), f32)],
        ),
        input_output_aliases={1: 0},
        compiler_params=params,
        name="top",
    )(group, partial, part, coefficients, far_rims, wide_p, other_p)
    return new_e, new_p, result


def solution(mesh):
    return jax.shard_map(
        shards,
        mesh=mesh,
        in_specs=(P("gx", ("gy", "gz")), P("gx", ("gy", "gz")), P("gx", "gy"), P("gz", "gx", "gy")),
        out_specs=(P("gx", ("gy", "gz")), P("gx", ("gy", "gz")), P("gz", "gx", "gy")),
        check_vma=False,
    )
```

```python
import functools

import jax
import jax.numpy as jnp
from jax import lax
from jax.experimental import pallas as pl
from jax.experimental.pallas import tpu as pltpu
from jax.sharding import PartitionSpec as P

time_step = 0.05
depth_unit = 0.015625
LANES = 128
SUBS = 8


def shift_lanes(left, cur, right, step):
    lane = lax.broadcasted_iota(jnp.int32, cur.shape, 1)
    if step < 0:
        return pltpu.roll(jnp.where(lane >= LANES + step, left, cur), -step, 1)
    return pltpu.roll(jnp.where(lane < step, right, cur), LANES - step, 1)


def square(tile, at_end):
    rest = jnp.zeros((LANES - tile.shape[0], LANES), tile.dtype)
    return jnp.concatenate([rest, tile] if at_end else [tile, rest], 0)


def first_pack(group, e, p, v, seam, outer, layer, edges, sems):
    rows, width = e.shape
    low = group[0] == 0
    source = jnp.where(low, v.shape[0] - 1, 0)
    whole = pltpu.make_async_copy(v.at[source], layer, sems.at[4])
    copies = []
    for index, (field, start) in enumerate(((e, 0), (p, 0), (e, width - LANES), (p, width - LANES))):
        into = edges.at[index // 2, (index % 2) * rows : (index % 2 + 1) * rows, :]
        copies.append(pltpu.make_async_copy(field.at[:, start : start + LANES], into, sems.at[index]))
    for copy in copies:
        copy.start()
    whole.start()
    for copy in copies:
        copy.wait()
    left = edges[0].T[:SUBS]
    right = edges[1].T[LANES - SUBS :]
    seam[...] = jnp.where(low, right, left)
    outer[...] = jnp.where(low, left, right)
    whole.wait()


def by_parity(odd, fill, first, second):
    @pl.when(odd[0] == 0)
    def _():
        fill(first, second)

    @pl.when(odd[0] == 1)
    def _():
        fill(second, first)


def lazy_pack(
    odd_x, odd_y, v_top, v_bottom, v_left, v_right, s_top, s_bottom, s_left, s_right, row_a, row_b, column_a, column_b
):
    by_parity(odd_x, functools.partial(pack_rows, v_top, v_bottom, s_top, s_bottom), row_a, row_b)
    by_parity(odd_y, functools.partial(pack_columns, v_left, v_right, s_left, s_right), column_a, column_b)


def pack_rows(v_top, v_bottom, s_top, s_bottom, up, down):
    layers, _, width = v_top.shape
    piece = width // SUBS
    for k in range(layers):
        up[k : k + 1, :width] = v_bottom[k, SUBS - 1 : SUBS, :]
        down[k : k + 1, :width] = v_top[k, 0:1, :]
    for q in range(SUBS):
        part = slice(q * piece, (q + 1) * piece)
        up[q : q + 1, width:] = s_bottom[SUBS - 1 : SUBS, part].astype(jnp.float32) * depth_unit
        down[q : q + 1, width:] = s_top[0:1, part].astype(jnp.float32) * depth_unit


def pack_columns(v_left, v_right, s_left, s_right, to_right, to_left):
    layers = v_left.shape[0]
    to_right[...] = jnp.zeros_like(to_right)
    to_left[...] = jnp.zeros_like(to_left)
    for j in range(layers // 2):
        both = jnp.concatenate([v_right[2 * j], v_right[2 * j + 1]], 0).T
        to_right[j : j + 1, :] = both[LANES - 1 :]
        both = jnp.concatenate([v_left[2 * j], v_left[2 * j + 1]], 0).T
        to_left[j : j + 1, :] = both[:1]
    j = layers // 2
    both = jnp.concatenate([s_right[...], s_right[...]], 0).astype(jnp.float32) * depth_unit
    to_right[j : j + 1, :] = both.T[LANES - 1 :]
    both = jnp.concatenate([s_left[...], s_left[...]], 0).astype(jnp.float32) * depth_unit
    to_left[j : j + 1, :] = both.T[:1]


def side_blocks(low, seam, outer):
    left = square(jnp.where(low, outer, seam), True).T
    right = square(jnp.where(low, seam, outer), False).T
    return left, right


def block_pack(group, seam, outer, blocks):
    blocks[0], blocks[1] = side_blocks(group[0] == 0, seam[...], outer[...])


def row_pack(group, odd_x, e_top, e_bottom, p_top, p_bottom, seam, outer, row_a, row_b):
    left, right = side_blocks(group[0] == 0, seam[...], outer[...])
    by_parity(odd_x, functools.partial(pack_surface_rows, left, right, e_top, e_bottom, p_top, p_bottom), row_a, row_b)


REACH = 5


def spare_piece(index, tiles):
    start = (tiles + index // SUBS) * LANES
    return slice(index % SUBS, index % SUBS + 1), slice(start, start + LANES)


def pack_surface_rows(left, right, e_top, e_bottom, p_top, p_bottom, up, down):
    rows = LANES // 2
    tiles = e_top.shape[1] // LANES + 2
    fit = SUBS - REACH
    for into, first, e_rows, p_rows in ((up, rows - REACH, e_bottom, p_bottom), (down, 0, e_top, p_top)):
        start = first % SUBS
        for t in range(tiles):
            part = slice(t * LANES, (t + 1) * LANES)
            if 0 < t < tiles - 1:
                own = slice((t - 1) * LANES, t * LANES)
                e_part = e_rows[start : start + REACH, own]
                p_part = p_rows[start : start + REACH, own]
            else:
                side = left if t == 0 else right
                e_part = side[first : first + REACH]
                p_part = side[rows + first : rows + first + REACH]
            into[:REACH, part] = e_part
            into[REACH:, part] = p_part[:fit]
            for extra in range(REACH - fit):
                row, lanes = spare_piece(extra * tiles + t, tiles)
                into[row, lanes] = p_part[fit + extra : fit + extra + 1]


def neighbourhood(ref, lane_tile, row):
    last = ref.shape[0] - 1
    at = lambda column, step: ref[column, pl.ds(row + step, SUBS), :]
    cur = at(lane_tile, 0)
    left, right = at(max(lane_tile - 1, 0), 0), at(min(lane_tile + 1, last), 0)
    rows = [at(lane_tile, step) for step in (-2, -1, 1, 2)]
    lanes = [shift_lanes(left, cur, right, step) for step in (-2, -1, 1, 2)]
    return cur, rows, lanes


def slope(values):
    return (2.0 / 3.0) * (values[2] - values[1]) - (1.0 / 12.0) * (values[3] - values[0])


def tile_rates(e_near, p_near):
    e, e_rows, e_lanes = e_near
    p, p_rows, p_lanes = p_near
    p_x, p_y = slope(p_rows), slope(p_lanes)
    near = (p_rows[1] + p_rows[2]) + (p_lanes[1] + p_lanes[2])
    far = (p_rows[0] + p_rows[3]) + (p_lanes[0] + p_lanes[3])
    bend = (4.0 / 3.0) * near - (1.0 / 12.0) * far - 5.0 * p
    rate_e = bend - (slope(e_rows) * p_x + slope(e_lanes) * p_y)
    rate_p = 0.5 * (p_x * p_x + p_y * p_y) + e
    return e, p, time_step * rate_e, -time_step * rate_p


def surface(
    odd_x, e, p, side_tiles, group, row_a, row_b, v, sea,
    new_e, new_p, wide_e, wide_p, volume, depth, e0, p0, e1, p1, sems,
):
    rows, width = e.shape
    left, right = side_tiles[0], side_tiles[1]
    copies = []
    for t in range(v.shape[2] // LANES):
        part = slice(t * LANES, (t + 1) * LANES)
        into = volume.at[:, t + 1, SUBS : SUBS + rows, :]
        copies.append(pltpu.make_async_copy(v.at[:, :, part], into, sems.at[t]))
        copies[-1].start()
    tiles = width // LANES + 2
    inner = slice(SUBS, SUBS + rows)
    fields = ((e0, e, 0), (p0, p, LANES // 2))
    fit = SUBS - REACH

    def ends(south, north):
        for source, first in ((north, SUBS - REACH), (south, SUBS + rows)):
            for t in range(tiles):
                part = slice(t * LANES, (t + 1) * LANES)
                e0[t, first : first + REACH, :] = source[:REACH, part]
                p0[t, first : first + fit, :] = source[REACH:, part]
                for extra in range(REACH - fit):
                    row = first + fit + extra
                    p0[t, row : row + 1, :] = source[spare_piece(extra * tiles + t, tiles)]

    by_parity(odd_x, ends, row_a, row_b)
    for old, source, base in fields:
        for t in range(1, tiles - 1):
            old[t, inner, :] = source[:, (t - 1) * LANES : t * LANES]
        old[0, inner, :] = left[base : base + rows]
        old[tiles - 1, inner, :] = right[base : base + rows]
    blocks = rows // SUBS + 1

    def first(block, carry):
        row = block * SUBS + SUBS - 3
        for t in range(tiles):
            old_e, old_p, step_e, step_p = tile_rates(neighbourhood(e0, t, row), neighbourhood(p0, t, row))
            e1[t, pl.ds(row, SUBS), :] = old_e + step_e
            p1[t, pl.ds(row, SUBS), :] = old_p + step_p
        return carry

    lax.fori_loop(0, blocks, first, 0, unroll=True)

    def second(block, carry):
        row = block * SUBS + SUBS - 1
        for t in range(tiles):
            one_e, one_p, step_e, step_p = tile_rates(neighbourhood(e1, t, row), neighbourhood(p1, t, row))
            old_e = e0[t, pl.ds(row, SUBS), :]
            old_p = p0[t, pl.ds(row, SUBS), :]
            wide_e[t, pl.ds(row, SUBS), :] = 0.5 * ((old_e + one_e) + step_e)
            wide_p[t, pl.ds(row, SUBS), :] = 0.5 * ((old_p + one_p) + step_p)
        return carry

    lax.fori_loop(0, blocks, second, 0, unroll=True)
    for t in range(1, tiles - 1):
        part = slice((t - 1) * LANES, t * LANES)
        new_e[:, part] = wide_e[t, inner, :]
        new_p[:, part] = wide_p[t, inner, :]
    for t in range(v.shape[2] // LANES):
        depth[t + 1, inner, :] = sea[:, t * LANES : (t + 1) * LANES].astype(jnp.float32) * depth_unit
    for copy in copies:
        copy.wait()


def rim_pack(group, odd_x, odd_y, far_a, far_b, x_a, x_b, wide_e, wide_p, rims):
    low = group[0] == 0
    layers = far_a.shape[0]
    width = rims.shape[1] - LANES
    pairs = layers // 2
    last = width // LANES + 1
    half_lanes = LANES // 2
    inner = slice(SUBS, SUBS + half_lanes)
    rims[:, width:] = jnp.zeros((SUBS, LANES), jnp.float32)
    for row, wide in ((4, wide_e), (6, wide_p)):
        for t in range(1, last):
            part = slice((t - 1) * LANES, t * LANES)
            rims[row : row + 1, part] = wide[t, SUBS - 1 : SUBS, :]
            rims[row + 1 : row + 2, part] = wide[t, SUBS + half_lanes : SUBS + half_lanes + 1, :]
    left = jnp.concatenate([wide_e[0, inner, :], wide_p[0, inner, :]], 0).T[LANES - 1 :]
    right = jnp.concatenate([wide_e[last, inner, :], wide_p[last, inner, :]], 0).T[:1]
    rims[2:3, width:] = jnp.where(low, left, right)

    def rows(far_south, far_north):
        for row, side in ((0, far_north), (2, far_south)):
            for half in range(2):
                part = slice(half * width, (half + 1) * width)
                rims[row + half : row + half + 1, :width] = jnp.where(low, side[layers - 1 : layers, part], side[0:1, part])

    by_parity(odd_x, rows, far_a, far_b)

    def columns(x_right, x_left):
        for row, side in ((0, x_left), (1, x_right)):
            top_pair = pltpu.roll(side[...], LANES // 2, 1)[pairs - 1 : pairs]
            rims[row : row + 1, width:] = jnp.where(low, top_pair, side[0:1, :])

    by_parity(odd_y, columns, x_a, x_b)


def fill(
    odd_x, odd_y, old_volume, old_depth, far_a, far_b, x_a, x_b, volume, depth, sides, depths, edges, ends, sems
):
    del old_volume, old_depth
    layers, tiles, tall = volume.shape[0], volume.shape[1], volume.shape[2]
    rows, tile = tall - 2 * SUBS, (tiles - 2) * LANES
    inner = slice(SUBS, SUBS + rows)
    even = odd_y[0] == 0
    left = square(jnp.where(even, x_b[...], x_a[...]), False).T
    right = square(jnp.where(even, x_a[...], x_b[...]), False).T
    half, pairs = LANES // 2, layers // 2
    for k in range(layers):
        base = (k % 2) * half
        sides[0, k] = pltpu.roll(left, LANES - 1 - k // 2, 1)[base : base + rows]
        sides[1, k] = pltpu.roll(right, (LANES - k // 2) % LANES, 1)[base : base + rows]
    depths[0] = pltpu.roll(left, LANES - 1 - pairs, 1)[:rows]
    depths[1] = pltpu.roll(right, LANES - pairs, 1)[:rows]
    piece = tile // SUBS // LANES

    def fill_ends(far_south, far_north):
        for end, source, row in ((0, far_north, SUBS - 1), (1, far_south, 0)):
            for t in range(tiles - 2):
                for k in range(layers):
                    edges[end, k, t, row : row + 1, :] = source[k : k + 1, t * LANES : (t + 1) * LANES]
                q, start = t // piece, tile + (t % piece) * LANES
                ends[end, t, row : row + 1, :] = source[q : q + 1, start : start + LANES]

    by_parity(odd_x, fill_ends, far_a, far_b)
    copies = []
    for index, (t, at) in enumerate(((0, slice(0, SUBS)), (tiles - 1, slice(tall - SUBS, tall)))):
        for source, target in (
            (sides.at[index], volume.at[:, t, inner, :]),
            (depths.at[index], depth.at[t, inner, :]),
            (edges.at[index], volume.at[:, 1 : tiles - 1, at, :]),
            (ends.at[index], depth.at[1 : tiles - 1, at, :]),
        ):
            copies.append(pltpu.make_async_copy(source, target, sems.at[len(copies)]))
    for copy in copies:
        copy.start()
    for copy in copies:
        copy.wait()


def apply_tile(total_layers, group, block, volume, depth, t, heights, local, ghost, spot, mine, write, rest=None):
    low = group == 0
    layers = volume.shape[0]
    spacing = 1.0 / total_layers
    sigma = (group * layers).astype(jnp.float32) * spacing + 0.5 * spacing
    gain = (2 * group).astype(jnp.float32)
    here = pl.multiple_of((block + 1) * SUBS, SUBS)

    def near(ref, t):
        at = lambda column, step: ref[column, pl.ds(here + step, SUBS), :]
        cur = at(t, 0)
        left, right = at(t - 1, 0), at(t + 1, 0)
        return cur, at(t, -1), at(t, 1), shift_lanes(left, cur, right, -1), shift_lanes(left, cur, right, 1)

    def differences(ref, t):
        p, up, down, left, right = near(ref, t)
        return p, down - up, right - left

    d, d_x, d_y = differences(depth, t)
    h, h_x, h_y = differences(heights, local)
    inverse = 1.0 / (d + h)
    scale = (0.25 / spacing) * inverse
    bx, by = scale * (d_x + h_x), scale * (d_y + h_y)
    ux, uy = scale * d_x - sigma * bx, scale * d_y - sigma * by
    bx, by = spacing * bx, spacing * by
    scaled = inverse * (1.0 / spacing)
    weight = 4.0 * (ux * ux + uy * uy) + scaled * scaled
    bend = 4.0 * (bx * bx + by * by)
    step = bend - 8.0 * (ux * bx + uy * by)
    bend = bend + bend

    def level(k):
        p, up, down, left, right = near(volume.at[k], t)
        return p, down - up, right - left, ((down + up) + (right + left)) - 4.0 * p

    far = differences(ghost, spot)
    this = level(0)
    lower = [jnp.where(low, a, b) for a, b in zip(this, far)]
    rise_below = this[0] - lower[0]
    for k in range(layers):
        if k < layers - 1:
            upper = level(k + 1)
        else:
            upper = [jnp.where(low, a, -b) for a, b in zip(far, this)]
            if mine is not None:
                upper = [a + gain * b for a, b in zip(upper, differences(mine, local))]
        rise = upper[0] - this[0]
        value = this[3] + ux * (upper[1] - lower[1]) + uy * (upper[2] - lower[2])
        value = value + weight * (rise - rise_below)
        write(k, value)
        if k < layers - 1:
            ux, uy = ux - bx, uy - by
            weight, step = weight + step, step + bend
        elif rest is not None:
            rest(value, ux, uy, weight)
        lower, this, rise_below = this, upper, rise


def own_half(total_layers, group_ref, volume, depth, far_layer, rims, wide_e, wide_p, out, ghost):
    block = pl.program_id(0)
    group = group_ref[0]
    halves = volume.shape[1] // 2 - 1

    @pl.when(block == 0)
    def _():
        fill_ghost(group == 0, group, far_layer, rims, ghost)

    for local in range(1, halves + 1):

        def write(k, value):
            out[k, :, (local - 1) * LANES : local * LANES] = value

        apply_tile(
            total_layers, group, block, volume, depth, group * halves + local, wide_e, local, ghost, local, wide_p,
            write,
        )


def other_half(
    total_layers, group_ref, before, volume, depth, far_layer, rims, wide_e, height,
    out, part, coefficients, ghost, other_e,
):
    del before
    block = pl.program_id(0)
    group = group_ref[0]
    low = group == 0
    rows, width = other_e.shape[1] - 2 * SUBS, height.shape[1]
    halves = width // LANES
    inner = slice(SUBS, SUBS + rows)

    @pl.when(block == 0)
    def _():
        fill_ghost(group == 1, 1 - group, far_layer, rims, ghost)
        for t in range(halves):
            spot = slice(t * LANES, (t + 1) * LANES)
            other_e[t + 1, inner, :] = height[:, spot]
            other_e[t + 1, SUBS - 1 : SUBS, :] = rims[4:5, spot]
            other_e[t + 1, SUBS + rows : SUBS + rows + 1, :] = rims[5:6, spot]
        edge = square(rims[:, width:], False).T[:rows]
        at_right, at_left = pltpu.roll(edge, LANES - 2, 1), pltpu.roll(edge, LANES - 3, 1)
        other_e[0, inner, :] = jnp.where(low, wide_e[halves, inner, :], at_left)
        other_e[halves + 1, inner, :] = jnp.where(low, at_right, wide_e[1, inner, :])

    for local in range(1, halves + 1):
        spot = slice((local - 1) * LANES, local * LANES)

        def write(k, value):
            out[k, :, spot] = value

        def rest(value, ux, uy, weight):
            part[:, spot] = value
            coefficients[0, :, spot] = ux
            coefficients[1, :, spot] = uy
            coefficients[2, :, spot] = weight

        apply_tile(
            total_layers, group, block, volume, depth, (1 - group) * halves + local, other_e, local, ghost, local,
            None, write, rest,
        )


def fill_ghost(first, half, far_layer, rims, ghost):
    rows, tile = far_layer.shape
    width = tile // 2
    halves = width // LANES
    inner = slice(SUBS, SUBS + rows)
    side = pltpu.roll(square(rims[:, width:], False).T, LANES - 1, 1)[:rows]
    ghost[0, inner, :] = jnp.where(first, side, far_layer[:, width - LANES : width])
    ghost[halves + 1, inner, :] = jnp.where(first, far_layer[:, width : width + LANES], side)
    for t in range(halves):
        spot = slice(t * LANES, (t + 1) * LANES)
        lanes = pl.ds(pl.multiple_of(half * width + t * LANES, LANES), LANES)
        ghost[t + 1, inner, :] = far_layer[:, lanes]
        ghost[t + 1, SUBS - 1 : SUBS, :] = jnp.where(first, rims[0:1, spot], rims[1:2, spot])
        ghost[t + 1, SUBS + rows : SUBS + rows + 1, :] = jnp.where(first, rims[2:3, spot], rims[3:4, spot])


def top(group_ref, before, part, coefficients, rims, wide_p, other_p, out, potential):
    del before
    low = group_ref[0] == 0
    rows, width = other_p.shape
    halves = width // LANES
    inner = slice(SUBS, SUBS + rows)
    edge = square(rims[:, width:], False).T[LANES // 2 : LANES // 2 + rows]
    potential[0, inner, :] = pltpu.roll(edge, LANES - 3, 1)
    potential[halves + 1, inner, :] = wide_p[1, inner, :]
    for t in range(halves):
        spot = slice(t * LANES, (t + 1) * LANES)
        potential[t + 1, inner, :] = other_p[:, spot]
        potential[t + 1, SUBS - 1 : SUBS, :] = rims[6:7, spot]
        potential[t + 1, SUBS + rows : SUBS + rows + 1, :] = rims[7:8, spot]

    def body(block, carry):
        here = pl.multiple_of((block + 1) * SUBS, SUBS)
        to = pl.ds(pl.multiple_of(block * SUBS, SUBS), SUBS)
        for t in range(1, halves + 1):
            at = lambda column, step: potential[column, pl.ds(here + step, SUBS), :]
            cur, left, right = at(t, 0), at(t - 1, 0), at(t + 1, 0)
            east = shift_lanes(left, cur, right, 1) - shift_lanes(left, cur, right, -1)
            spot = slice((t - 1) * LANES, t * LANES)
            value = coefficients[0, to, spot] * (at(t, 1) - at(t, -1)) + coefficients[1, to, spot] * east
            value = value + coefficients[2, to, spot] * cur
            partial = part[to, spot]
            out[0, to, spot] = jnp.where(low, partial, partial + 2.0 * value)
        return carry

    lax.fori_loop(0, rows // SUBS, body, 0, unroll=True)


def couples(axis, shifted):
    count = lax.axis_size(axis)
    start = 1 if shifted else 0
    one_way = [((i + start) % count, (i + start + 1) % count) for i in range(0, count, 2)]
    return one_way + [(b, a) for a, b in one_way]


def shards(elevation, surface_potential, seabed, interior_potential):
    rows, width = elevation.shape
    layers, _, tile = interior_potential.shape
    assert 2 * rows == LANES and tile == 2 * width and layers == SUBS
    assert lax.axis_size("gz") == 2
    total_layers = layers * lax.axis_size("gz")
    f32 = jnp.float32
    shape = lambda *dims: jax.ShapeDtypeStruct(dims, f32)
    whole = lambda *dims: pl.BlockSpec(dims, lambda *_: (0,) * len(dims))
    group = lax.axis_index("gz").astype(jnp.int32).reshape((1,))
    odd_x = (lax.axis_index("gx") & 1).astype(jnp.int32).reshape((1,))
    odd_y = (lax.axis_index("gy") & 1).astype(jnp.int32).reshape((1,))
    assert lax.axis_size("gx") % 2 == 0 and lax.axis_size("gy") % 2 == 0
    scalar = pl.BlockSpec(memory_space=pltpu.SMEM)
    last_row, last_tile = rows // SUBS - 1, tile // LANES - 1

    def block(dims, *index):
        return pl.BlockSpec(dims, lambda *_: index)

    params = pltpu.CompilerParams(vmem_limit_bytes=24 * 1024 * 1024)
    vmem = pl.BlockSpec(memory_space=pltpu.VMEM)
    hbm = pl.BlockSpec(memory_space=pltpu.HBM)
    seam, outer, layer = pl.pallas_call(
        first_pack,
        out_shape=(shape(SUBS, LANES), shape(SUBS, LANES), shape(rows, tile)),
        in_specs=[scalar, hbm, hbm, hbm],
        out_specs=[vmem] * 3,
        scratch_shapes=[pltpu.VMEM((2, LANES, LANES), f32), pltpu.SemaphoreType.DMA((5,))],
        compiler_params=params,
        name="first_pack",
    )(group, *(pltpu.with_memory_space_constraint(x, pltpu.HBM) for x in (elevation, surface_potential, interior_potential)))

    flat = ("gy", "gz")
    count = lax.axis_size("gy")
    partner = [(2 * i + g, 2 * i + 1 - g) for i in range(count) for g in range(2)]
    across = [(2 * i + 1, (2 * i + 2) % (2 * count)) for i in range(count)]
    across = across + [(b, a) for a, b in across]
    seam = lax.ppermute(seam, flat, partner)
    far_layer = lax.ppermute(layer, flat, partner)
    outer = lax.ppermute(outer, flat, across)

    side_tiles = pl.pallas_call(
        block_pack,
        out_shape=shape(2, LANES, LANES),
        in_specs=[scalar] + [vmem] * 2,
        out_specs=vmem,
        compiler_params=params,
        name="block_pack",
    )(group, seam, outer)
    tiles = tile // LANES
    tall = rows + 2 * SUBS
    tables = (shape(layers, tiles + 2, tall, LANES), shape(tiles + 2, tall, LANES))
    anywhere = pl.BlockSpec(memory_space=pl.ANY)
    far_a, far_b, x_a, x_b = pl.pallas_call(
        lazy_pack,
        out_shape=(shape(SUBS, tile + tile // SUBS),) * 2 + (shape(SUBS, LANES),) * 2,
        grid=(1,),
        in_specs=[
            scalar,
            scalar,
            block((layers, SUBS, tile), 0, 0, 0),
            block((layers, SUBS, tile), 0, last_row, 0),
            block((layers, rows, LANES), 0, 0, 0),
            block((layers, rows, LANES), 0, 0, last_tile),
            block((SUBS, tile), 0, 0),
            block((SUBS, tile), last_row, 0),
            block((rows, LANES), 0, 0),
            block((rows, LANES), 0, last_tile),
        ],
        out_specs=[whole(SUBS, tile + tile // SUBS)] * 2 + [whole(SUBS, LANES)] * 2,
        compiler_params=params,
        name="lazy_pack",
    )(odd_x, odd_y, *(pltpu.with_memory_space_constraint(interior_potential, pltpu.HBM),) * 4, *(seabed,) * 4)

    wide = width + 2 * LANES
    packed = wide + pl.cdiv((2 * REACH - SUBS) * (wide // LANES), SUBS) * LANES
    row_a, row_b = pl.pallas_call(
        row_pack,
        out_shape=(shape(SUBS, packed),) * 2,
        grid=(1,),
        in_specs=[
            scalar,
            scalar,
            block((SUBS, width), 0, 0),
            block((SUBS, width), last_row, 0),
            block((SUBS, width), 0, 0),
            block((SUBS, width), last_row, 0),
            whole(SUBS, LANES),
            whole(SUBS, LANES),
        ],
        out_specs=[whole(SUBS, packed)] * 2,
        compiler_params=params,
        name="row_pack",
    )(group, odd_x, elevation, elevation, surface_potential, surface_potential, seam, outer)
    sides = {}
    for name, value, axis, shifted in (
        ("row_b", row_b, "gx", True), ("row_a", row_a, "gx", False), ("x_b", x_b, "gy", True),
        ("x_a", x_a, "gy", False), ("far_b", far_b, "gx", True), ("far_a", far_a, "gx", False),
    ):
        sides[name] = lax.ppermute(value, axis, couples(axis, shifted))

    tiles = tile // LANES
    tall = rows + 2 * SUBS
    anywhere = pl.BlockSpec(memory_space=pl.ANY)
    tables = (shape(layers, tiles + 2, tall, LANES), shape(tiles + 2, tall, LANES))
    deep = rows + 3 * SUBS
    padded = (width // LANES + 2, deep, LANES)
    new_e, new_p, wide_e, wide_p, volume, depth = pl.pallas_call(
        surface,
        out_shape=(shape(rows, width),) * 2 + (shape(*padded),) * 2 + tables,
        in_specs=[scalar] + [vmem] * 3 + [scalar] + [vmem] * 2 + [hbm, vmem],
        out_specs=[vmem] * 6,
        scratch_shapes=[pltpu.VMEM(padded, f32)] * 4 + [pltpu.SemaphoreType.DMA((tiles,))],
        compiler_params=params,
        name="surface",
    )(
        odd_x, elevation, surface_potential, side_tiles, group, sides["row_a"], sides["row_b"],
        pltpu.with_memory_space_constraint(interior_potential, pltpu.HBM), seabed,
    )
    far_sides = [sides[name] for name in ("far_a", "far_b", "x_a", "x_b")]
    rims = pl.pallas_call(
        rim_pack,
        out_shape=shape(SUBS, width + LANES),
        in_specs=[scalar] * 3 + [vmem] * 6,
        out_specs=vmem,
        compiler_params=params,
        name="rim_pack",
    )(group, odd_x, odd_y, *far_sides, wide_e, wide_p)
    far_rims = lax.ppermute(rims, flat, partner)
    far_height = lax.ppermute(new_e, flat, partner)
    other_p = lax.ppermute(new_p, flat, partner)
    volume, depth = pl.pallas_call(
        fill,
        out_shape=tables,
        in_specs=[scalar] * 2 + [anywhere] * 2 + [vmem] * 4,
        out_specs=[anywhere] * 2,
        scratch_shapes=[
            pltpu.VMEM((2, layers, rows, LANES), f32),
            pltpu.VMEM((2, rows, LANES), f32),
            pltpu.VMEM((2, layers, tiles, SUBS, LANES), f32),
            pltpu.VMEM((2, tiles, SUBS, LANES), f32),
            pltpu.SemaphoreType.DMA((8,)),
        ],
        input_output_aliases={2: 0, 3: 1},
        compiler_params=params,
        name="fill",
    )(odd_x, odd_y, volume, depth, *far_sides)
    blocks = rows // SUBS
    tables = (volume, depth, far_layer, far_rims, wide_e)
    ghost = pltpu.VMEM((width // LANES + 2, tall, LANES), f32)
    partial = pl.pallas_call(
        functools.partial(own_half, total_layers),
        out_shape=shape(layers, rows, tile),
        grid_spec=pltpu.PrefetchScalarGridSpec(
            num_scalar_prefetch=1,
            grid=(blocks,),
            in_specs=[vmem] * 6,
            out_specs=pl.BlockSpec((layers, SUBS, width), lambda i, g: (0, i, g[0])),
            scratch_shapes=[ghost],
        ),
        compiler_params=params,
        name="own_half",
    )(group, *tables, wide_p)
    partial, part, coefficients = pl.pallas_call(
        functools.partial(other_half, total_layers),
        out_shape=(shape(layers, rows, tile), shape(rows, width), shape(3, rows, width)),
        grid_spec=pltpu.PrefetchScalarGridSpec(
            num_scalar_prefetch=1,
            grid=(blocks,),
            in_specs=[hbm] + [vmem] * 6,
            out_specs=[
                pl.BlockSpec((layers, SUBS, width), lambda i, g: (0, i, 1 - g[0])),
                pl.BlockSpec((SUBS, width), lambda i, g: (i, 0)),
                pl.BlockSpec((3, SUBS, width), lambda i, g: (0, i, 0)),
            ],
            scratch_shapes=[ghost] * 2,
        ),
        input_output_aliases={1: 0},
        compiler_params=params,
        name="other_half",
    )(group, partial, *tables, far_height)
    result = pl.pallas_call(
        top,
        out_shape=shape(layers, rows, tile),
        grid_spec=pltpu.PrefetchScalarGridSpec(
            num_scalar_prefetch=1,
            grid=(1,),
            in_specs=[hbm] + [vmem] * 5,
            out_specs=pl.BlockSpec((1, rows, width), lambda i, g: (layers - 1, 0, 1 - g[0])),
            scratch_shapes=[pltpu.VMEM((width // LANES + 2, tall, LANES), f32)],
        ),
        input_output_aliases={1: 0},
        compiler_params=params,
        name="top",
    )(group, partial, part, coefficients, far_rims, wide_p, other_p)
    return new_e, new_p, result


def solution(mesh):
    return jax.shard_map(
        shards,
        mesh=mesh,
        in_specs=(P("gx", ("gy", "gz")), P("gx", ("gy", "gz")), P("gx", "gy"), P("gz", "gx", "gy")),
        out_specs=(P("gx", ("gy", "gz")), P("gx", ("gy", "gz")), P("gz", "gx", "gy")),
        check_vma=False,
    )
```
